32 devices in a mesh: state: 8 (over z, y), tile: 4 (over x, core).
Axes of the slice: x: 2, y: 2, z: 4, core: 2. Of those that a mesh axis runs over, the one named last changes fastest.
Arguments:
- pair_tiles: bfloat16 [8, 4, 64, 64, 128], P('state', 'tile'), may hold values from -60 to 60
- targets: int32 [8, 4, 16, 2, 128], P('state', 'tile'), may hold values from 0 to 63, as said below
- offsets: int32 [8], replicated, may hold values from 0 to 128, as said below
- ln_gain: float32 [128], replicated, may hold values from 0.5 to 1.5
- ln_bias: float32 [128], replicated, may hold values from -3 to 3
- w_query: bfloat16 [128, 128], replicated, may hold values from -0.5 to 0.5
- w_key: bfloat16 [128, 128], replicated, may hold values from -0.5 to 0.5
- w_value: bfloat16 [128, 128], replicated, may hold values from -0.5 to 0.5
- w_pairbias: float32 [128, 4], replicated, may hold values from -25 to 25
- w_gate: bfloat16 [128, 128], replicated, may hold values from -0.5 to 0.5
- gate_bias: float32 [128], replicated, may hold values from -4 to 4
- w_output: bfloat16 [128, 128], replicated, may hold values from -0.5 to 0.5
- out_bias: float32 [128], replicated, may hold values from -3 to 3
- w_distogram: float32 [128, 64], replicated, may hold values from -4 to 4
- dist_bias: float32 [64], replicated, may hold values from -4 to 4
Outputs:
- shared_grad: float32 [4, 4, 16, 2, 128, 128], P(None, 'tile', None, None, 'state')
The draws below stay inside these ranges and needn't reach their ends.
Inputs may be any that keep to these rules, and one draw needn't show every extreme that they name: `targets`: symmetric: the bin of crop pair (x, y) equals that of (y, x) in every state. `offsets`: each is a multiple of 64; some state starts at 0 and some state at 128.
All inputs are finite; a program needn't handle non-finite values.
Results may differ from the reference program's by a relative error of at most 0.015.
Values may be sent and summed in bfloat16 or wider, within the bound.
No kernel may reach another device: no remote copies, remote signals or barrier semaphores. Data moves between devices by JAX's collectives and lax.ppermute only.
A program may use at most 64 MiB of HBM per device.

```python
import math
import jax
import jax.numpy as jnp
from jax import lax

C = 128
H = 4
HD = 32
NB = 64
L = 128
STATES = 8
NT = 4
TG = 2
B = 64
RA = 16
LFULL = 256
UT = 4


def draw_pair_tiles(key, part):
    base_key = jax.random.fold_in(key, 11)
    full_shape = (STATES, L, L, C)
    pair_field = jnp.clip(jax.random.normal(base_key, full_shape, jnp.float32), -6.0, 6.0)
    tiled = pair_field.reshape(STATES, TG, B, TG, B, C).transpose(0, 1, 3, 2, 4, 5).reshape(STATES, NT, B, B, C)
    return tiled.astype(jnp.bfloat16)


def draw_targets(key, part):
    raw_bins = jax.random.randint(jax.random.fold_in(key, 21), (STATES, L, L), 0, NB)
    index = jnp.arange(L, dtype=jnp.int32)
    upper_mask = (index[:, None] <= index[None, :])[None]
    symmetric = jnp.where(upper_mask, raw_bins, jnp.swapaxes(raw_bins, 1, 2))
    return symmetric.reshape(STATES, TG, NT, RA, L).transpose(0, 2, 3, 1, 4).astype(jnp.int32)


def draw_offsets(key, part):
    steps_drawn = jax.random.randint(jax.random.fold_in(key, 31), (STATES,), 0, TG + 1)
    top_state = jax.random.randint(jax.random.fold_in(key, 32), (), 0, STATES)
    bottom_state = (top_state + 1 + jax.random.randint(jax.random.fold_in(key, 33), (), 0, STATES - 1)) % STATES
    index = jnp.arange(STATES, dtype=jnp.int32)
    chosen = jnp.where(index == top_state, TG, jnp.where(index == bottom_state, 0, steps_drawn))
    return (B * chosen).astype(jnp.int32)


def draw_w_pairbias(key, part):
    base_key = jax.random.fold_in(key, 41)
    matrix = jnp.clip(jax.random.normal(base_key, (C, H), jnp.float32), -6.0, 6.0) / math.sqrt(C)
    return matrix.astype(jnp.float32)


def draw_w_distogram(key, part):
    base_key = jax.random.fold_in(key, 51)
    matrix = jnp.clip(jax.random.normal(base_key, (C, NB), jnp.float32), -6.0, 6.0) / math.sqrt(C)
    return matrix.astype(jnp.float32)


def noise(own_key, shape, spread, limit, kind=jnp.bfloat16):
    values = spread * jax.random.normal(own_key, shape, jnp.float32)
    return jnp.clip(values, min=-limit, max=limit).astype(kind)


def setup_inputs(seed: int = 0) -> dict:
    splits = jax.random.split(jax.random.key(seed), 16)
    pair_tiles = draw_pair_tiles(jax.random.fold_in(splits[15], 71), 0)
    targets = draw_targets(jax.random.fold_in(splits[15], 71), 0)
    offsets = draw_offsets(jax.random.fold_in(splits[15], 71), 0)
    ln_gain = jnp.clip(1.0 + 0.1 * jax.random.normal(splits[3], (C,), jnp.float32), 0.5, 1.5)
    ln_bias = noise(splits[4], (C,), 0.5, 3.0, jnp.float32)
    w_query = noise(splits[5], (C, H * HD), C ** -0.5, 0.5)
    w_key = noise(splits[6], (C, H * HD), C ** -0.5, 0.5)
    w_value = noise(splits[7], (C, H * HD), C ** -0.5, 0.5)
    w_pairbias = draw_w_pairbias(jax.random.fold_in(splits[15], 71), 0)
    w_gate = noise(splits[9], (C, H * HD), C ** -0.5, 0.5)
    gate_bias = noise(splits[10], (H * HD,), 1.0, 4.0, jnp.float32)
    w_output = noise(splits[11], (H * HD, C), (H * HD) ** -0.5, 0.5)
    out_bias = noise(splits[12], (C,), 0.5, 3.0, jnp.float32)
    w_distogram = draw_w_distogram(jax.random.fold_in(splits[15], 71), 0)
    dist_bias = noise(splits[14], (NB,), 1.0, 4.0, jnp.float32)
    return dict(pair_tiles=pair_tiles, targets=targets, offsets=offsets, ln_gain=ln_gain, ln_bias=ln_bias, w_query=w_query, w_key=w_key, w_value=w_value, w_pairbias=w_pairbias, w_gate=w_gate, gate_bias=gate_bias, w_output=w_output, out_bias=out_bias, w_distogram=w_distogram, dist_bias=dist_bias)


def layer_norm(pair_field, ln_gain, ln_bias):
    center = pair_field - lax.optimization_barrier(jnp.mean(pair_field, axis=-1, keepdims=True))
    inverse = lax.rsqrt(lax.optimization_barrier(jnp.mean(center * center, axis=-1, keepdims=True)) + 1e-05)
    normed = center * inverse
    return (normed * ln_gain + ln_bias, normed, inverse)

def product(left_op, right_op, form):
    return jnp.einsum(form, left_op.astype(jnp.float32), right_op.astype(jnp.float32), precision=lax.Precision.HIGHEST)

def probabilities(queries, key_proj, bias_full):
    scores = product(queries, key_proj, 'rjhd,rkhd->rhjk')
    scores = scores * (1.0 / math.sqrt(HD)) + bias_full[None]
    row_max = lax.optimization_barrier(jnp.max(scores, axis=-1, keepdims=True))
    exp_scores = jnp.exp(scores - row_max)
    return exp_scores / lax.optimization_barrier(jnp.sum(exp_scores, axis=-1, keepdims=True))

def reference(pair_tiles, targets, offsets, ln_gain, ln_bias, w_query, w_key, w_value, w_pairbias, w_gate, gate_bias, w_output, out_bias, w_distogram, dist_bias):
    hidden_width = H * HD
    block_rows = 8
    groups = L // block_rows
    inv_root = 1.0 / math.sqrt(HD)

    def split_rows(values_in):
        return values_in.reshape((groups, block_rows) + values_in.shape[1:])

    def state_gradient(tiled, target_rows):
        pair_field = tiled.reshape(TG, TG, B, B, C).transpose(0, 2, 1, 3, 4).reshape(L, L, C).astype(jnp.float32)
        target = target_rows.transpose(2, 0, 1, 3).reshape(L, L)
        normed_out, normed, inverse = layer_norm(pair_field, ln_gain, ln_bias)
        flat_b = normed_out.astype(jnp.bfloat16).reshape(L * L, C)

        def project(weight):
            return jnp.dot(flat_b, weight, preferred_element_type=jnp.float32).astype(jnp.bfloat16).reshape(L, L, H, HD)
        queries = project(w_query)
        key_proj = project(w_key)
        value_proj = project(w_value)
        gate_act = jax.nn.sigmoid(jnp.dot(flat_b, w_gate, preferred_element_type=jnp.float32) + gate_bias).reshape(L, L, hidden_width)
        bias_full = product(normed_out, w_pairbias, 'jkc,ch->hjk')

        def forward_block(block_args):
            query_blk, key_blk, value_blk = block_args
            weights_b = probabilities(query_blk, key_blk, bias_full).astype(jnp.bfloat16)
            return product(weights_b, value_blk, 'rhjk,rkhd->rjhd')
        attended = lax.map(forward_block, (split_rows(queries), split_rows(key_proj), split_rows(value_proj))).reshape(L, L, hidden_width)
        gated_out = (gate_act * attended).astype(jnp.bfloat16)
        updated = pair_field + jnp.dot(gated_out.reshape(L * L, hidden_width), w_output, preferred_element_type=jnp.float32).reshape(L, L, C) + out_bias
        logits = product(updated + jnp.swapaxes(updated, 0, 1), w_distogram, 'xyc,cb->xyb') + dist_bias
        row_max = lax.optimization_barrier(jnp.max(logits, axis=-1, keepdims=True))
        exp_logits = jnp.exp(logits - row_max)
        bin_prob = exp_logits / lax.optimization_barrier(jnp.sum(exp_logits, axis=-1, keepdims=True))
        onehot = (target[:, :, None] == jnp.arange(NB, dtype=jnp.int32)[None, None, :]).astype(jnp.float32)
        residual_grad = bin_prob - onehot
        logit_grad = residual_grad + jnp.swapaxes(residual_grad, 0, 1)
        pair_grad = product(logit_grad, w_distogram, 'xyb,cb->xyc')
        out_grad = product(pair_grad.astype(jnp.bfloat16), w_output, 'xyc,wc->xyw')
        att_grad_b = (out_grad * gate_act).astype(jnp.bfloat16).reshape(L, L, H, HD)
        gate_grad = out_grad * attended * gate_act * (1.0 - gate_act)

        def backward_block(bias_sum, block_args):
            query_blk, key_blk, value_blk, grad_blk = block_args
            attn_prob = probabilities(query_blk, key_blk, bias_full)
            weights_b = attn_prob.astype(jnp.bfloat16)
            value_grad = product(weights_b, grad_blk, 'rhjk,rjhd->rkhd')
            weight_grad = product(grad_blk, value_blk, 'rjhd,rkhd->rhjk')
            score_grad = attn_prob * (weight_grad - lax.optimization_barrier(jnp.sum(attn_prob * weight_grad, axis=-1, keepdims=True)))
            score_b = score_grad.astype(jnp.bfloat16)
            query_grad = product(score_b, key_blk, 'rhjk,rkhd->rjhd') * inv_root
            key_grad = product(score_b, query_blk, 'rhjk,rjhd->rkhd') * inv_root
            return (bias_sum + lax.optimization_barrier(jnp.sum(score_grad, axis=0)), (query_grad, key_grad, value_grad))
        bias_grad, grad_parts = lax.scan(backward_block, jnp.zeros((H, L, L), jnp.float32), (split_rows(queries), split_rows(key_proj), split_rows(value_proj), split_rows(att_grad_b)))
        query_grad, key_grad, value_grad = grad_parts

        def back_project(grad_part, weight):
            return product(grad_part.reshape(L, L, hidden_width).astype(jnp.bfloat16), weight, 'xyw,cw->xyc')
        normed_grad = back_project(query_grad, w_query) + back_project(key_grad, w_key) + back_project(value_grad, w_value) + back_project(gate_grad, w_gate)
        normed_grad = normed_grad + product(bias_grad, w_pairbias, 'hjk,ch->jkc')
        scaled = normed_grad * ln_gain
        ln_back = inverse * (scaled - lax.optimization_barrier(jnp.mean(scaled, axis=-1, keepdims=True)) - normed * lax.optimization_barrier(jnp.mean(scaled * normed, axis=-1, keepdims=True)))
        return (pair_grad + ln_back).astype(jnp.bfloat16)

    def accumulate(accum, state_args):
        tiled, target_rows, offset = state_args
        grad_state = state_gradient(tiled, target_rows).astype(jnp.float32)
        row_start = offset.astype(jnp.int32)
        zero_index = jnp.zeros((), jnp.int32)
        window = lax.dynamic_slice(accum, (row_start, row_start, zero_index), (L, L, C))
        accum = lax.dynamic_update_slice(accum, window + grad_state, (row_start, row_start, zero_index))
        return (accum, None)
    accum, _ = lax.scan(accumulate, jnp.zeros((LFULL, LFULL, C), jnp.float32), (pair_tiles, targets, offsets))
    return accum.reshape(UT, NT, RA, 2, L, C)
```

```python
import functools
import math

import jax
import jax.numpy as jnp
from jax import lax
from jax.experimental import pallas as pl
from jax.experimental.pallas import tpu as pltpu
from jax.sharding import PartitionSpec as P

H = 4
HD = 32
NB = 64
EPS = 1e-5
LOG2E = 1.0 / math.log(2.0)
BF = jnp.bfloat16
F32 = jnp.float32
HIGHEST = lax.Precision.HIGHEST


def nn(left, right, **kw):
    return lax.dot_general(left, right, (((1,), (0,)), ((), ())), preferred_element_type=F32, **kw)


def nt(left, right, **kw):
    return lax.dot_general(left, right, (((1,), (1,)), ((), ())), preferred_element_type=F32, **kw)


def split(value):
    high = value.astype(BF)
    low = (value - high.astype(F32)).astype(BF)
    return high, low


def transposed(value):
    return value.astype(F32).T.astype(value.dtype)


def column(row, lanes):
    return jnp.broadcast_to(row, (lanes, row.shape[1])).T


def eye(size):
    rows = lax.broadcasted_iota(jnp.int32, (size, size), 0)
    cols = lax.broadcasted_iota(jnp.int32, (size, size), 1)
    return jnp.where(rows == cols, 1.0, 0.0).astype(BF)


def rows_norm(pair_rows):
    mean = jnp.mean(pair_rows, axis=-1, keepdims=True)
    center = pair_rows - mean
    inverse = lax.rsqrt(jnp.mean(center * center, axis=-1, keepdims=True) + EPS)
    return center * inverse


def full(shape):
    return pl.BlockSpec(shape, lambda *_: (0,) * len(shape))


def prep_kernel(wq, wk, wv, wg, wo, gb, ob, wd, db, wpb, lng, w4t, w3, wod, wdt, wd3, wqg, wkv, gbc, lgc, cst, wgc):
    wide = gbc.shape[1]
    w4t[...] = jnp.concatenate([transposed(w[...]) for w in (wq, wk, wv, wg)], axis=0)
    w3[...] = jnp.concatenate([wq[...], wk[...], wv[...]], axis=1)
    wqg[...] = jnp.concatenate([wq[...], wg[...]], axis=1)
    wkv[...] = jnp.concatenate([wk[...], wv[...]], axis=1)
    dist = wd[...]
    dist_hi, dist_lo = split(dist)
    wd3[...] = jnp.concatenate([dist_hi, dist_hi, dist_lo], axis=1)
    dist_t = dist.T
    wdt[...] = jnp.concatenate(split(dist_t), axis=0)
    both = nn(wo[...].astype(F32), dist, precision=HIGHEST)
    wod[...] = jnp.concatenate(split(both.T), axis=0)
    gbc[...] = column(gb[...], wide)
    lgc[...] = column(lng[...], wide)
    shift = 2.0 * jnp.sum(dist_t * ob[...], axis=1, keepdims=True)
    cst[...] = column(db[...], wide) + shift
    gain = column(lng[...], wide)
    proj = wpb[...]
    for h in range(H):
        wgc[h] = jnp.broadcast_to(proj[:, h : h + 1], gain.shape) * gain


def bias_kernel(tile, targets, lng, lnb, wpb, out, *, per_head):
    step = pl.program_id(0)
    fold, lines, side, chans = tile.shape
    pieces = [tile[f, q] for q in range(lines) for f in range(fold)]
    normed = rows_norm(jnp.concatenate(pieces, axis=0).astype(F32)) * lng[...] + lnb[...]
    proj = jnp.concatenate([wpb[...].T, jnp.zeros((8 - H, chans), F32)], axis=0)
    bias = nt(proj, normed, precision=HIGHEST)
    width = fold * side
    for q in range(lines):
        for h in range(H):
            out[pl.ds(h * per_head + step * lines + q, 1), :] = bias[
                h : h + 1, q * width : (q + 1) * width
            ]

    @pl.when(step == 0)
    def _():
        count = targets.shape[0]
        out[pl.ds(H * per_head, count), :] = targets[...].astype(F32)


def project_kernel(*refs, parts):
    here = lax.axis_index("tile")
    part_refs = refs[:parts]
    lng, lnb, w4t, w3, gbc, zr, qt, kt, vt, qn, kn, vn, gt = refs[parts:]
    own = lax.rem(here, parts)
    rows, side, _ = part_refs[0].shape
    width = H * HD
    for row in range(rows):
        for k in range(parts):
            block = lax.rem(own + parts - k, parts)
            zr[row, pl.ds(pl.multiple_of(block * side, side), side), :] = part_refs[k][row]
    for row in range(rows):
        flat = (rows_norm(zr[row].astype(F32)) * lng[...] + lnb[...]).astype(BF)
        up = nt(w4t[...], flat)
        qt[row] = up[:width].astype(BF)
        kt[row] = up[width : 2 * width].astype(BF)
        vt[row] = up[2 * width : 3 * width].astype(BF)
        gt[row] = jax.nn.sigmoid(up[3 * width :] + gbc[...])
        flatp = nn(flat, w3[...])
        qn[row] = flatp[:, :width].astype(BF)
        kn[row] = flatp[:, width : 2 * width].astype(BF)
        vn[row] = flatp[:, 2 * width :].astype(BF)


def head_blocks(packed):
    rows, lanes = packed.shape
    blocks = []
    for h in range(H):
        pieces = []
        if h:
            pieces.append(jnp.zeros((h * HD, lanes), packed.dtype))
        pieces.append(packed[h * HD : (h + 1) * HD])
        if h < H - 1:
            pieces.append(jnp.zeros((rows - (h + 1) * HD, lanes), packed.dtype))
        blocks.append(jnp.concatenate(pieces, axis=0))
    return jnp.concatenate(blocks, axis=1)


def head_rows(packed):
    lane = lax.broadcasted_iota(jnp.int32, packed.shape, 1) // HD
    zero = jnp.zeros_like(packed)
    return jnp.concatenate([jnp.where(lane == h, packed, zero) for h in range(H)], axis=0)


def forward_kernel(gath, kn, qt, vt, gt, zr, wod, wdt, at, ot, ut, snd, bias_t, stage, *, grid_side, groups, group_rows):
    step = pl.program_id(0)
    rows = kn.shape[0]
    wide = kn.shape[1]
    side = wide // grid_side
    per_head = side * side // wide
    count = snd.shape[2]
    share = snd.shape[1]

    @pl.when(step == 0)
    def _():
        lane = lax.broadcasted_iota(jnp.int32, (per_head, wide), 1) // side
        for h in range(H):
            pieces = []
            for i in range(grid_side):
                for f in range(grid_side):
                    total = None
                    for j in range(grid_side):
                        part = gath[i * grid_side + j, h * per_head : (h + 1) * per_head, :]
                        turn = ((j - f) * side) % wide
                        if turn:
                            part = pltpu.roll(part, turn, 1)
                        total = part if total is None else jnp.where(lane == j, part, total)
                    pieces.append(total)
            bias_t[h] = jnp.concatenate(pieces, axis=0).T * LOG2E

    scale = LOG2E / math.sqrt(HD)
    for row in range(rows):
        scores = nn(kn[row], head_blocks(qt[row]))
        outs = []
        for h in range(H):
            part = scores[:, h * wide : (h + 1) * wide] * scale + bias_t[h]
            part = jnp.exp2(part - jnp.max(part, axis=0, keepdims=True))
            part = part * (1.0 / jnp.sum(part, axis=0, keepdims=True))
            part_b = part.astype(BF)
            at[row, :, h * wide : (h + 1) * wide] = part_b
            outs.append(nn(vt[row, h * HD : (h + 1) * HD, :], part_b))
        attended = jnp.concatenate(outs, axis=0)
        ot[row] = attended
        gated = (gt[row] * attended).astype(BF)
        both = nn(wod[...], gated) + nt(wdt[...], zr[row])
        mine = both[:NB] + both[NB:]
        ut[row] = mine
        high = mine.astype(BF).astype(F32)
        packed = jnp.concatenate([high, mine - high], axis=0).T
        here = step * rows + row
        for i in range(grid_side):
            for p in range(groups):
                for j in range(grid_side):
                    source = ((i * groups + p) * grid_side + j) * group_rows
                    target = ((i * grid_side + j) * share + p * group_rows) * count
                    stage[pl.ds(target + here, group_rows, stride=count), :] = packed[
                        source : source + group_rows
                    ]

    @pl.when(step == pl.num_programs(0) - 1)
    def _():
        for e in range(snd.shape[0]):
            for r in range(share):
                snd[e, r] = stage[(e * share + r) * count : (e * share + r + 1) * count, :].astype(BF)


def backward_kernel(
    gath, rcv, at, ot, ut, gt, vn, kt, qn, zr, wo, wd3, wqg, wkv, lgc, cst, dzm, dbo, acc,
    *, grid_side, groups, group_rows, owner_rows, bias_rows
):
    step = pl.program_id(0)
    rows = vn.shape[0]
    wide = vn.shape[1]
    here = lax.axis_index("tile")
    tile_i = here // grid_side
    tile_j = lax.rem(here, grid_side)
    group_span = wide // grid_side // groups
    inv_root = 1.0 / math.sqrt(HD)
    ident = eye(wide)
    adder = jnp.concatenate([ident[:NB, :NB], ident[:NB, :NB]], axis=1)
    bins = lax.broadcasted_iota(jnp.int32, (NB, wide), 0).astype(F32)

    @pl.when(step == 0)
    def _():
        acc[...] = jnp.zeros_like(acc)

    db_parts = [None] * H
    for row in range(rows):
        local = step * rows + row
        within = (local // group_rows) * group_span + tile_j * group_rows + lax.rem(local, group_rows)
        target = gath[
            within // owner_rows,
            pl.ds(bias_rows + lax.rem(within, owner_rows) * grid_side + tile_i, 1),
            :,
        ]
        mirror = [rcv[e, row].astype(F32) for e in range(rcv.shape[0])]
        pieces = []
        for i in range(grid_side):
            for p in range(groups):
                for j in range(grid_side):
                    pieces.append(
                        mirror[i * grid_side + j][p * group_rows : (p + 1) * group_rows]
                    )
        other = nt(adder, jnp.concatenate(pieces, axis=0).astype(BF))
        logits = ut[row] + other + cst[...]
        probs = jnp.exp(logits - jnp.max(logits, axis=0, keepdims=True))
        probs = probs * (1.0 / jnp.sum(probs, axis=0, keepdims=True))
        resid = 2.0 * (probs - jnp.where(bins == target, 1.0, 0.0))
        res_hi, res_lo = split(resid)
        pair_grad = nn(wd3[...], jnp.concatenate([res_hi, res_lo, res_hi], axis=0))
        out_grad = nn(wo[...], pair_grad.astype(BF))
        gate = gt[row]
        gated = out_grad * gate
        gate_grad = (gated * ot[row] * (1.0 - gate)).astype(BF)
        grad_t = gated.astype(BF)
        grad_n = gated.T.astype(BF)
        weight_grad = nn(vn[row], head_blocks(grad_t))
        score_parts = []
        query_parts = []
        for h in range(H):
            prob = at[row, :, h * wide : (h + 1) * wide].astype(F32)
            prod = weight_grad[:, h * wide : (h + 1) * wide]
            prod = prob * (prod - jnp.sum(prob * prod, axis=0, keepdims=True))
            db_parts[h] = prod if db_parts[h] is None else db_parts[h] + prod
            prod_b = prod.astype(BF)
            score_parts.append(prod_b)
            query_parts.append(nn(kt[row, h * HD : (h + 1) * HD, :], prod_b))
        query_grad = (jnp.concatenate(query_parts, axis=0) * inv_root).astype(BF)
        key_grad = nn(jnp.concatenate(score_parts, axis=1), head_rows(qn[row])) * inv_root
        value_grad = nn(at[row], head_rows(grad_n))
        normed_grad = nn(wqg[...], jnp.concatenate([query_grad, gate_grad], axis=0)) + nt(
            wkv[...], jnp.concatenate([key_grad.astype(BF), value_grad.astype(BF)], axis=1)
        )
        pair_t = nt(ident, zr[row])
        center = pair_t - jnp.mean(pair_t, axis=0, keepdims=True)
        inverse = lax.rsqrt(jnp.mean(center * center, axis=0, keepdims=True) + EPS)
        normed = center * inverse
        scaled = normed_grad * lgc[...]
        back = (
            scaled
            - jnp.mean(scaled, axis=0, keepdims=True)
            - normed * jnp.mean(scaled * normed, axis=0, keepdims=True)
        )
        dzm[row] = pair_grad + inverse * back
    for h in range(H):
        acc[h] += db_parts[h]

    @pl.when(step == pl.num_programs(0) - 1)
    def _():
        for h in range(H):
            grad = acc[h].T
            for i in range(grid_side):
                for j in range(grid_side):
                    pieces = []
                    for p in range(groups):
                        source = ((i * groups + p) * grid_side + j) * group_rows
                        pieces.append(grad[source : source + group_rows])
                    dbo[i * grid_side + j, h] = jnp.concatenate(pieces, axis=0).astype(BF)


def finish_kernel(offsets, rdb, dzm, zr, wgc, out, sums):
    step = pl.program_id(0)
    rows, chans, wide = dzm.shape
    states, _, piece, _ = out.shape
    total_rows = rdb.shape[2]
    turn = offsets[lax.axis_index("state")] // piece

    @pl.when(step == 0)
    def _():
        for h in range(H):
            total = rdb[0, h].astype(F32)
            for e in range(1, rdb.shape[0]):
                total = total + rdb[e, h].astype(F32)
            sums[pl.ds(h * total_rows, total_rows), :] = total

    ident = eye(chans)
    for row in range(rows):
        local = step * rows + row
        scaled = None
        for h in range(H):
            term = wgc[h] * sums[pl.ds(h * total_rows + local, 1), :]
            scaled = term if scaled is None else scaled + term
        pair_t = nt(ident, zr[row])
        center = pair_t - jnp.mean(pair_t, axis=0, keepdims=True)
        inverse = lax.rsqrt(jnp.mean(center * center, axis=0, keepdims=True) + EPS)
        normed = center * inverse
        back = (
            scaled
            - jnp.mean(scaled, axis=0, keepdims=True)
            - normed * jnp.mean(scaled * normed, axis=0, keepdims=True)
        )
        total = (dzm[row] + inverse * back).T.astype(BF)
        for c in range(wide // piece):
            out[lax.rem(turn + c, states), row] = total[c * piece : (c + 1) * piece]


def place_kernel(offsets, rcv, out, *, side):
    states, grid_side, rows, piece, chans = rcv.shape
    start = lax.axis_index("state") * piece
    out[...] = jnp.zeros_like(out)
    for s in range(states):
        offset = offsets[s]
        half = (start < offset).astype(jnp.int32)
        base = offset // side
        for i in range(grid_side):
            out[base + i, :, half] += rcv[s, i].astype(F32)


def on_device(
    pair_tiles,
    targets,
    offsets,
    ln_gain,
    ln_bias,
    w_query,
    w_key,
    w_value,
    w_pairbias,
    w_gate,
    gate_bias,
    w_output,
    out_bias,
    w_distogram,
    dist_bias,
):
    tiles = lax.axis_size("tile")
    states = lax.axis_size("state")
    side, chans = pair_tiles.shape[3], pair_tiles.shape[4]
    wide = targets.shape[4]
    grid_side = wide // side
    owner_rows = side // tiles
    width = H * HD
    here = lax.axis_index("tile")
    tile_i = here // grid_side
    tile_j = lax.rem(here, grid_side)
    even = owner_rows % grid_side == 0
    groups = tiles if even else 1
    group_rows = side // groups // grid_side
    share = groups * group_rows
    per_head = side * side // wide
    piece = wide // states

    def shapes(*pairs):
        return [jax.ShapeDtypeStruct(s, t) for s, t in pairs]

    tile = pair_tiles.reshape(groups, grid_side, group_rows, side, chans)

    def rows_of(j):
        return lax.dynamic_index_in_dim(tile, j, 1, keepdims=False).reshape(share, side, chans)

    parts = [rows_of(tile_j)]
    for k in range(1, grid_side):
        perm = [
            (i * grid_side + j, i * grid_side + (j + k) % grid_side)
            for i in range(grid_side)
            for j in range(grid_side)
        ]
        parts.append(lax.ppermute(rows_of(lax.rem(tile_j + k, grid_side)), "tile", perm))

    gain_row = ln_gain.reshape(1, chans)
    shift_row = ln_bias.reshape(1, chans)
    prep_shapes = shapes(
        ((4 * width, chans), BF),
        ((chans, 3 * width), BF),
        ((2 * NB, width), BF),
        ((2 * NB, chans), BF),
        ((chans, 3 * NB), BF),
        ((chans, 2 * width), BF),
        ((chans, 2 * width), BF),
        ((width, wide), F32),
        ((chans, wide), F32),
        ((NB, wide), F32),
        ((H, chans, wide), F32),
    )
    w4t, w3, wod, wdt, wd3, wqg, wkv, gbc, lgc, cst, wgc = pl.pallas_call(
        prep_kernel, out_shape=prep_shapes, name="prep"
    )(
        w_query,
        w_key,
        w_value,
        w_gate,
        w_output,
        gate_bias.reshape(1, width),
        out_bias.reshape(1, chans),
        w_distogram,
        dist_bias.reshape(1, NB),
        w_pairbias,
        gain_row,
    )

    lines = 8
    bias_rows = H * per_head
    target_rows = owner_rows * grid_side
    bias_mine = pl.pallas_call(
        functools.partial(bias_kernel, per_head=per_head),
        grid=(per_head // lines,),
        in_specs=[
            pl.BlockSpec((grid_side, lines, side, chans), lambda g: (0, g, 0, 0)),
            full((target_rows, wide)),
            full((1, chans)),
            full((1, chans)),
            full((chans, H)),
        ],
        out_specs=full((bias_rows + target_rows, wide)),
        out_shape=jax.ShapeDtypeStruct((bias_rows + target_rows, wide), F32),
        name="bias",
    )(
        pair_tiles.reshape(grid_side, per_head, side, chans),
        targets.reshape(target_rows, wide),
        gain_row,
        shift_row,
        w_pairbias,
    )
    gathered = lax.all_gather(bias_mine, "tile", axis=0, tiled=False)

    block = 4 if share % 4 == 0 else 1

    def by_row(*shape, rows=block):
        return pl.BlockSpec((rows,) + shape, lambda g: (g,) + (0,) * len(shape))

    square_b = ((share, wide, width), BF)
    zr, qt, kt, vt, qn, kn, vn, gt = pl.pallas_call(
        functools.partial(project_kernel, parts=grid_side),
        grid=(share // block,),
        in_specs=[by_row(side, chans)] * grid_side
        + [full((1, chans)), full((1, chans)), full(w4t.shape), full(w3.shape), full(gbc.shape)],
        out_specs=[by_row(wide, width)] * 8,
        out_shape=shapes(*([square_b] * 7), ((share, width, wide), F32)),
        name="project",
    )(*parts, gain_row, shift_row, w4t, w3, gbc)

    block = 2
    layout = dict(grid_side=grid_side, groups=groups, group_rows=group_rows)
    at, ot, ut, snd = pl.pallas_call(
        functools.partial(forward_kernel, **layout),
        grid=(share // block,),
        in_specs=[full(gathered.shape)]
        + [by_row(wide, width, rows=block)] * 5
        + [full(wod.shape), full(wdt.shape)],
        out_specs=[
            by_row(wide, H * wide, rows=block),
            by_row(width, wide, rows=block),
            by_row(NB, wide, rows=block),
            full((tiles, share, share, 2 * NB)),
        ],
        out_shape=shapes(
            ((share, wide, H * wide), BF),
            ((share, width, wide), F32),
            ((share, NB, wide), F32),
            ((tiles, share, share, 2 * NB), BF),
        ),
        scratch_shapes=[
            pltpu.VMEM((H, wide, wide), F32),
            pltpu.VMEM((tiles * share * share, 2 * NB), F32),
        ],
        name="forward",
    )(gathered, kn, qt, vt, gt, zr, wod, wdt)

    mirrored = lax.all_to_all(snd, "tile", split_axis=0, concat_axis=0, tiled=True)

    dzm, dbo = pl.pallas_call(
        functools.partial(
            backward_kernel, owner_rows=owner_rows, bias_rows=bias_rows, **layout
        ),
        grid=(share // block,),
        in_specs=[
            full(gathered.shape),
            pl.BlockSpec((tiles, block, share, 2 * NB), lambda g: (0, g, 0, 0)),
            by_row(wide, H * wide, rows=block),
            by_row(width, wide, rows=block),
            by_row(NB, wide, rows=block),
        ]
        + [by_row(wide, width, rows=block)] * 5
        + [full(w.shape) for w in (w_output, wd3, wqg, wkv, lgc, cst)],
        out_specs=[by_row(chans, wide, rows=block), full((tiles, H, share, wide))],
        out_shape=shapes(((share, chans, wide), F32), ((tiles, H, share, wide), BF)),
        scratch_shapes=[pltpu.VMEM((H, wide, wide), F32)],
        name="backward",
    )(gathered, mirrored, at, ot, ut, gt, vn, kt, qn, zr, w_output, wd3, wqg, wkv, lgc, cst)

    rdb = lax.all_to_all(dbo, "tile", split_axis=0, concat_axis=0, tiled=True)

    block = 4 if share % 4 == 0 else 1
    outgoing = pl.pallas_call(
        finish_kernel,
        grid_spec=pltpu.PrefetchScalarGridSpec(
            num_scalar_prefetch=1,
            grid=(share // block,),
            in_specs=[
                full(rdb.shape),
                pl.BlockSpec((block, chans, wide), lambda g, _: (g, 0, 0)),
                pl.BlockSpec((block, wide, chans), lambda g, _: (g, 0, 0)),
                full(wgc.shape),
            ],
            out_specs=pl.BlockSpec((states, block, piece, chans), lambda g, _: (0, g, 0, 0)),
            scratch_shapes=[pltpu.VMEM((H * share, wide), F32)],
        ),
        out_shape=jax.ShapeDtypeStruct((states, share, piece, chans), BF),
        name="finish",
    )(offsets, rdb, dzm, zr, wgc)

    if even:
        slots = outgoing.reshape(states * tiles, group_rows, piece, chans)
    else:
        slots = lax.dynamic_update_slice(
            jnp.zeros((states, tiles, owner_rows, piece, chans), BF),
            outgoing.reshape(states, grid_side, owner_rows, piece, chans),
            (0, tile_j * grid_side, 0, 0, 0),
        ).reshape(states * tiles, owner_rows, piece, chans)
    received = lax.all_to_all(slots, ("state", "tile"), split_axis=0, concat_axis=0, tiled=True)
    if even:
        received = received.reshape(states, grid_side, owner_rows, piece, chans)
    else:
        received = lax.dynamic_index_in_dim(
            received.reshape(states, grid_side, grid_side, owner_rows, piece, chans),
            tile_i,
            2,
            keepdims=False,
        )

    block = 4 if owner_rows % 4 == 0 else 1
    out_shape = (2 * grid_side, owner_rows, 2, piece, chans)
    placed = pl.pallas_call(
        functools.partial(place_kernel, side=side),
        grid_spec=pltpu.PrefetchScalarGridSpec(
            num_scalar_prefetch=1,
            grid=(owner_rows // block,),
            in_specs=[
                pl.BlockSpec(
                    (states, grid_side, block, piece, chans), lambda g, _: (0, 0, g, 0, 0)
                )
            ],
            out_specs=pl.BlockSpec(
                (2 * grid_side, block, 2, piece, chans), lambda g, _: (0, g, 0, 0, 0)
            ),
        ),
        out_shape=jax.ShapeDtypeStruct(out_shape, F32),
        name="place",
    )(offsets, received)
    return placed.reshape(2 * grid_side, 1, owner_rows, 2, piece, chans)


def solution(mesh):
    in_specs = (
        P("state", "tile", None, None, None),
        P("state", "tile", None, None, None),
    ) + (P(),) * 13
    out_specs = P(None, "tile", None, None, "state", None)
    return jax.shard_map(
        on_device, mesh=mesh, in_specs=in_specs, out_specs=out_specs, check_vma=False
    )
```

```python
import functools
import math

import jax
import jax.numpy as jnp
from jax import lax
from jax.experimental import pallas as pl
from jax.experimental.pallas import tpu as pltpu
from jax.sharding import PartitionSpec as P

H = 4
HD = 32
NB = 64
FWD_ROWS = 8
BWD_ROWS = 8
FWD_PACE = (8, 1, 0)
BWD_PACE = (8, 0, 0)
PROJ_PACE = (2, 0, 3)
FIN_PACE = (8, 0, 0)
PROJ_ROWS = 8
FIN_ROWS = 8
EPS = 1e-5
LOG2E = 1.0 / math.log(2.0)
BF = jnp.bfloat16
F32 = jnp.float32
HIGHEST = lax.Precision.HIGHEST


def nn(left, right, **kw):
    return lax.dot_general(left, right, (((1,), (0,)), ((), ())), preferred_element_type=F32, **kw)


def nt(left, right, **kw):
    return lax.dot_general(left, right, (((1,), (1,)), ((), ())), preferred_element_type=F32, **kw)


def split(value):
    high = value.astype(BF)
    low = (value - high.astype(F32)).astype(BF)
    return high, low


def transposed(value):
    return value.astype(F32).T.astype(value.dtype)


def column(row, lanes):
    return jnp.broadcast_to(row, (lanes, row.shape[1])).T


def eye(size):
    rows = lax.broadcasted_iota(jnp.int32, (size, size), 0)
    cols = lax.broadcasted_iota(jnp.int32, (size, size), 1)
    return jnp.where(rows == cols, 1.0, 0.0).astype(BF)


def rows_norm(pair_rows):
    mean = jnp.mean(pair_rows, axis=-1, keepdims=True)
    center = pair_rows - mean
    inverse = lax.rsqrt(jnp.mean(center * center, axis=-1, keepdims=True) + EPS)
    return center * inverse


def interleave(rows, pace):
    size, inner, outer = pace
    begin = {row: (r % size) * inner + (r // size) * outer for r, row in enumerate(rows)}
    tick = 0
    while begin:
        for row in list(begin):
            if begin[row] <= tick:
                try:
                    next(row)
                except StopIteration:
                    del begin[row]
        tick += 1


def full(shape):
    return pl.BlockSpec(shape, lambda *_: (0,) * len(shape))


def prep_kernel(wq, wk, wv, wg, wo, gb, ob, wd, db, wpb, lng, w4t, w3, wod, wdt, wd3, wqg, wkv, gbc, lgc, cst, wgc):
    wide = gbc.shape[1]
    w4t[...] = jnp.concatenate([transposed(w[...]) for w in (wq, wk, wv, wg)], axis=0)
    w3[...] = jnp.concatenate([wq[...], wk[...], wv[...]], axis=1)
    wqg[...] = jnp.concatenate([wq[...], wg[...]], axis=1)
    wkv[...] = jnp.concatenate([wk[...], wv[...]], axis=1)
    dist = wd[...]
    dist_hi, dist_lo = split(dist)
    wd3[...] = jnp.concatenate([dist_hi, dist_hi, dist_lo], axis=1)
    dist_t = dist.T
    wdt[...] = jnp.concatenate(split(dist_t), axis=0)
    both = nn(wo[...].astype(F32), dist, precision=HIGHEST)
    wod[...] = jnp.concatenate(split(both.T), axis=0)
    gbc[...] = column(gb[...], wide)
    lgc[...] = column(lng[...], wide)
    shift = 2.0 * jnp.sum(dist_t * ob[...], axis=1, keepdims=True)
    cst[...] = column(db[...], wide) + shift
    gain = column(lng[...], wide)
    proj = wpb[...]
    for h in range(H):
        wgc[h] = jnp.broadcast_to(proj[:, h : h + 1], gain.shape) * gain


def bias_kernel(tile, targets, lng, lnb, wpb, out, *, per_head):
    step = pl.program_id(0)
    fold, lines, side, chans = tile.shape
    pieces = [tile[f, q] for q in range(lines) for f in range(fold)]
    normed = rows_norm(jnp.concatenate(pieces, axis=0).astype(F32)) * lng[...] + lnb[...]
    proj = jnp.concatenate([wpb[...].T, jnp.zeros((8 - H, chans), F32)], axis=0)
    bias = nt(proj, normed, precision=HIGHEST)
    width = fold * side
    for q in range(lines):
        for h in range(H):
            out[pl.ds(h * per_head + step * lines + q, 1), :] = bias[
                h : h + 1, q * width : (q + 1) * width
            ]

    @pl.when(step == 0)
    def _():
        count = targets.shape[0]
        out[pl.ds(H * per_head, count), :] = targets[...].astype(F32)


def project_kernel(*refs, parts):
    here = lax.axis_index("tile")
    part_refs = refs[:parts]
    lng, lnb, w4t, w3, gbc, zr, qt, kt, vt, qn, kn, vn, gt = refs[parts:]
    own = lax.rem(here, parts)
    rows, side, _ = part_refs[0].shape
    width = H * HD
    for row in range(rows):
        for k in range(parts):
            block = lax.rem(own + parts - k, parts)
            zr[row, pl.ds(pl.multiple_of(block * side, side), side), :] = part_refs[k][row]

    def one_row(row):
        pair_row = zr[row].astype(F32)
        center = pair_row - jnp.mean(pair_row, axis=-1, keepdims=True)
        yield
        inverse = lax.rsqrt(jnp.mean(center * center, axis=-1, keepdims=True) + EPS)
        yield
        flat = (center * inverse * lng[...] + lnb[...]).astype(BF)
        yield
        for k, out in enumerate((qt, kt, vt)):
            out[row] = nt(w4t[k * width : (k + 1) * width], flat).astype(BF)
            yield
        gt[row] = jax.nn.sigmoid(nt(w4t[3 * width :], flat) + gbc[...])
        yield
        for k, out in enumerate((qn, kn, vn)):
            out[row] = nn(flat, w3[:, k * width : (k + 1) * width]).astype(BF)
            yield

    interleave([one_row(row) for row in range(rows)], PROJ_PACE)


def head_blocks(packed):
    rows, lanes = packed.shape
    blocks = []
    for h in range(H):
        pieces = []
        if h:
            pieces.append(jnp.zeros((h * HD, lanes), packed.dtype))
        pieces.append(packed[h * HD : (h + 1) * HD])
        if h < H - 1:
            pieces.append(jnp.zeros((rows - (h + 1) * HD, lanes), packed.dtype))
        blocks.append(jnp.concatenate(pieces, axis=0))
    return jnp.concatenate(blocks, axis=1)


def head_rows(packed):
    lane = lax.broadcasted_iota(jnp.int32, packed.shape, 1) // HD
    zero = jnp.zeros_like(packed)
    return jnp.concatenate([jnp.where(lane == h, packed, zero) for h in range(H)], axis=0)


def forward_kernel(gath, kn, qt, vt, gt, zr, wod, wdt, at, ot, ut, snd, bias_t, stage, *, grid_side, groups, group_rows):
    step = pl.program_id(0)
    rows = kn.shape[0]
    wide = kn.shape[1]
    side = wide // grid_side
    per_head = side * side // wide
    count = snd.shape[2]
    share = snd.shape[1]

    @pl.when(step == 0)
    def _():
        lane = lax.broadcasted_iota(jnp.int32, (per_head, wide), 1) // side
        for h in range(H):
            pieces = []
            for i in range(grid_side):
                for f in range(grid_side):
                    total = None
                    for j in range(grid_side):
                        part = gath[i * grid_side + j, h * per_head : (h + 1) * per_head, :]
                        turn = ((j - f) * side) % wide
                        if turn:
                            part = pltpu.roll(part, turn, 1)
                        total = part if total is None else jnp.where(lane == j, part, total)
                    pieces.append(total)
            bias_t[h] = jnp.concatenate(pieces, axis=0).T * LOG2E

    scale = LOG2E / math.sqrt(HD)

    def one_row(row):
        blocks = head_blocks(qt[row])
        outs = []
        for pair in range(0, H, 2):
            scores = nn(kn[row], blocks[:, pair * wide : (pair + 2) * wide])
            yield
            for h in range(pair, pair + 2):
                part = scores[:, (h - pair) * wide : (h - pair + 1) * wide] * scale + bias_t[h]
                peak = jnp.max(part, axis=0, keepdims=True)
                yield
                part = jnp.exp2(part - peak)
                total = jnp.sum(part, axis=0, keepdims=True)
                yield
                part_b = (part * (1.0 / total)).astype(BF)
                at[row, :, h * wide : (h + 1) * wide] = part_b
                yield
                outs.append(nn(vt[row, h * HD : (h + 1) * HD, :], part_b))
                ot[row, h * HD : (h + 1) * HD, :] = outs[-1]
                yield
        gated = (gt[row] * ot[row]).astype(BF)
        yield
        both = nn(wod[...], gated) + nt(wdt[...], zr[row])
        yield
        mine = both[:NB] + both[NB:]
        ut[row] = mine
        high = mine.astype(BF).astype(F32)
        yield
        packed = jnp.concatenate([high, mine - high], axis=0).T
        here = step * rows + row
        yield
        for i in range(grid_side):
            for p in range(groups):
                for j in range(grid_side):
                    source = ((i * groups + p) * grid_side + j) * group_rows
                    target = ((i * grid_side + j) * share + p * group_rows) * count
                    stage[pl.ds(target + here, group_rows, stride=count), :] = packed[
                        source : source + group_rows
                    ]
                yield

    interleave([one_row(row) for row in range(rows)], FWD_PACE)

    @pl.when(step == pl.num_programs(0) - 1)
    def _():
        for e in range(snd.shape[0]):
            for r in range(share):
                snd[e, r] = stage[(e * share + r) * count : (e * share + r + 1) * count, :].astype(BF)


def backward_kernel(
    gath, rcv, at, ot, ut, gt, vn, kt, qn, zr, wo, wd3, wqg, wkv, lgc, cst, dzm, dbo, acc, grad_s, gate_s, value_s, score_s, query_s,
    *, grid_side, groups, group_rows, owner_rows, bias_rows
):
    step = pl.program_id(0)
    rows = vn.shape[0]
    wide = vn.shape[1]
    here = lax.axis_index("tile")
    tile_i = here // grid_side
    tile_j = lax.rem(here, grid_side)
    group_span = wide // grid_side // groups
    inv_root = 1.0 / math.sqrt(HD)
    ident = eye(wide)
    adder = jnp.concatenate([ident[:NB, :NB], ident[:NB, :NB]], axis=1)
    bins = lax.broadcasted_iota(jnp.int32, (NB, wide), 0).astype(F32)

    @pl.when(step == 0)
    def _():
        acc[...] = jnp.zeros_like(acc)

    def one_row(row):
        local = step * rows + row
        within = (local // group_rows) * group_span + tile_j * group_rows + lax.rem(local, group_rows)
        target = gath[
            within // owner_rows,
            pl.ds(bias_rows + lax.rem(within, owner_rows) * grid_side + tile_i, 1),
            :,
        ]
        mirror = [rcv[e, row].astype(F32) for e in range(rcv.shape[0])]
        pieces = []
        for i in range(grid_side):
            for p in range(groups):
                for j in range(grid_side):
                    pieces.append(
                        mirror[i * grid_side + j][p * group_rows : (p + 1) * group_rows]
                    )
        other = nt(adder, jnp.concatenate(pieces, axis=0).astype(BF))
        yield
        logits = ut[row] + other + cst[...]
        peak = jnp.max(logits, axis=0, keepdims=True)
        yield
        probs = jnp.exp(logits - peak)
        total = jnp.sum(probs, axis=0, keepdims=True)
        yield
        resid = 2.0 * (probs * (1.0 / total) - jnp.where(bins == target, 1.0, 0.0))
        res_hi, res_lo = split(resid)
        yield
        pair_grad = nn(wd3[...], jnp.concatenate([res_hi, res_lo, res_hi], axis=0))
        dzm[row] = pair_grad
        yield
        out_grad = nn(wo[...], pair_grad.astype(BF))
        yield
        gate = gt[row]
        gated = out_grad * gate
        grad_s[row] = gated.astype(BF)
        yield
        gate_s[row] = (gated * ot[row] * (1.0 - gate)).astype(BF)
        yield
        grad_n = gated.T.astype(BF)
        yield
        value_s[row] = nn(at[row], head_rows(grad_n)).astype(BF)
        yield
        blocks = head_blocks(grad_s[row])
        yield
        for pair in range(0, H, 2):
            weight_grad = nn(vn[row], blocks[:, pair * wide : (pair + 2) * wide])
            yield
            for h in range(pair, pair + 2):
                prob = at[row, :, h * wide : (h + 1) * wide].astype(F32)
                prod = prob * weight_grad[:, (h - pair) * wide : (h - pair + 1) * wide]
                total = jnp.sum(prod, axis=0, keepdims=True)
                yield
                prod = prod - prob * total
                score_s[row, :, h * wide : (h + 1) * wide] = prod.astype(BF)
                acc[h] += prod
                yield
                query_s[row, h * HD : (h + 1) * HD, :] = (
                    nn(kt[row, h * HD : (h + 1) * HD, :], score_s[row, :, h * wide : (h + 1) * wide])
                    * inv_root
                ).astype(BF)
                yield
        key_grad = nn(score_s[row], head_rows(qn[row])) * inv_root
        yield
        normed_grad = nn(wqg[...], jnp.concatenate([query_s[row], gate_s[row]], axis=0)) + nt(
            wkv[...], jnp.concatenate([key_grad.astype(BF), value_s[row]], axis=1)
        )
        yield
        pair_t = nt(ident, zr[row])
        center = pair_t - jnp.mean(pair_t, axis=0, keepdims=True)
        yield
        inverse = lax.rsqrt(jnp.mean(center * center, axis=0, keepdims=True) + EPS)
        normed = center * inverse
        yield
        scaled = normed_grad * lgc[...]
        mean_a = jnp.mean(scaled, axis=0, keepdims=True)
        mean_b = jnp.mean(scaled * normed, axis=0, keepdims=True)
        yield
        dzm[row] = dzm[row] + inverse * (scaled - mean_a - normed * mean_b)
        yield

    interleave([one_row(row) for row in range(rows)], BWD_PACE)

    @pl.when(step == pl.num_programs(0) - 1)
    def _():
        for h in range(H):
            grad = acc[h].T
            for i in range(grid_side):
                for j in range(grid_side):
                    pieces = []
                    for p in range(groups):
                        source = ((i * groups + p) * grid_side + j) * group_rows
                        pieces.append(grad[source : source + group_rows])
                    dbo[i * grid_side + j, h] = jnp.concatenate(pieces, axis=0).astype(BF)


def finish_kernel(offsets, rdb, dzm, zr, wgc, out, sums):
    step = pl.program_id(0)
    rows, chans, wide = dzm.shape
    states, _, piece, _ = out.shape
    total_rows = rdb.shape[2]
    turn = offsets[lax.axis_index("state")] // piece

    @pl.when(step == 0)
    def _():
        for h in range(H):
            total = rdb[0, h].astype(F32)
            for e in range(1, rdb.shape[0]):
                total = total + rdb[e, h].astype(F32)
            sums[pl.ds(h * total_rows, total_rows), :] = total

    ident = eye(chans)

    def one_row(row):
        local = step * rows + row
        pair_t = nt(ident, zr[row])
        yield
        center = pair_t - jnp.mean(pair_t, axis=0, keepdims=True)
        yield
        inverse = lax.rsqrt(jnp.mean(center * center, axis=0, keepdims=True) + EPS)
        normed = center * inverse
        yield
        scaled = None
        for h in range(H):
            term = wgc[h] * sums[pl.ds(h * total_rows + local, 1), :]
            scaled = term if scaled is None else scaled + term
        yield
        mean_a = jnp.mean(scaled, axis=0, keepdims=True)
        mean_b = jnp.mean(scaled * normed, axis=0, keepdims=True)
        yield
        total = dzm[row] + inverse * (scaled - mean_a - normed * mean_b)
        yield
        total = total.T.astype(BF)
        for c in range(wide // piece):
            out[lax.rem(turn + c, states), row] = total[c * piece : (c + 1) * piece]
        yield

    interleave([one_row(row) for row in range(rows)], FIN_PACE)


def place_kernel(offsets, rcv, out, *, side):
    states, grid_side, rows, piece, chans = rcv.shape
    start = lax.axis_index("state") * piece
    out[...] = jnp.zeros_like(out)
    for s in range(states):
        offset = offsets[s]
        half = (start < offset).astype(jnp.int32)
        base = offset // side
        for i in range(grid_side):
            out[base + i, :, half] += rcv[s, i].astype(F32)


def on_device(
    pair_tiles,
    targets,
    offsets,
    ln_gain,
    ln_bias,
    w_query,
    w_key,
    w_value,
    w_pairbias,
    w_gate,
    gate_bias,
    w_output,
    out_bias,
    w_distogram,
    dist_bias,
):
    tiles = lax.axis_size("tile")
    states = lax.axis_size("state")
    side, chans = pair_tiles.shape[3], pair_tiles.shape[4]
    wide = targets.shape[4]
    grid_side = wide // side
    owner_rows = side // tiles
    width = H * HD
    here = lax.axis_index("tile")
    tile_i = here // grid_side
    tile_j = lax.rem(here, grid_side)
    even = owner_rows % grid_side == 0
    groups = tiles if even else 1
    group_rows = side // groups // grid_side
    share = groups * group_rows
    per_head = side * side // wide
    piece = wide // states

    def shapes(*pairs):
        return [jax.ShapeDtypeStruct(s, t) for s, t in pairs]

    tile = pair_tiles.reshape(groups, grid_side, group_rows, side, chans)

    def rows_of(j):
        return lax.dynamic_index_in_dim(tile, j, 1, keepdims=False).reshape(share, side, chans)

    parts = [rows_of(tile_j)]
    for k in range(1, grid_side):
        perm = [
            (i * grid_side + j, i * grid_side + (j + k) % grid_side)
            for i in range(grid_side)
            for j in range(grid_side)
        ]
        parts.append(lax.ppermute(rows_of(lax.rem(tile_j + k, grid_side)), "tile", perm))

    gain_row = ln_gain.reshape(1, chans)
    shift_row = ln_bias.reshape(1, chans)
    prep_shapes = shapes(
        ((4 * width, chans), BF),
        ((chans, 3 * width), BF),
        ((2 * NB, width), BF),
        ((2 * NB, chans), BF),
        ((chans, 3 * NB), BF),
        ((chans, 2 * width), BF),
        ((chans, 2 * width), BF),
        ((width, wide), F32),
        ((chans, wide), F32),
        ((NB, wide), F32),
        ((H, chans, wide), F32),
    )
    w4t, w3, wod, wdt, wd3, wqg, wkv, gbc, lgc, cst, wgc = pl.pallas_call(
        prep_kernel, out_shape=prep_shapes, name="prep"
    )(
        w_query,
        w_key,
        w_value,
        w_gate,
        w_output,
        gate_bias.reshape(1, width),
        out_bias.reshape(1, chans),
        w_distogram,
        dist_bias.reshape(1, NB),
        w_pairbias,
        gain_row,
    )

    lines = 8
    bias_rows = H * per_head
    target_rows = owner_rows * grid_side
    bias_mine = pl.pallas_call(
        functools.partial(bias_kernel, per_head=per_head),
        grid=(per_head // lines,),
        in_specs=[
            pl.BlockSpec((grid_side, lines, side, chans), lambda g: (0, g, 0, 0)),
            full((target_rows, wide)),
            full((1, chans)),
            full((1, chans)),
            full((chans, H)),
        ],
        out_specs=full((bias_rows + target_rows, wide)),
        out_shape=jax.ShapeDtypeStruct((bias_rows + target_rows, wide), F32),
        name="bias",
    )(
        pair_tiles.reshape(grid_side, per_head, side, chans),
        targets.reshape(target_rows, wide),
        gain_row,
        shift_row,
        w_pairbias,
    )
    gathered = lax.all_gather(bias_mine, "tile", axis=0, tiled=False)

    block = PROJ_ROWS if share % PROJ_ROWS == 0 else 1

    def by_row(*shape, rows=block):
        return pl.BlockSpec((rows,) + shape, lambda g: (g,) + (0,) * len(shape))

    square_b = ((share, wide, width), BF)
    zr, qt, kt, vt, qn, kn, vn, gt = pl.pallas_call(
        functools.partial(project_kernel, parts=grid_side),
        grid=(share // block,),
        in_specs=[by_row(side, chans)] * grid_side
        + [full((1, chans)), full((1, chans)), full(w4t.shape), full(w3.shape), full(gbc.shape)],
        out_specs=[by_row(wide, width)] * 8,
        out_shape=shapes(*([square_b] * 7), ((share, width, wide), F32)),
        name="project",
    )(*parts, gain_row, shift_row, w4t, w3, gbc)

    block = FWD_ROWS if share % FWD_ROWS == 0 else 1
    layout = dict(grid_side=grid_side, groups=groups, group_rows=group_rows)
    at, ot, ut, snd = pl.pallas_call(
        functools.partial(forward_kernel, **layout),
        grid=(share // block,),
        in_specs=[full(gathered.shape)]
        + [by_row(wide, width, rows=block)] * 5
        + [full(wod.shape), full(wdt.shape)],
        out_specs=[
            by_row(wide, H * wide, rows=block),
            by_row(width, wide, rows=block),
            by_row(NB, wide, rows=block),
            full((tiles, share, share, 2 * NB)),
        ],
        out_shape=shapes(
            ((share, wide, H * wide), BF),
            ((share, width, wide), F32),
            ((share, NB, wide), F32),
            ((tiles, share, share, 2 * NB), BF),
        ),
        scratch_shapes=[
            pltpu.VMEM((H, wide, wide), F32),
            pltpu.VMEM((tiles * share * share, 2 * NB), F32),
        ],
        name="forward",
    )(gathered, kn, qt, vt, gt, zr, wod, wdt)

    mirrored = lax.all_to_all(snd, "tile", split_axis=0, concat_axis=0, tiled=True)

    block = BWD_ROWS if share % BWD_ROWS == 0 else 1
    dzm, dbo = pl.pallas_call(
        functools.partial(
            backward_kernel, owner_rows=owner_rows, bias_rows=bias_rows, **layout
        ),
        grid=(share // block,),
        in_specs=[
            full(gathered.shape),
            pl.BlockSpec((tiles, block, share, 2 * NB), lambda g: (0, g, 0, 0)),
            by_row(wide, H * wide, rows=block),
            by_row(width, wide, rows=block),
            by_row(NB, wide, rows=block),
        ]
        + [by_row(wide, width, rows=block)] * 5
        + [full(w.shape) for w in (w_output, wd3, wqg, wkv, lgc, cst)],
        out_specs=[by_row(chans, wide, rows=block), full((tiles, H, share, wide))],
        out_shape=shapes(((share, chans, wide), F32), ((tiles, H, share, wide), BF)),
        scratch_shapes=[pltpu.VMEM((H, wide, wide), F32)]
        + [
            pltpu.VMEM((block,) + shape, BF)
            for shape in ((width, wide), (width, wide), (wide, width), (wide, H * wide), (width, wide))
        ],
        name="backward",
    )(gathered, mirrored, at, ot, ut, gt, vn, kt, qn, zr, w_output, wd3, wqg, wkv, lgc, cst)

    rdb = lax.all_to_all(dbo, "tile", split_axis=0, concat_axis=0, tiled=True)

    block = FIN_ROWS if share % FIN_ROWS == 0 else 1
    outgoing = pl.pallas_call(
        finish_kernel,
        grid_spec=pltpu.PrefetchScalarGridSpec(
            num_scalar_prefetch=1,
            grid=(share // block,),
            in_specs=[
                full(rdb.shape),
                pl.BlockSpec((block, chans, wide), lambda g, _: (g, 0, 0)),
                pl.BlockSpec((block, wide, chans), lambda g, _: (g, 0, 0)),
                full(wgc.shape),
            ],
            out_specs=pl.BlockSpec((states, block, piece, chans), lambda g, _: (0, g, 0, 0)),
            scratch_shapes=[pltpu.VMEM((H * share, wide), F32)],
        ),
        out_shape=jax.ShapeDtypeStruct((states, share, piece, chans), BF),
        name="finish",
    )(offsets, rdb, dzm, zr, wgc)

    if even:
        slots = outgoing.reshape(states * tiles, group_rows, piece, chans)
    else:
        slots = lax.dynamic_update_slice(
            jnp.zeros((states, tiles, owner_rows, piece, chans), BF),
            outgoing.reshape(states, grid_side, owner_rows, piece, chans),
            (0, tile_j * grid_side, 0, 0, 0),
        ).reshape(states * tiles, owner_rows, piece, chans)
    received = lax.all_to_all(slots, ("state", "tile"), split_axis=0, concat_axis=0, tiled=True)
    if even:
        received = received.reshape(states, grid_side, owner_rows, piece, chans)
    else:
        received = lax.dynamic_index_in_dim(
            received.reshape(states, grid_side, grid_side, owner_rows, piece, chans),
            tile_i,
            2,
            keepdims=False,
        )

    block = 4 if owner_rows % 4 == 0 else 1
    out_shape = (2 * grid_side, owner_rows, 2, piece, chans)
    placed = pl.pallas_call(
        functools.partial(place_kernel, side=side),
        grid_spec=pltpu.PrefetchScalarGridSpec(
            num_scalar_prefetch=1,
            grid=(owner_rows // block,),
            in_specs=[
                pl.BlockSpec(
                    (states, grid_side, block, piece, chans), lambda g, _: (0, 0, g, 0, 0)
                )
            ],
            out_specs=pl.BlockSpec(
                (2 * grid_side, block, 2, piece, chans), lambda g, _: (0, g, 0, 0, 0)
            ),
        ),
        out_shape=jax.ShapeDtypeStruct(out_shape, F32),
        name="place",
    )(offsets, received)
    return placed.reshape(2 * grid_side, 1, owner_rows, 2, piece, chans)


def solution(mesh):
    in_specs = (
        P("state", "tile", None, None, None),
        P("state", "tile", None, None, None),
    ) + (P(),) * 13
    out_specs = P(None, "tile", None, None, "state", None)
    return jax.shard_map(
        on_device, mesh=mesh, in_specs=in_specs, out_specs=out_specs, check_vma=False
    )
```

```python
import functools
import math

import jax
import jax.numpy as jnp
from jax import lax
from jax.experimental import pallas as pl
from jax.experimental.pallas import tpu as pltpu
from jax.sharding import PartitionSpec as P

H = 4
HD = 32
NB = 64
FWD_ROWS = 8
BWD_ROWS = 8
FWD_PACE = (8, 1, 0)
BWD_PACE = (8, 0, 0)
PROJ_PACE = (2, 0, 3)
FIN_PACE = (8, 0, 0)
PROJ_ROWS = 8
FIN_ROWS = 8
EPS = 1e-5
LOG2E = 1.0 / math.log(2.0)
BF = jnp.bfloat16
F32 = jnp.float32
HIGHEST = lax.Precision.HIGHEST


def nn(left, right, **kw):
    return lax.dot_general(left, right, (((1,), (0,)), ((), ())), preferred_element_type=F32, **kw)


def nt(left, right, **kw):
    return lax.dot_general(left, right, (((1,), (1,)), ((), ())), preferred_element_type=F32, **kw)


def split(value):
    high = value.astype(BF)
    low = (value - high.astype(F32)).astype(BF)
    return high, low


def transposed(value):
    return value.astype(F32).T.astype(value.dtype)


def column(row, lanes):
    return jnp.broadcast_to(row, (lanes, row.shape[1])).T


def eye(size):
    rows = lax.broadcasted_iota(jnp.int32, (size, size), 0)
    cols = lax.broadcasted_iota(jnp.int32, (size, size), 1)
    return jnp.where(rows == cols, 1.0, 0.0).astype(BF)


def rows_norm(pair_rows):
    mean = jnp.mean(pair_rows, axis=-1, keepdims=True)
    center = pair_rows - mean
    inverse = lax.rsqrt(jnp.mean(center * center, axis=-1, keepdims=True) + EPS)
    return center * inverse


def interleave(rows, pace):
    size, inner, outer = pace
    begin = {row: (r % size) * inner + (r // size) * outer for r, row in enumerate(rows)}
    tick = 0
    while begin:
        for row in list(begin):
            if begin[row] <= tick:
                try:
                    next(row)
                except StopIteration:
                    del begin[row]
        tick += 1


def full(shape):
    return pl.BlockSpec(shape, lambda *_: (0,) * len(shape))


def prep_kernel(wq, wk, wv, wg, wo, gb, ob, wd, db, wpb, lng, w4t, w3, wod, wdt, wd3, wqg, wkv, gbc, lgc, cst, wgc):
    wide = gbc.shape[1]
    w4t[...] = jnp.concatenate([transposed(w[...]) for w in (wq, wk, wv, wg)], axis=0)
    w3[...] = jnp.concatenate([wq[...], wk[...], wv[...]], axis=1)
    wqg[...] = jnp.concatenate([wq[...], wg[...]], axis=1)
    wkv[...] = jnp.concatenate([wk[...], wv[...]], axis=1)
    dist_t = wd[...]
    dist = dist_t.T
    dist_hi, dist_lo = split(dist)
    wd3[...] = jnp.concatenate([dist_hi, dist_hi, dist_lo], axis=1)
    wdt[...] = jnp.concatenate(split(dist_t), axis=0)
    both = nn(wo[...].astype(F32), dist, precision=HIGHEST)
    wod[...] = jnp.concatenate(split(both.T), axis=0)
    gbc[...] = column(gb[...], wide)
    lgc[...] = column(lng[...], wide)
    shift = 2.0 * jnp.sum(dist_t * ob[...], axis=1, keepdims=True)
    cst[...] = column(db[...], wide) + shift
    gain = column(lng[...], wide)
    for h in range(H):
        wgc[h] = column(wpb[h : h + 1], wide) * gain


def bias_kernel(tile, targets, lng, lnb, wpb, out, *, per_head):
    step = pl.program_id(0)
    fold, lines, side, chans = tile.shape
    pieces = [tile[f, q] for q in range(lines) for f in range(fold)]
    normed = rows_norm(jnp.concatenate(pieces, axis=0).astype(F32)) * lng[...] + lnb[...]
    proj = jnp.concatenate([wpb[...], jnp.zeros((8 - H, chans), F32)], axis=0)
    bias = nt(proj, normed, precision=HIGHEST)
    width = fold * side
    for q in range(lines):
        for h in range(H):
            out[pl.ds(h * per_head + step * lines + q, 1), :] = bias[
                h : h + 1, q * width : (q + 1) * width
            ]

    @pl.when(step == 0)
    def _():
        count = targets.shape[0]
        out[pl.ds(H * per_head, count), :] = targets[...].astype(F32)


def project_kernel(own_ref, *refs, parts):
    own = own_ref[0]
    part_refs = refs[:parts]
    lng, lnb, w4t, w3, gbc, zr, qt, kt, vt, qn, kn, vn, gt = refs[parts:]
    rows, side, _ = part_refs[0].shape
    width = H * HD
    for row in range(rows):
        for k in range(parts):
            block = lax.rem(own + parts - k, parts)
            zr[row, pl.ds(pl.multiple_of(block * side, side), side), :] = part_refs[k][row]

    def one_row(row):
        pair_row = zr[row].astype(F32)
        center = pair_row - jnp.mean(pair_row, axis=-1, keepdims=True)
        yield
        inverse = lax.rsqrt(jnp.mean(center * center, axis=-1, keepdims=True) + EPS)
        yield
        flat = (center * inverse * lng[...] + lnb[...]).astype(BF)
        yield
        for k, out in enumerate((qt, kt, vt)):
            out[row] = nt(w4t[k * width : (k + 1) * width], flat).astype(BF)
            yield
        gt[row] = jax.nn.sigmoid(nt(w4t[3 * width :], flat) + gbc[...])
        yield
        for k, out in enumerate((qn, kn, vn)):
            out[row] = nn(flat, w3[:, k * width : (k + 1) * width]).astype(BF)
            yield

    interleave([one_row(row) for row in range(rows)], PROJ_PACE)


def head_blocks(packed):
    rows, lanes = packed.shape
    blocks = []
    for h in range(H):
        pieces = []
        if h:
            pieces.append(jnp.zeros((h * HD, lanes), packed.dtype))
        pieces.append(packed[h * HD : (h + 1) * HD])
        if h < H - 1:
            pieces.append(jnp.zeros((rows - (h + 1) * HD, lanes), packed.dtype))
        blocks.append(jnp.concatenate(pieces, axis=0))
    return jnp.concatenate(blocks, axis=1)


def head_rows(packed):
    lane = lax.broadcasted_iota(jnp.int32, packed.shape, 1) // HD
    zero = jnp.zeros_like(packed)
    return jnp.concatenate([jnp.where(lane == h, packed, zero) for h in range(H)], axis=0)


def forward_kernel(
    *refs, tiles, base, count, bias_rows, owner_rows, extra, grid_side, groups, group_rows
):
    gath = refs[:tiles]
    kn, qt, vt, gt, zr, wod, wdt = refs[tiles : tiles + 7]
    at, ot, ut, tgt, bias_t = refs[tiles + 7 + extra : tiles + 12 + extra]
    sends = refs[tiles + 12 + extra : 2 * tiles + 12 + extra]
    order, stage = refs[2 * tiles + 12 + extra :]
    step = pl.program_id(0)
    mine = lax.axis_index("tile")
    tile_i = mine // grid_side
    tile_j = lax.rem(mine, grid_side)
    rows = kn.shape[0]
    wide = kn.shape[1]
    side = wide // grid_side
    per_head = side * side // wide
    share = groups * group_rows
    span = side // groups

    @pl.when(step == 0)
    def _():
        for k in range(tiles):
            order[mine ^ k] = gath[k][...]
        lane = lax.broadcasted_iota(jnp.int32, (per_head, wide), 1) // side
        for h in range(H):
            pieces = []
            for i in range(grid_side):
                for f in range(grid_side):
                    total = None
                    for j in range(grid_side):
                        part = order[i * grid_side + j, h * per_head : (h + 1) * per_head, :]
                        turn = ((j - f) * side) % wide
                        if turn:
                            part = pltpu.roll(part, turn, 1)
                        total = part if total is None else jnp.where(lane == j, part, total)
                    pieces.append(total)
            bias_t[h] = jnp.concatenate(pieces, axis=0).T * LOG2E

    for row in range(rows):
        within = (base + step) * span + tile_j * group_rows + row
        tgt[row : row + 1, :] = order[
            within // owner_rows,
            pl.ds(bias_rows + lax.rem(within, owner_rows) * grid_side + tile_i, 1),
            :,
        ]

    scale = LOG2E / math.sqrt(HD)

    def one_row(row):
        blocks = head_blocks(qt[row])
        outs = []
        for pair in range(0, H, 2):
            scores = nn(kn[row], blocks[:, pair * wide : (pair + 2) * wide])
            yield
            for h in range(pair, pair + 2):
                part = scores[:, (h - pair) * wide : (h - pair + 1) * wide] * scale + bias_t[h]
                peak = jnp.max(part, axis=0, keepdims=True)
                yield
                part = jnp.exp2(part - peak)
                total = jnp.sum(part, axis=0, keepdims=True)
                yield
                part_b = (part * (1.0 / total)).astype(BF)
                at[row, :, h * wide : (h + 1) * wide] = part_b
                yield
                outs.append(nn(vt[row, h * HD : (h + 1) * HD, :], part_b))
                ot[row, h * HD : (h + 1) * HD, :] = outs[-1]
                yield
        gated = (gt[row] * ot[row]).astype(BF)
        yield
        both = nn(wod[...], gated) + nt(wdt[...], zr[row])
        yield
        logit = both[:NB] + both[NB:]
        ut[row] = logit
        high = logit.astype(BF).astype(F32)
        yield
        packed = jnp.concatenate([high, logit - high], axis=0).T
        here = step * rows + row
        yield
        for i in range(grid_side):
            for p in range(groups):
                for j in range(grid_side):
                    source = ((i * groups + p) * grid_side + j) * group_rows
                    target = ((i * grid_side + j) * share + p * group_rows) * count
                    stage[pl.ds(target + here, group_rows, stride=count), :] = packed[
                        source : source + group_rows
                    ]
                yield

    interleave([one_row(row) for row in range(rows)], FWD_PACE)

    @pl.when(step == pl.num_programs(0) - 1)
    def _():
        for k in range(tiles):
            start = (mine ^ k) * (share * count)
            for r in range(share):
                sends[k][r] = stage[
                    pl.ds(pl.multiple_of(start + r * count, 8), count), :
                ].astype(BF)


def backward_kernel(*refs, tiles, chunks, grid_side, groups, group_rows):
    rcv = refs[: tiles * chunks]
    tgt, at, ot, ut, gt, vn, kt, qn, zr, wo, wd3, wqg, wkv, lgc, cst, dzm = refs[
        tiles * chunks : tiles * chunks + 16
    ]
    sends = refs[tiles * chunks + 16 : tiles * chunks + 16 + tiles]
    acc, grad_s, gate_s, value_s, score_s, query_s, mirror_s, order = refs[
        tiles * chunks + 16 + tiles :
    ]
    step = pl.program_id(0)
    mine = lax.axis_index("tile")
    rows = vn.shape[0]
    wide = vn.shape[1]
    chunk_groups = groups // chunks
    share = groups * group_rows
    inv_root = 1.0 / math.sqrt(HD)
    ident = eye(wide)
    adder = jnp.concatenate([ident[:NB, :NB], ident[:NB, :NB]], axis=1)
    bins = lax.broadcasted_iota(jnp.int32, (NB, wide), 0).astype(F32)

    @pl.when(step == 0)
    def _():
        acc[...] = jnp.zeros_like(acc)

    def one_row(row):
        for k in range(tiles):
            source_i = (mine ^ k) // grid_side
            source_j = lax.rem(mine ^ k, grid_side)
            for p in range(groups):
                start = ((source_i * groups + p) * grid_side + source_j) * group_rows
                local = (p % chunk_groups) * group_rows
                mirror_s[row, pl.ds(pl.multiple_of(start, group_rows), group_rows), :] = rcv[
                    (p // chunk_groups) * tiles + k
                ][row, local : local + group_rows].astype(F32)
        yield
        other = nt(adder, mirror_s[row].astype(BF))
        yield
        logits = ut[row] + other + cst[...]
        peak = jnp.max(logits, axis=0, keepdims=True)
        yield
        probs = jnp.exp(logits - peak)
        total = jnp.sum(probs, axis=0, keepdims=True)
        yield
        resid = 2.0 * (probs * (1.0 / total) - jnp.where(bins == tgt[row : row + 1, :], 1.0, 0.0))
        res_hi, res_lo = split(resid)
        yield
        pair_grad = nn(wd3[...], jnp.concatenate([res_hi, res_lo, res_hi], axis=0))
        dzm[row] = pair_grad
        yield
        out_grad = nn(wo[...], pair_grad.astype(BF))
        yield
        gate = gt[row]
        gated = out_grad * gate
        grad_s[row] = gated.astype(BF)
        yield
        gate_s[row] = (gated * ot[row] * (1.0 - gate)).astype(BF)
        yield
        grad_n = gated.T.astype(BF)
        yield
        value_s[row] = nn(at[row], head_rows(grad_n)).astype(BF)
        yield
        blocks = head_blocks(grad_s[row])
        yield
        for pair in range(0, H, 2):
            weight_grad = nn(vn[row], blocks[:, pair * wide : (pair + 2) * wide])
            yield
            for h in range(pair, pair + 2):
                prob = at[row, :, h * wide : (h + 1) * wide].astype(F32)
                prod = prob * weight_grad[:, (h - pair) * wide : (h - pair + 1) * wide]
                total = jnp.sum(prod, axis=0, keepdims=True)
                yield
                prod = prod - prob * total
                score_s[row, :, h * wide : (h + 1) * wide] = prod.astype(BF)
                acc[h] += prod
                yield
                query_s[row, h * HD : (h + 1) * HD, :] = (
                    nn(kt[row, h * HD : (h + 1) * HD, :], score_s[row, :, h * wide : (h + 1) * wide])
                    * inv_root
                ).astype(BF)
                yield
        key_grad = nn(score_s[row], head_rows(qn[row])) * inv_root
        yield
        normed_grad = nn(wqg[...], jnp.concatenate([query_s[row], gate_s[row]], axis=0)) + nt(
            wkv[...], jnp.concatenate([key_grad.astype(BF), value_s[row]], axis=1)
        )
        yield
        pair_t = nt(ident, zr[row])
        center = pair_t - jnp.mean(pair_t, axis=0, keepdims=True)
        yield
        inverse = lax.rsqrt(jnp.mean(center * center, axis=0, keepdims=True) + EPS)
        normed = center * inverse
        yield
        scaled = normed_grad * lgc[...]
        mean_a = jnp.mean(scaled, axis=0, keepdims=True)
        mean_b = jnp.mean(scaled * normed, axis=0, keepdims=True)
        yield
        dzm[row] = dzm[row] + inverse * (scaled - mean_a - normed * mean_b)
        yield

    interleave([one_row(row) for row in range(rows)], BWD_PACE)

    @pl.when(step == pl.num_programs(0) - 1)
    def _():
        for h in range(H):
            grad = acc[h].T
            for i in range(grid_side):
                for j in range(grid_side):
                    pieces = []
                    for p in range(groups):
                        source = ((i * groups + p) * grid_side + j) * group_rows
                        pieces.append(grad[source : source + group_rows])
                    order[i * grid_side + j, h * share : (h + 1) * share, :] = jnp.concatenate(
                        pieces, axis=0
                    )
        for k in range(tiles):
            sends[k][...] = order[mine ^ k].reshape(H, share, wide).astype(BF)


def finish_kernel(offsets, *refs, tiles):
    rdb = refs[:tiles]
    dzm, zr, wgc, out, sums = refs[tiles:]
    step = pl.program_id(0)
    rows, chans, wide = dzm.shape
    states, _, piece, _ = out.shape
    total_rows = rdb[0].shape[1]
    turn = offsets[lax.axis_index("state")] // piece

    @pl.when(step == 0)
    def _():
        for h in range(H):
            total = rdb[0][h].astype(F32)
            for part in rdb[1:]:
                total = total + part[h].astype(F32)
            sums[pl.ds(h * total_rows, total_rows), :] = total

    ident = eye(chans)

    def one_row(row):
        local = step * rows + row
        pair_t = nt(ident, zr[row])
        yield
        center = pair_t - jnp.mean(pair_t, axis=0, keepdims=True)
        yield
        inverse = lax.rsqrt(jnp.mean(center * center, axis=0, keepdims=True) + EPS)
        normed = center * inverse
        yield
        scaled = None
        for h in range(H):
            term = wgc[h] * sums[pl.ds(h * total_rows + local, 1), :]
            scaled = term if scaled is None else scaled + term
        yield
        mean_a = jnp.mean(scaled, axis=0, keepdims=True)
        mean_b = jnp.mean(scaled * normed, axis=0, keepdims=True)
        yield
        total = dzm[row] + inverse * (scaled - mean_a - normed * mean_b)
        yield
        total = total.T.astype(BF)
        for c in range(wide // piece):
            out[lax.rem(turn + c, states), row] = total[c * piece : (c + 1) * piece]
        yield

    interleave([one_row(row) for row in range(rows)], FIN_PACE)


def place_kernel(offsets, rcv, out, *, side):
    states, grid_side, rows, piece, chans = rcv.shape
    start = lax.axis_index("state") * piece
    out[...] = jnp.zeros_like(out)
    for s in range(states):
        offset = offsets[s]
        half = (start < offset).astype(jnp.int32)
        base = offset // side
        for i in range(grid_side):
            out[base + i, :, half] += rcv[s, i].astype(F32)


def on_device(
    pair_tiles,
    targets,
    offsets,
    ln_gain,
    ln_bias,
    w_query,
    w_key,
    w_value,
    w_pairbias,
    w_gate,
    gate_bias,
    w_output,
    out_bias,
    w_distogram,
    dist_bias,
):
    tiles = lax.axis_size("tile")
    states = lax.axis_size("state")
    side, chans = pair_tiles.shape[3], pair_tiles.shape[4]
    wide = targets.shape[4]
    grid_side = wide // side
    owner_rows = side // tiles
    width = H * HD
    here = lax.axis_index("tile")
    tile_i = here // grid_side
    tile_j = lax.rem(here, grid_side)
    even = owner_rows % grid_side == 0
    groups = tiles if even else 1
    group_rows = side // groups // grid_side
    share = groups * group_rows
    per_head = side * side // wide
    piece = wide // states

    def shapes(*pairs):
        return [jax.ShapeDtypeStruct(s, t) for s, t in pairs]

    tile = pair_tiles.reshape(groups, grid_side, group_rows, side, chans)

    def rows_of(j):
        return lax.dynamic_index_in_dim(tile, j, 1, keepdims=False).reshape(share, side, chans)

    parts = [tile]
    for k in range(1, grid_side):
        perm = [
            (i * grid_side + j, i * grid_side + (j + k) % grid_side)
            for i in range(grid_side)
            for j in range(grid_side)
        ]
        parts.append(lax.ppermute(rows_of(lax.rem(tile_j + k, grid_side)), "tile", perm))

    gain_row = ln_gain.reshape(1, chans)
    shift_row = ln_bias.reshape(1, chans)
    prep_shapes = shapes(
        ((4 * width, chans), BF),
        ((chans, 3 * width), BF),
        ((2 * NB, width), BF),
        ((2 * NB, chans), BF),
        ((chans, 3 * NB), BF),
        ((chans, 2 * width), BF),
        ((chans, 2 * width), BF),
        ((width, wide), F32),
        ((chans, wide), F32),
        ((NB, wide), F32),
        ((H, chans, wide), F32),
    )
    w4t, w3, wod, wdt, wd3, wqg, wkv, gbc, lgc, cst, wgc = pl.pallas_call(
        prep_kernel, out_shape=prep_shapes, name="prep"
    )(
        w_query,
        w_key,
        w_value,
        w_gate,
        w_output,
        gate_bias.reshape(1, width),
        out_bias.reshape(1, chans),
        w_distogram.T,
        dist_bias.reshape(1, NB),
        w_pairbias.T,
        gain_row,
    )

    lines = 8
    bias_rows = H * per_head
    target_rows = owner_rows * grid_side
    bias_mine = pl.pallas_call(
        functools.partial(bias_kernel, per_head=per_head),
        grid=(per_head // lines,),
        in_specs=[
            pl.BlockSpec((grid_side, lines, side, chans), lambda g: (0, g, 0, 0)),
            full((target_rows, wide)),
            full((1, chans)),
            full((1, chans)),
            full((H, chans)),
        ],
        out_specs=full((bias_rows + target_rows, wide)),
        out_shape=jax.ShapeDtypeStruct((bias_rows + target_rows, wide), F32),
        name="bias",
    )(
        pair_tiles.reshape(grid_side, per_head, side, chans),
        targets.reshape(target_rows, wide),
        gain_row,
        shift_row,
        w_pairbias.T,
    )

    def to_partner(value, k):
        return lax.ppermute(value, "tile", [(t, t ^ k) for t in range(tiles)]) if k else value

    gathered = [to_partner(bias_mine, k) for k in range(tiles)]

    def by_row(*shape, rows, base=0):
        return pl.BlockSpec((rows,) + shape, lambda g, *_: (g + base,) + (0,) * len(shape))

    def cost(flops, moved):
        return pl.CostEstimate(flops=flops, bytes_accessed=moved, transcendentals=0)

    cell = wide * width * wide
    square_b = ((share, wide, width), BF)
    zr, qt, kt, vt, qn, kn, vn, gt = pl.pallas_call(
        functools.partial(project_kernel, parts=grid_side),
        grid_spec=pltpu.PrefetchScalarGridSpec(
            num_scalar_prefetch=1,
            grid=(groups,),
            in_specs=[
                pl.BlockSpec(
                    (None, None, group_rows, side, chans), lambda g, own: (g, own[0], 0, 0, 0)
                )
            ]
            + [by_row(side, chans, rows=group_rows)] * (grid_side - 1)
            + [full((1, chans)), full((1, chans)), full(w4t.shape), full(w3.shape), full(gbc.shape)],
            out_specs=[by_row(wide, width, rows=group_rows)] * 8,
        ),
        out_shape=shapes(*([square_b] * 7), ((share, width, wide), F32)),
        cost_estimate=cost(80 * share * cell, 12 * share * wide * width * 2),
        name="project",
    )(tile_j.reshape(1), *parts, gain_row, shift_row, w4t, w3, gbc)

    chunks = 2 if groups % 2 == 0 else 1
    chunk_groups = groups // chunks
    count = share // chunks
    block = group_rows
    layout = dict(grid_side=grid_side, groups=groups, group_rows=group_rows)
    saved_shapes = shapes(
        ((share, wide, H * wide), BF),
        ((share, width, wide), F32),
        ((share, NB, wide), F32),
        ((share, wide), F32),
        ((H, wide, wide), F32),
    )
    packed_shape = (share, count, 2 * NB)
    saved = []
    mirrored = []
    for c in range(chunks):
        base = c * chunk_groups
        inputs = [*gathered, kn, qt, vt, gt, zr, wod, wdt]
        first = len(inputs)
        call = pl.pallas_call(
            functools.partial(
                forward_kernel,
                tiles=tiles,
                base=base,
                count=count,
                bias_rows=bias_rows,
                owner_rows=owner_rows,
                extra=len(saved),
                **layout,
            ),
            grid=(count // block,),
            in_specs=[full(gathered[0].shape)] * tiles
            + [by_row(wide, width, rows=block, base=base)] * 5
            + [full(wod.shape), full(wdt.shape)]
            + [pl.BlockSpec(memory_space=pl.ANY)] * len(saved),
            out_specs=[
                by_row(wide, H * wide, rows=block, base=base),
                by_row(width, wide, rows=block, base=base),
                by_row(NB, wide, rows=block, base=base),
                by_row(wide, rows=block, base=base),
                full((H, wide, wide)),
            ]
            + [full(packed_shape)] * tiles,
            out_shape=saved_shapes + shapes(*([(packed_shape, BF)] * tiles)),
            scratch_shapes=[
                pltpu.VMEM((tiles,) + gathered[0].shape, F32),
                pltpu.VMEM((tiles * share * count, 2 * NB), F32),
            ],
            input_output_aliases={first + n: n for n in range(len(saved))},
            cost_estimate=cost(150 * count * cell, 14 * count * wide * width * 2),
            name="forward",
        )
        results = call(*inputs, *saved)
        saved = list(results[:4])
        mirrored.append([to_partner(results[5 + k], k) for k in range(tiles)])
    at, ot, ut, tgt = saved

    results = pl.pallas_call(
        functools.partial(backward_kernel, tiles=tiles, chunks=chunks, **layout),
        grid=(share // block,),
        in_specs=[by_row(count, 2 * NB, rows=block)] * (tiles * chunks)
        + [
            by_row(wide, rows=block),
            by_row(wide, H * wide, rows=block),
            by_row(width, wide, rows=block),
            by_row(NB, wide, rows=block),
        ]
        + [by_row(wide, width, rows=block)] * 5
        + [full(w.shape) for w in (w_output, wd3, wqg, wkv, lgc, cst)],
        out_specs=[by_row(chans, wide, rows=block)] + [full((H, share, wide))] * tiles,
        out_shape=shapes(((share, chans, wide), F32), *([((H, share, wide), BF)] * tiles)),
        scratch_shapes=[pltpu.VMEM((H, wide, wide), F32)]
        + [
            pltpu.VMEM((block,) + shape, BF)
            for shape in ((width, wide), (width, wide), (wide, width), (wide, H * wide), (width, wide))
        ]
        + [pltpu.VMEM((block, wide, 2 * NB), F32), pltpu.VMEM((tiles, H * share, wide), F32)],
        cost_estimate=cost(500 * share * cell, 20 * share * wide * width * 2),
        name="backward",
    )(
        *[part for parts_c in mirrored for part in parts_c],
        tgt, at, ot, ut, gt, vn, kt, qn, zr, w_output, wd3, wqg, wkv, lgc, cst,
    )
    dzm = results[0]
    rdb = [to_partner(results[1 + k], k) for k in range(tiles)]

    block = FIN_ROWS if share % FIN_ROWS == 0 else 1
    outgoing = pl.pallas_call(
        functools.partial(finish_kernel, tiles=tiles),
        grid_spec=pltpu.PrefetchScalarGridSpec(
            num_scalar_prefetch=1,
            grid=(share // block,),
            in_specs=[
                *([full(rdb[0].shape)] * tiles),
                pl.BlockSpec((block, chans, wide), lambda g, _: (g, 0, 0)),
                pl.BlockSpec((block, wide, chans), lambda g, _: (g, 0, 0)),
                full(wgc.shape),
            ],
            out_specs=pl.BlockSpec((states, block, piece, chans), lambda g, _: (0, g, 0, 0)),
            scratch_shapes=[pltpu.VMEM((H * share, wide), F32)],
        ),
        out_shape=jax.ShapeDtypeStruct((states, share, piece, chans), BF),
        name="finish",
    )(offsets, *rdb, dzm, zr, wgc)

    if even:
        slots = outgoing.reshape(states * tiles, group_rows, piece, chans)
    else:
        slots = lax.dynamic_update_slice(
            jnp.zeros((states, tiles, owner_rows, piece, chans), BF),
            outgoing.reshape(states, grid_side, owner_rows, piece, chans),
            (0, tile_j * grid_side, 0, 0, 0),
        ).reshape(states * tiles, owner_rows, piece, chans)
    received = lax.all_to_all(slots, ("state", "tile"), split_axis=0, concat_axis=0, tiled=True)
    if even:
        received = received.reshape(states, grid_side, owner_rows, piece, chans)
    else:
        received = lax.dynamic_index_in_dim(
            received.reshape(states, grid_side, grid_side, owner_rows, piece, chans),
            tile_i,
            2,
            keepdims=False,
        )

    block = 4 if owner_rows % 4 == 0 else 1
    out_shape = (2 * grid_side, owner_rows, 2, piece, chans)
    placed = pl.pallas_call(
        functools.partial(place_kernel, side=side),
        grid_spec=pltpu.PrefetchScalarGridSpec(
            num_scalar_prefetch=1,
            grid=(owner_rows // block,),
            in_specs=[
                pl.BlockSpec(
                    (states, grid_side, block, piece, chans), lambda g, _: (0, 0, g, 0, 0)
                )
            ],
            out_specs=pl.BlockSpec(
                (2 * grid_side, block, 2, piece, chans), lambda g, _: (0, g, 0, 0, 0)
            ),
        ),
        out_shape=jax.ShapeDtypeStruct(out_shape, F32),
        name="place",
    )(offsets, received)
    return placed.reshape(2 * grid_side, 1, owner_rows, 2, piece, chans)


def solution(mesh):
    in_specs = (
        P("state", "tile", None, None, None),
        P("state", "tile", None, None, None),
    ) + (P(),) * 13
    out_specs = P(None, "tile", None, None, "state", None)
    return jax.shard_map(
        on_device, mesh=mesh, in_specs=in_specs, out_specs=out_specs, check_vma=False
    )
```

```python
import functools
import math

import jax
import jax.numpy as jnp
from jax import lax
from jax.experimental import pallas as pl
from jax.experimental.pallas import tpu as pltpu
from jax.sharding import PartitionSpec as P

H = 4
HD = 32
NB = 64
FWD_ROWS = 8
BWD_ROWS = 8
FWD_PACE = (8, 1, 0)
BWD_PACE = (2, 0, 3)
PROJ_PACE = (2, 0, 3)
FIN_PACE = (8, 1, 0)
PROJ_ROWS = 8
FIN_ROWS = 8
EPS = 1e-5
LOG2E = 1.0 / math.log(2.0)
BF = jnp.bfloat16
F32 = jnp.float32
HIGHEST = lax.Precision.HIGHEST


def nn(left, right, **kw):
    return lax.dot_general(left, right, (((1,), (0,)), ((), ())), preferred_element_type=F32, **kw)


def nt(left, right, **kw):
    return lax.dot_general(left, right, (((1,), (1,)), ((), ())), preferred_element_type=F32, **kw)


def split(value):
    high = value.astype(BF)
    low = (value - high.astype(F32)).astype(BF)
    return high, low


def transposed(value):
    return value.astype(F32).T.astype(value.dtype)


def column(row, lanes):
    return jnp.broadcast_to(row, (lanes, row.shape[1])).T


def eye(size):
    rows = lax.broadcasted_iota(jnp.int32, (size, size), 0)
    cols = lax.broadcasted_iota(jnp.int32, (size, size), 1)
    return jnp.where(rows == cols, 1.0, 0.0).astype(BF)


def rows_norm(pair_rows):
    mean = jnp.mean(pair_rows, axis=-1, keepdims=True)
    center = pair_rows - mean
    inverse = lax.rsqrt(jnp.mean(center * center, axis=-1, keepdims=True) + EPS)
    return center * inverse


def interleave(rows, pace):
    size, inner, outer = pace
    begin = {row: (r % size) * inner + (r // size) * outer for r, row in enumerate(rows)}
    tick = 0
    while begin:
        for row in list(begin):
            if begin[row] <= tick:
                try:
                    next(row)
                except StopIteration:
                    del begin[row]
        tick += 1


def full(shape):
    return pl.BlockSpec(shape, lambda *_: (0,) * len(shape))


def prep_kernel(wq, wk, wv, wg, wo, gb, ob, wd, db, wpb, lng, w4t, w2, wod, wdt, wd3, wall, gbc, lgc, cst, wgs):
    wide = gbc.shape[1]
    w4t[...] = jnp.concatenate([transposed(w[...]) for w in (wq, wk, wv, wg)], axis=0)
    w2[...] = jnp.concatenate([wk[...], wv[...]], axis=1)
    wall[...] = jnp.concatenate([wq[...], wk[...], wv[...], wg[...]], axis=1)
    dist_t = wd[...]
    dist = dist_t.T
    dist_hi, dist_lo = split(dist)
    wd3[...] = jnp.concatenate([dist_hi, dist_hi, dist_lo], axis=1)
    wdt[...] = jnp.concatenate(split(dist_t), axis=0)
    both = nn(wo[...].astype(F32), dist, precision=HIGHEST)
    wod[...] = jnp.concatenate(split(both.T), axis=0)
    gbc[...] = column(gb[...], wide)
    lgc[...] = column(lng[...], wide)
    shift = 2.0 * jnp.sum(dist_t * ob[...], axis=1, keepdims=True)
    cst[...] = column(db[...], wide) + shift
    proj = jnp.concatenate([wpb[...], jnp.zeros((wide - H, wpb.shape[1]), F32)], axis=0).T[:, :H]
    proj_hi, proj_lo = split(proj)
    wgs[...] = jnp.concatenate([proj_hi, proj_hi, proj_lo, jnp.zeros_like(proj_lo)], axis=1)


def bias_kernel(tile, targets, lng, lnb, wpb, out, *, per_head):
    step = pl.program_id(0)
    fold, lines, side, chans = tile.shape
    pieces = [tile[f, q] for q in range(lines) for f in range(fold)]
    pair = jnp.concatenate(pieces, axis=0)
    proj = wpb[...] * lng[...]
    high, rest = split(proj)
    mid = rest
    last = (proj - high.astype(F32) - mid.astype(F32)).astype(BF)
    left = jnp.concatenate(
        [high.astype(F32), mid.astype(F32), last.astype(F32), jnp.ones((H, chans), F32)], axis=0
    ).astype(BF)
    left = jnp.concatenate([eye(chans), left], axis=0)
    total = jnp.sum(proj, axis=1, keepdims=True)
    const = jnp.sum(wpb[...] * lnb[...], axis=1, keepdims=True)
    size = fold * side
    rows_out = []
    for q in range(lines):
        up = nt(left, pair[q * size : (q + 1) * size])
        extra = up[chans:]
        mean = extra[3 * H : 3 * H + 1] * (1.0 / chans)
        center = up[:chans] - mean
        inverse = lax.rsqrt(jnp.mean(center * center, axis=0, keepdims=True) + EPS)
        dotted = extra[:H] + extra[H : 2 * H] + extra[2 * H : 3 * H]
        rows_out.append(inverse * (dotted - mean * total) + const)
    bias = jnp.concatenate(rows_out, axis=1)
    width = fold * side
    for q in range(lines):
        for h in range(H):
            out[pl.ds(h * per_head + step * lines + q, 1), :] = bias[
                h : h + 1, q * width : (q + 1) * width
            ]

    @pl.when(step == 0)
    def _():
        count = targets.shape[0]
        out[pl.ds(H * per_head, count), :] = targets[...].astype(F32)


def project_kernel(own_ref, *refs, parts):
    own = own_ref[0]
    part_refs = refs[:parts]
    lng, lnb, w4t, w2, gbc, zr, qt, kt, vt, kn, vn, gt, flat_s = refs[parts:]
    rows, side, _ = part_refs[0].shape
    wide = zr.shape[1]
    width = H * HD
    for row in range(rows):
        for k in range(parts):
            block = lax.rem(own + parts - k, parts)
            zr[row, pl.ds(pl.multiple_of(block * side, side), side), :] = part_refs[k][row]

    def one_row(row):
        pair_row = zr[row].astype(F32)
        center = pair_row - jnp.mean(pair_row, axis=-1, keepdims=True)
        yield
        inverse = lax.rsqrt(jnp.mean(center * center, axis=-1, keepdims=True) + EPS)
        yield
        flat_s[row * wide : (row + 1) * wide, :] = (
            center * inverse * lng[...] + lnb[...]
        ).astype(BF)
        yield

    def one_pair(first):
        both = one_row(first), one_row(first + 1)
        for _ in range(3):
            for row in both:
                next(row)
            yield
        flat = flat_s[first * wide : (first + 2) * wide, :]
        for k, out in enumerate((qt, kt, vt)):
            up = nt(w4t[k * width : (k + 1) * width], flat)
            for n in range(2):
                out[first + n] = up[:, n * wide : (n + 1) * wide].astype(BF)
            yield
        up = nt(w4t[3 * width :], flat)
        for n in range(2):
            gt[first + n] = jax.nn.sigmoid(up[:, n * wide : (n + 1) * wide] + gbc[...])
            yield
        down = nn(flat, w2[...])
        for n in range(2):
            kn[first + n] = down[n * wide : (n + 1) * wide, :width].astype(BF)
            vn[first + n] = down[n * wide : (n + 1) * wide, width:].astype(BF)
        yield

    interleave([one_pair(row) for row in range(0, rows, 2)], PROJ_PACE)


def head_block(part, h):
    lanes = part.shape[1]
    pieces = []
    if h:
        pieces.append(jnp.zeros((h * HD, lanes), part.dtype))
    pieces.append(part)
    if h < H - 1:
        pieces.append(jnp.zeros(((H - 1 - h) * HD, lanes), part.dtype))
    return jnp.concatenate(pieces, axis=0)


def head_blocks(packed):
    return jnp.concatenate(
        [head_block(packed[h * HD : (h + 1) * HD], h) for h in range(H)], axis=1
    )


def forward_kernel(
    *refs, tiles, base, count, bias_rows, owner_rows, extra, grid_side, groups, group_rows
):
    gath = refs[:tiles]
    kn, qt, vt, gt, zr, wod, wdt = refs[tiles : tiles + 7]
    at, ot, ut, tgt, bias_t = refs[tiles + 7 + extra : tiles + 12 + extra]
    sends = refs[tiles + 12 + extra : 2 * tiles + 12 + extra]
    order, stage = refs[2 * tiles + 12 + extra :]
    step = pl.program_id(0)
    mine = lax.axis_index("tile")
    tile_i = mine // grid_side
    tile_j = lax.rem(mine, grid_side)
    rows = kn.shape[0]
    wide = kn.shape[1]
    side = wide // grid_side
    per_head = side * side // wide
    share = groups * group_rows
    span = side // groups

    @pl.when(step == 0)
    def _():
        for k in range(tiles):
            order[mine ^ k] = gath[k][...]
        lane = lax.broadcasted_iota(jnp.int32, (per_head, wide), 1) // side
        for h in range(H):
            pieces = []
            for i in range(grid_side):
                for f in range(grid_side):
                    total = None
                    for j in range(grid_side):
                        part = order[i * grid_side + j, h * per_head : (h + 1) * per_head, :]
                        turn = ((j - f) * side) % wide
                        if turn:
                            part = pltpu.roll(part, turn, 1)
                        total = part if total is None else jnp.where(lane == j, part, total)
                    pieces.append(total)
            bias_t[h] = jnp.concatenate(pieces, axis=0).T * LOG2E

    for row in range(rows):
        within = (base + step) * span + tile_j * group_rows + row
        tgt[row : row + 1, :] = order[
            within // owner_rows,
            pl.ds(bias_rows + lax.rem(within, owner_rows) * grid_side + tile_i, 1),
            :,
        ]

    scale = LOG2E / math.sqrt(HD)

    def one_row(row):
        blocks = head_blocks(qt[row])
        outs = []
        for pair in range(0, H, 2):
            scores = nn(kn[row], blocks[:, pair * wide : (pair + 2) * wide])
            yield
            for h in range(pair, pair + 2):
                part = scores[:, (h - pair) * wide : (h - pair + 1) * wide] * scale + bias_t[h]
                peak = jnp.max(part, axis=0, keepdims=True)
                yield
                part = jnp.exp2(part - peak)
                total = jnp.sum(part, axis=0, keepdims=True)
                yield
                part_b = (part * (1.0 / total)).astype(BF)
                at[row, :, h * wide : (h + 1) * wide] = part_b
                yield
                outs.append(nn(vt[row, h * HD : (h + 1) * HD, :], part_b))
                ot[row, h * HD : (h + 1) * HD, :] = outs[-1]
                yield
        gated = (gt[row] * ot[row]).astype(BF)
        yield
        both = nn(wod[...], gated) + nt(wdt[...], zr[row])
        yield
        logit = both[:NB] + both[NB:]
        ut[row] = logit
        high = logit.astype(BF).astype(F32)
        yield
        packed = jnp.concatenate([high, logit - high], axis=0).T
        here = step * rows + row
        yield
        for i in range(grid_side):
            for p in range(groups):
                for j in range(grid_side):
                    source = ((i * groups + p) * grid_side + j) * group_rows
                    target = ((i * grid_side + j) * share + p * group_rows) * count
                    stage[pl.ds(target + here, group_rows, stride=count), :] = packed[
                        source : source + group_rows
                    ]
                yield

    interleave([one_row(row) for row in range(rows)], FWD_PACE)

    @pl.when(step == pl.num_programs(0) - 1)
    def _():
        for k in range(tiles):
            start = (mine ^ k) * (share * count)
            for r in range(share):
                sends[k][r] = stage[
                    pl.ds(pl.multiple_of(start + r * count, 8), count), :
                ].astype(BF)


def backward_kernel(*refs, tiles, chunks, grid_side, groups, group_rows):
    rcv = refs[: tiles * chunks]
    tgt, at, ot, ut, gt, vn, kt, qt, wo, wd3, wall, cst, dpt, dzn = refs[
        tiles * chunks : tiles * chunks + 14
    ]
    sends = refs[tiles * chunks + 14 : tiles * chunks + 14 + tiles]
    acc, grad_s, back_s, mirror_s, order = refs[tiles * chunks + 14 + tiles :]
    width = H * HD
    step = pl.program_id(0)
    mine = lax.axis_index("tile")
    rows = vn.shape[0]
    wide = vn.shape[1]
    chunk_groups = groups // chunks
    share = groups * group_rows
    inv_root = 1.0 / math.sqrt(HD)
    adder = jnp.concatenate([eye(NB)] * 2, axis=1)
    bins = lax.broadcasted_iota(jnp.int32, (NB, 2 * wide), 0).astype(F32)

    @pl.when(step == 0)
    def _():
        acc[...] = jnp.zeros_like(acc)

    shift = jnp.concatenate([cst[...]] * 2, axis=1)

    def one_pair(first):
        pair = (first, first + 1)
        for row in pair:
            for k in range(tiles):
                source_i = (mine ^ k) // grid_side
                source_j = lax.rem(mine ^ k, grid_side)
                for p in range(groups):
                    start = ((source_i * groups + p) * grid_side + source_j) * group_rows
                    local = (p % chunk_groups) * group_rows
                    mirror_s[pl.ds(pl.multiple_of(row * wide + start, group_rows), group_rows), :] = rcv[
                        (p // chunk_groups) * tiles + k
                    ][row, local : local + group_rows].astype(F32)
        yield
        other = nt(adder, mirror_s[first * wide : (first + 2) * wide, :].astype(BF))
        yield
        logits = jnp.concatenate([ut[row] for row in pair], axis=1) + other + shift
        peak = jnp.max(logits, axis=0, keepdims=True)
        yield
        probs = jnp.exp(logits - peak)
        total = jnp.sum(probs, axis=0, keepdims=True)
        yield
        target = jnp.concatenate([tgt[row : row + 1, :] for row in pair], axis=1)
        resid = 2.0 * (probs * (1.0 / total) - jnp.where(bins == target, 1.0, 0.0))
        res_hi, res_lo = split(resid)
        yield
        pair_grad = nn(wd3[...], jnp.concatenate([res_hi, res_lo, res_hi], axis=0))
        for n, row in enumerate(pair):
            dpt[row] = pair_grad[:, n * wide : (n + 1) * wide]
        yield
        out_grad = nn(wo[...], pair_grad.astype(BF))
        yield
        for n, row in enumerate(pair):
            gate = gt[row]
            gated = out_grad[:, n * wide : (n + 1) * wide] * gate
            grad_s[row] = gated.astype(BF)
            back_s[3 * width :, row * wide : (row + 1) * wide] = (
                gated * ot[row] * (1.0 - gate)
            ).astype(BF)
            yield

        def heads(row):
            lanes = slice(row * wide, (row + 1) * wide)
            for h in range(H):
                part = slice(h * HD, (h + 1) * HD)
                back_s[2 * width + h * HD : 2 * width + (h + 1) * HD, lanes] = nt(
                    grad_s[row, part, :], at[row, :, h * wide : (h + 1) * wide]
                ).astype(BF)
                yield
                weight_grad = nn(vn[row], head_block(grad_s[row, part, :], h))
                yield
                prob = at[row, :, h * wide : (h + 1) * wide].astype(F32)
                prod = prob * weight_grad
                total = jnp.sum(prod, axis=0, keepdims=True)
                yield
                prod = prod - prob * total
                prod_b = prod.astype(BF)
                acc[h] += prod
                yield
                back_s[h * HD : (h + 1) * HD, lanes] = (nn(kt[row, part, :], prod_b) * inv_root).astype(BF)
                back_s[width + h * HD : width + (h + 1) * HD, lanes] = (
                    nt(qt[row, part, :], prod_b) * inv_root
                ).astype(BF)
                yield

        both = [heads(row) for row in pair]
        while both:
            for row in list(both):
                try:
                    next(row)
                except StopIteration:
                    both.remove(row)
            yield
        normed_grad = nn(wall[...], back_s[:, first * wide : (first + 2) * wide])
        for n, row in enumerate(pair):
            dzn[row] = normed_grad[:, n * wide : (n + 1) * wide]
        yield

    interleave([one_pair(row) for row in range(0, rows, 2)], BWD_PACE)

    @pl.when(step == pl.num_programs(0) - 1)
    def _():
        for h in range(H):
            grad = acc[h].T
            for i in range(grid_side):
                for j in range(grid_side):
                    pieces = []
                    for p in range(groups):
                        source = ((i * groups + p) * grid_side + j) * group_rows
                        pieces.append(grad[source : source + group_rows])
                    order[i * grid_side + j, h * share : (h + 1) * share, :] = jnp.concatenate(
                        pieces, axis=0
                    )
        for k in range(tiles):
            sends[k][...] = order[mine ^ k].reshape(H, share, wide).astype(BF)


def finish_kernel(offsets, *refs, tiles):
    rdb = refs[:tiles]
    dpt, dzn, zr, wgs, lgc, out, sums = refs[tiles:]
    step = pl.program_id(0)
    rows, chans, wide = dzn.shape
    states, _, piece, _ = out.shape
    total_rows = rdb[0].shape[1]
    turn = offsets[lax.axis_index("state")] // piece

    @pl.when(step == 0)
    def _():
        for h in range(H):
            total = rdb[0][h].astype(F32)
            for part in rdb[1:]:
                total = total + part[h].astype(F32)
            sums[pl.ds(h * total_rows, total_rows), :] = total

    ident = eye(chans)

    def one_row(row):
        local = step * rows + row
        pair_t = nt(ident, zr[row])
        yield
        center = pair_t - jnp.mean(pair_t, axis=0, keepdims=True)
        yield
        inverse = lax.rsqrt(jnp.mean(center * center, axis=0, keepdims=True) + EPS)
        normed = center * inverse
        yield
        parts = [sums[pl.ds(h * total_rows + local, 1), :] for h in range(H)]
        high, low = split(jnp.concatenate(parts, axis=0))
        spread = jnp.concatenate([high.astype(F32), low.astype(F32), high.astype(F32), jnp.zeros((H, wide), F32)], axis=0)
        yield
        scaled = (dzn[row] + nn(wgs[...], spread.astype(BF))) * lgc[...]
        yield
        mean_a = jnp.mean(scaled, axis=0, keepdims=True)
        mean_b = jnp.mean(scaled * normed, axis=0, keepdims=True)
        yield
        total = dpt[row] + inverse * (scaled - mean_a - normed * mean_b)
        yield
        total = total.T.astype(BF)
        for c in range(wide // piece):
            out[lax.rem(turn + c, states), row] = total[c * piece : (c + 1) * piece]
        yield

    interleave([one_row(row) for row in range(rows)], FIN_PACE)


def place_kernel(offsets, rcv, out, *, side):
    states, grid_side, rows, piece, chans = rcv.shape
    start = lax.axis_index("state") * piece
    out[...] = jnp.zeros_like(out)
    for s in range(states):
        offset = offsets[s]
        half = (start < offset).astype(jnp.int32)
        base = offset // side
        for i in range(grid_side):
            out[base + i, :, half] += rcv[s, i].astype(F32)


def on_device(
    pair_tiles,
    targets,
    offsets,
    ln_gain,
    ln_bias,
    w_query,
    w_key,
    w_value,
    w_pairbias,
    w_gate,
    gate_bias,
    w_output,
    out_bias,
    w_distogram,
    dist_bias,
):
    tiles = lax.axis_size("tile")
    states = lax.axis_size("state")
    side, chans = pair_tiles.shape[3], pair_tiles.shape[4]
    wide = targets.shape[4]
    grid_side = wide // side
    owner_rows = side // tiles
    width = H * HD
    here = lax.axis_index("tile")
    tile_i = here // grid_side
    tile_j = lax.rem(here, grid_side)
    even = owner_rows % grid_side == 0
    groups = tiles if even else 1
    group_rows = side // groups // grid_side
    share = groups * group_rows
    per_head = side * side // wide
    piece = wide // states

    def shapes(*pairs):
        return [jax.ShapeDtypeStruct(s, t) for s, t in pairs]

    tile = pair_tiles.reshape(groups, grid_side, group_rows, side, chans)

    def rows_of(j):
        return lax.dynamic_index_in_dim(tile, j, 1, keepdims=False).reshape(share, side, chans)

    parts = [tile]
    for k in range(1, grid_side):
        perm = [
            (i * grid_side + j, i * grid_side + (j + k) % grid_side)
            for i in range(grid_side)
            for j in range(grid_side)
        ]
        parts.append(lax.ppermute(rows_of(lax.rem(tile_j + k, grid_side)), "tile", perm))

    gain_row = ln_gain.reshape(1, chans)
    shift_row = ln_bias.reshape(1, chans)
    prep_shapes = shapes(
        ((4 * width, chans), BF),
        ((chans, 2 * width), BF),
        ((2 * NB, width), BF),
        ((2 * NB, chans), BF),
        ((chans, 3 * NB), BF),
        ((chans, 4 * width), BF),
        ((width, wide), F32),
        ((chans, wide), F32),
        ((NB, wide), F32),
        ((chans, 4 * H), BF),
    )
    w4t, w2, wod, wdt, wd3, wall, gbc, lgc, cst, wgs = pl.pallas_call(
        prep_kernel, out_shape=prep_shapes, name="prep"
    )(
        w_query,
        w_key,
        w_value,
        w_gate,
        w_output,
        gate_bias.reshape(1, width),
        out_bias.reshape(1, chans),
        w_distogram.T,
        dist_bias.reshape(1, NB),
        w_pairbias.T,
        gain_row,
    )

    lines = 8
    bias_rows = H * per_head
    target_rows = owner_rows * grid_side
    bias_mine = pl.pallas_call(
        functools.partial(bias_kernel, per_head=per_head),
        grid=(per_head // lines,),
        in_specs=[
            pl.BlockSpec((grid_side, lines, side, chans), lambda g: (0, g, 0, 0)),
            full((target_rows, wide)),
            full((1, chans)),
            full((1, chans)),
            full((H, chans)),
        ],
        out_specs=full((bias_rows + target_rows, wide)),
        out_shape=jax.ShapeDtypeStruct((bias_rows + target_rows, wide), F32),
        name="bias",
    )(
        pair_tiles.reshape(grid_side, per_head, side, chans),
        targets.reshape(target_rows, wide),
        gain_row,
        shift_row,
        w_pairbias.T,
    )

    def to_partner(value, k):
        return lax.ppermute(value, "tile", [(t, t ^ k) for t in range(tiles)]) if k else value

    gathered = [to_partner(bias_mine, k) for k in range(tiles)]

    def by_row(*shape, rows, base=0):
        return pl.BlockSpec((rows,) + shape, lambda g, *_: (g + base,) + (0,) * len(shape))

    def cost(flops, moved):
        return pl.CostEstimate(flops=flops, bytes_accessed=moved, transcendentals=0)

    cell = wide * width * wide
    square_b = ((share, wide, width), BF)
    zr, qt, kt, vt, kn, vn, gt = pl.pallas_call(
        functools.partial(project_kernel, parts=grid_side),
        grid_spec=pltpu.PrefetchScalarGridSpec(
            num_scalar_prefetch=1,
            grid=(groups,),
            in_specs=[
                pl.BlockSpec(
                    (None, None, group_rows, side, chans), lambda g, own: (g, own[0], 0, 0, 0)
                )
            ]
            + [by_row(side, chans, rows=group_rows)] * (grid_side - 1)
            + [full((1, chans)), full((1, chans)), full(w4t.shape), full(w2.shape), full(gbc.shape)],
            out_specs=[by_row(wide, width, rows=group_rows)] * 7,
            scratch_shapes=[pltpu.VMEM((group_rows * wide, chans), BF)],
        ),
        out_shape=shapes(*([square_b] * 6), ((share, width, wide), F32)),
        cost_estimate=cost(80 * share * cell, 12 * share * wide * width * 2),
        name="project",
    )(tile_j.reshape(1), *parts, gain_row, shift_row, w4t, w2, gbc)

    chunks = 2 if groups % 2 == 0 else 1
    chunk_groups = groups // chunks
    count = share // chunks
    block = group_rows
    layout = dict(grid_side=grid_side, groups=groups, group_rows=group_rows)
    saved_shapes = shapes(
        ((share, wide, H * wide), BF),
        ((share, width, wide), F32),
        ((share, NB, wide), F32),
        ((share, wide), F32),
        ((H, wide, wide), F32),
    )
    packed_shape = (share, count, 2 * NB)
    saved = []
    mirrored = []
    for c in range(chunks):
        base = c * chunk_groups
        inputs = [*gathered, kn, qt, vt, gt, zr, wod, wdt]
        first = len(inputs)
        call = pl.pallas_call(
            functools.partial(
                forward_kernel,
                tiles=tiles,
                base=base,
                count=count,
                bias_rows=bias_rows,
                owner_rows=owner_rows,
                extra=len(saved),
                **layout,
            ),
            grid=(count // block,),
            in_specs=[full(gathered[0].shape)] * tiles
            + [by_row(wide, width, rows=block, base=base)] * 5
            + [full(wod.shape), full(wdt.shape)]
            + [pl.BlockSpec(memory_space=pl.ANY)] * len(saved),
            out_specs=[
                by_row(wide, H * wide, rows=block, base=base),
                by_row(width, wide, rows=block, base=base),
                by_row(NB, wide, rows=block, base=base),
                by_row(wide, rows=block, base=base),
                full((H, wide, wide)),
            ]
            + [full(packed_shape)] * tiles,
            out_shape=saved_shapes + shapes(*([(packed_shape, BF)] * tiles)),
            scratch_shapes=[
                pltpu.VMEM((tiles,) + gathered[0].shape, F32),
                pltpu.VMEM((tiles * share * count, 2 * NB), F32),
            ],
            input_output_aliases={first + n: n for n in range(len(saved))},
            cost_estimate=cost(150 * count * cell, 14 * count * wide * width * 2),
            name="forward",
        )
        results = call(*inputs, *saved)
        saved = list(results[:4])
        mirrored.append([to_partner(results[5 + k], k) for k in range(tiles)])
    at, ot, ut, tgt = saved

    results = pl.pallas_call(
        functools.partial(backward_kernel, tiles=tiles, chunks=chunks, **layout),
        grid=(share // block,),
        in_specs=[by_row(count, 2 * NB, rows=block)] * (tiles * chunks)
        + [
            by_row(wide, rows=block),
            by_row(wide, H * wide, rows=block),
            by_row(width, wide, rows=block),
            by_row(NB, wide, rows=block),
        ]
        + [by_row(wide, width, rows=block)] * 4
        + [full(w.shape) for w in (w_output, wd3, wall, cst)],
        out_specs=[by_row(chans, wide, rows=block)] * 2 + [full((H, share, wide))] * tiles,
        out_shape=shapes(*([((share, chans, wide), F32)] * 2), *([((H, share, wide), BF)] * tiles)),
        scratch_shapes=[
            pltpu.VMEM((H, wide, wide), F32),
            pltpu.VMEM((block, width, wide), BF),
            pltpu.VMEM((4 * width, block * wide), BF),
            pltpu.VMEM((block * wide, 2 * NB), F32),
            pltpu.VMEM((tiles, H * share, wide), F32),
        ],
        cost_estimate=cost(500 * share * cell, 20 * share * wide * width * 2),
        name="backward",
    )(
        *[part for parts_c in mirrored for part in parts_c],
        tgt, at, ot, ut, gt, vn, kt, qt, w_output, wd3, wall, cst,
    )
    dpt, dzn = results[:2]
    rdb = [to_partner(results[2 + k], k) for k in range(tiles)]

    block = FIN_ROWS if share % FIN_ROWS == 0 else 1
    outgoing = pl.pallas_call(
        functools.partial(finish_kernel, tiles=tiles),
        grid_spec=pltpu.PrefetchScalarGridSpec(
            num_scalar_prefetch=1,
            grid=(share // block,),
            in_specs=[
                *([full(rdb[0].shape)] * tiles),
                pl.BlockSpec((block, chans, wide), lambda g, _: (g, 0, 0)),
                pl.BlockSpec((block, chans, wide), lambda g, _: (g, 0, 0)),
                pl.BlockSpec((block, wide, chans), lambda g, _: (g, 0, 0)),
                full(wgs.shape),
                full(lgc.shape),
            ],
            out_specs=pl.BlockSpec((states, block, piece, chans), lambda g, _: (0, g, 0, 0)),
            scratch_shapes=[pltpu.VMEM((H * share, wide), F32)],
        ),
        out_shape=jax.ShapeDtypeStruct((states, share, piece, chans), BF),
        name="finish",
    )(offsets, *rdb, dpt, dzn, zr, wgs, lgc)

    if even:
        slots = outgoing.reshape(states * tiles, group_rows, piece, chans)
    else:
        slots = lax.dynamic_update_slice(
            jnp.zeros((states, tiles, owner_rows, piece, chans), BF),
            outgoing.reshape(states, grid_side, owner_rows, piece, chans),
            (0, tile_j * grid_side, 0, 0, 0),
        ).reshape(states * tiles, owner_rows, piece, chans)
    received = lax.all_to_all(slots, ("state", "tile"), split_axis=0, concat_axis=0, tiled=True)
    if even:
        received = received.reshape(states, grid_side, owner_rows, piece, chans)
    else:
        received = lax.dynamic_index_in_dim(
            received.reshape(states, grid_side, grid_side, owner_rows, piece, chans),
            tile_i,
            2,
            keepdims=False,
        )

    block = 4 if owner_rows % 4 == 0 else 1
    out_shape = (2 * grid_side, owner_rows, 2, piece, chans)
    placed = pl.pallas_call(
        functools.partial(place_kernel, side=side),
        grid_spec=pltpu.PrefetchScalarGridSpec(
            num_scalar_prefetch=1,
            grid=(owner_rows // block,),
            in_specs=[
                pl.BlockSpec(
                    (states, grid_side, block, piece, chans), lambda g, _: (0, 0, g, 0, 0)
                )
            ],
            out_specs=pl.BlockSpec(
                (2 * grid_side, block, 2, piece, chans), lambda g, _: (0, g, 0, 0, 0)
            ),
        ),
        out_shape=jax.ShapeDtypeStruct(out_shape, F32),
        name="place",
    )(offsets, received)
    return placed.reshape(2 * grid_side, 1, owner_rows, 2, piece, chans)


def solution(mesh):
    in_specs = (
        P("state", "tile", None, None, None),
        P("state", "tile", None, None, None),
    ) + (P(),) * 13
    out_specs = P(None, "tile", None, None, "state", None)
    return jax.shard_map(
        on_device, mesh=mesh, in_specs=in_specs, out_specs=out_specs, check_vma=False
    )
```

```python
import functools
import math

import jax
import jax.numpy as jnp
from jax import lax
from jax.experimental import pallas as pl
from jax.experimental.pallas import tpu as pltpu
from jax.sharding import PartitionSpec as P

VMEM_BYTES = 16 << 20
H = 4
HD = 32
NB = 64
FWD_ROWS = 8
BWD_ROWS = 8
FWD_PACE = (8, 1, 0)
BWD_PACE = (2, 0, 3)
PROJ_PACE = (2, 0, 3)
FIN_PACE = (8, 1, 0)
PROJ_ROWS = 8
FIN_ROWS = 8
EPS = 1e-5
LOG2E = 1.0 / math.log(2.0)
BF = jnp.bfloat16
F32 = jnp.float32
HIGHEST = lax.Precision.HIGHEST


def nn(left, right, **kw):
    return lax.dot_general(left, right, (((1,), (0,)), ((), ())), preferred_element_type=F32, **kw)


def nt(left, right, **kw):
    return lax.dot_general(left, right, (((1,), (1,)), ((), ())), preferred_element_type=F32, **kw)


def split(value):
    high = value.astype(BF)
    low = (value - high.astype(F32)).astype(BF)
    return high, low


def transposed(value):
    return value.astype(F32).T.astype(value.dtype)


def column(row, lanes):
    return jnp.broadcast_to(row, (lanes, row.shape[1])).T


def eye(size):
    rows = lax.broadcasted_iota(jnp.int32, (size, size), 0)
    cols = lax.broadcasted_iota(jnp.int32, (size, size), 1)
    return jnp.where(rows == cols, 1.0, 0.0).astype(BF)


def rows_norm(pair_rows):
    mean = jnp.mean(pair_rows, axis=-1, keepdims=True)
    center = pair_rows - mean
    inverse = lax.rsqrt(jnp.mean(center * center, axis=-1, keepdims=True) + EPS)
    return center * inverse


def interleave(rows, pace):
    size, inner, outer = pace
    begin = {row: (r % size) * inner + (r // size) * outer for r, row in enumerate(rows)}
    tick = 0
    while begin:
        for row in list(begin):
            if begin[row] <= tick:
                try:
                    next(row)
                except StopIteration:
                    del begin[row]
        tick += 1


def full(shape):
    return pl.BlockSpec(shape, lambda *_: (0,) * len(shape))


def prep_kernel(wq, wk, wv, wg, wo, gb, ob, wd, db, wpb, lng, w4t, w2, wod, wdt, wd3, wall, gbc, lgc, cst, wgs):
    wide = gbc.shape[1]
    w4t[...] = jnp.concatenate([transposed(w[...]) for w in (wq, wk, wv, wg)], axis=0)
    w2[...] = jnp.concatenate([wk[...], wv[...]], axis=1)
    wall[...] = jnp.concatenate([wq[...], wk[...], wv[...], wg[...]], axis=1)
    dist_t = wd[...]
    dist = dist_t.T
    dist_hi, dist_lo = split(dist)
    wd3[...] = jnp.concatenate([dist_hi, dist_hi, dist_lo], axis=1)
    wdt[...] = jnp.concatenate(split(dist_t), axis=0)
    both = nn(wo[...].astype(F32), dist, precision=HIGHEST)
    wod[...] = jnp.concatenate(split(both.T), axis=0)
    gbc[...] = column(gb[...], wide)
    lgc[...] = column(lng[...], wide)
    shift = 2.0 * jnp.sum(dist_t * ob[...], axis=1, keepdims=True)
    cst[...] = column(db[...], wide) + shift
    proj = jnp.concatenate([wpb[...], jnp.zeros((wide - H, wpb.shape[1]), F32)], axis=0).T[:, :H]
    proj_hi, proj_lo = split(proj)
    wgs[...] = jnp.concatenate([proj_hi, proj_hi, proj_lo, jnp.zeros_like(proj_lo)], axis=1)


def bias_kernel(tile, targets, lng, lnb, wpb, out, *, per_head):
    step = pl.program_id(0)
    fold, lines, side, chans = tile.shape
    pieces = [tile[f, q] for q in range(lines) for f in range(fold)]
    pair = jnp.concatenate(pieces, axis=0)
    proj = wpb[...] * lng[...]
    high, rest = split(proj)
    mid = rest
    last = (proj - high.astype(F32) - mid.astype(F32)).astype(BF)
    left = jnp.concatenate(
        [high.astype(F32), mid.astype(F32), last.astype(F32), jnp.ones((H, chans), F32)], axis=0
    ).astype(BF)
    left = jnp.concatenate([eye(chans), left], axis=0)
    total = jnp.sum(proj, axis=1, keepdims=True)
    const = jnp.sum(wpb[...] * lnb[...], axis=1, keepdims=True)
    size = fold * side
    rows_out = []
    for q in range(lines):
        up = nt(left, pair[q * size : (q + 1) * size])
        extra = up[chans:]
        mean = extra[3 * H : 3 * H + 1] * (1.0 / chans)
        center = up[:chans] - mean
        inverse = lax.rsqrt(jnp.mean(center * center, axis=0, keepdims=True) + EPS)
        dotted = extra[:H] + extra[H : 2 * H] + extra[2 * H : 3 * H]
        rows_out.append(inverse * (dotted - mean * total) + const)
    bias = jnp.concatenate(rows_out, axis=1)
    width = fold * side
    for q in range(lines):
        for h in range(H):
            out[pl.ds(h * per_head + step * lines + q, 1), :] = bias[
                h : h + 1, q * width : (q + 1) * width
            ]

    @pl.when(step == 0)
    def _():
        count = targets.shape[0]
        out[pl.ds(H * per_head, count), :] = targets[...].astype(F32)


def project_kernel(own_ref, *refs, parts):
    own = own_ref[0]
    part_refs = refs[:parts]
    lng, lnb, w4t, w2, gbc, zr, qt, kt, vt, kn, vn, gt, flat_s = refs[parts:]
    rows, side, _ = part_refs[0].shape
    wide = zr.shape[1]
    width = H * HD
    for row in range(rows):
        for k in range(parts):
            block = lax.rem(own + parts - k, parts)
            zr[row, pl.ds(pl.multiple_of(block * side, side), side), :] = part_refs[k][row]

    def one_row(row):
        pair_row = zr[row].astype(F32)
        center = pair_row - jnp.mean(pair_row, axis=-1, keepdims=True)
        yield
        inverse = lax.rsqrt(jnp.mean(center * center, axis=-1, keepdims=True) + EPS)
        yield
        flat_s[row * wide : (row + 1) * wide, :] = (
            center * inverse * lng[...] + lnb[...]
        ).astype(BF)
        yield

    def one_pair(first):
        both = one_row(first), one_row(first + 1)
        for _ in range(3):
            for row in both:
                next(row)
            yield
        flat = flat_s[first * wide : (first + 2) * wide, :]
        for k, out in enumerate((qt, kt, vt)):
            up = nt(w4t[k * width : (k + 1) * width], flat)
            for n in range(2):
                out[first + n] = up[:, n * wide : (n + 1) * wide].astype(BF)
            yield
        up = nt(w4t[3 * width :], flat)
        for n in range(2):
            gt[first + n] = jax.nn.sigmoid(up[:, n * wide : (n + 1) * wide] + gbc[...])
            yield
        down = nn(flat, w2[...])
        for n in range(2):
            kn[first + n] = down[n * wide : (n + 1) * wide, :width].astype(BF)
            vn[first + n] = down[n * wide : (n + 1) * wide, width:].astype(BF)
        yield

    interleave([one_pair(row) for row in range(0, rows, 2)], PROJ_PACE)


def head_block(part, h):
    lanes = part.shape[1]
    pieces = []
    if h:
        pieces.append(jnp.zeros((h * HD, lanes), part.dtype))
    pieces.append(part)
    if h < H - 1:
        pieces.append(jnp.zeros(((H - 1 - h) * HD, lanes), part.dtype))
    return jnp.concatenate(pieces, axis=0)


def head_blocks(packed):
    return jnp.concatenate(
        [head_block(packed[h * HD : (h + 1) * HD], h) for h in range(H)], axis=1
    )


def forward_kernel(
    *refs, tiles, base, count, bias_rows, owner_rows, extra, grid_side, groups, group_rows
):
    gath = refs[:tiles]
    kn, qt, vt, gt, zr, wod, wdt = refs[tiles : tiles + 7]
    at, ot, ut, tgt, bias_t = refs[tiles + 7 + extra : tiles + 12 + extra]
    sends = refs[tiles + 12 + extra : 2 * tiles + 12 + extra]
    order, stage = refs[2 * tiles + 12 + extra :]
    step = pl.program_id(0)
    mine = lax.axis_index("tile")
    tile_i = mine // grid_side
    tile_j = lax.rem(mine, grid_side)
    rows = kn.shape[0]
    wide = kn.shape[1]
    side = wide // grid_side
    per_head = side * side // wide
    share = groups * group_rows
    span = side // groups

    @pl.when(step == 0)
    def _():
        for k in range(tiles):
            order[mine ^ k] = gath[k][...]
        lane = lax.broadcasted_iota(jnp.int32, (per_head, wide), 1) // side
        for h in range(H):
            pieces = []
            for i in range(grid_side):
                for f in range(grid_side):
                    total = None
                    for j in range(grid_side):
                        part = order[i * grid_side + j, h * per_head : (h + 1) * per_head, :]
                        turn = ((j - f) * side) % wide
                        if turn:
                            part = pltpu.roll(part, turn, 1)
                        total = part if total is None else jnp.where(lane == j, part, total)
                    pieces.append(total)
            bias_t[h] = jnp.concatenate(pieces, axis=0).T * LOG2E

    for row in range(rows):
        within = (base + step) * span + tile_j * group_rows + row
        tgt[row : row + 1, :] = order[
            within // owner_rows,
            pl.ds(bias_rows + lax.rem(within, owner_rows) * grid_side + tile_i, 1),
            :,
        ]

    scale = LOG2E / math.sqrt(HD)

    def one_row(row):
        blocks = head_blocks(qt[row])
        outs = []
        for pair in range(0, H, 2):
            scores = nn(kn[row], blocks[:, pair * wide : (pair + 2) * wide])
            yield
            for h in range(pair, pair + 2):
                part = scores[:, (h - pair) * wide : (h - pair + 1) * wide] * scale + bias_t[h]
                peak = jnp.max(part, axis=0, keepdims=True)
                yield
                part = jnp.exp2(part - peak)
                total = jnp.sum(part, axis=0, keepdims=True)
                yield
                part_b = (part * (1.0 / total)).astype(BF)
                at[row, :, h * wide : (h + 1) * wide] = part_b
                yield
                outs.append(nn(vt[row, h * HD : (h + 1) * HD, :], part_b))
                ot[row, h * HD : (h + 1) * HD, :] = outs[-1]
                yield
        gated = (gt[row] * ot[row]).astype(BF)
        yield
        both = nn(wod[...], gated) + nt(wdt[...], zr[row])
        yield
        logit = both[:NB] + both[NB:]
        ut[row] = logit
        high = logit.astype(BF).astype(F32)
        yield
        packed = jnp.concatenate([high, logit - high], axis=0).T
        here = step * rows + row
        yield
        for i in range(grid_side):
            for p in range(groups):
                for j in range(grid_side):
                    source = ((i * groups + p) * grid_side + j) * group_rows
                    target = ((i * grid_side + j) * share + p * group_rows) * count
                    stage[pl.ds(target + here, group_rows, stride=count), :] = packed[
                        source : source + group_rows
                    ]
                yield

    interleave([one_row(row) for row in range(rows)], FWD_PACE)

    @pl.when(step == pl.num_programs(0) - 1)
    def _():
        for k in range(tiles):
            start = (mine ^ k) * (share * count)
            for r in range(share):
                sends[k][r] = stage[
                    pl.ds(pl.multiple_of(start + r * count, 8), count), :
                ].astype(BF)


def backward_kernel(*refs, tiles, chunks, grid_side, groups, group_rows):
    rcv = refs[: tiles * chunks]
    tgt, at, ot, ut, gt, vn, kt, qt, wo, wd3, wall, cst, dpt, dzn = refs[
        tiles * chunks : tiles * chunks + 14
    ]
    sends = refs[tiles * chunks + 14 : tiles * chunks + 14 + tiles]
    acc, grad_s, back_s, mirror_s, order = refs[tiles * chunks + 14 + tiles :]
    width = H * HD
    step = pl.program_id(0)
    mine = lax.axis_index("tile")
    rows = vn.shape[0]
    wide = vn.shape[1]
    chunk_groups = groups // chunks
    share = groups * group_rows
    inv_root = 1.0 / math.sqrt(HD)
    adder = jnp.concatenate([eye(NB)] * 2, axis=1)
    bins = lax.broadcasted_iota(jnp.int32, (NB, 2 * wide), 0).astype(F32)

    @pl.when(step == 0)
    def _():
        acc[...] = jnp.zeros_like(acc)

    shift = jnp.concatenate([cst[...]] * 2, axis=1)

    def one_pair(first):
        pair = (first, first + 1)
        for row in pair:
            for k in range(tiles):
                source_i = (mine ^ k) // grid_side
                source_j = lax.rem(mine ^ k, grid_side)
                for p in range(groups):
                    start = ((source_i * groups + p) * grid_side + source_j) * group_rows
                    local = (p % chunk_groups) * group_rows
                    mirror_s[pl.ds(pl.multiple_of(row * wide + start, group_rows), group_rows), :] = rcv[
                        (p // chunk_groups) * tiles + k
                    ][row, local : local + group_rows].astype(F32)
        yield
        other = nt(adder, mirror_s[first * wide : (first + 2) * wide, :].astype(BF))
        yield
        logits = jnp.concatenate([ut[row] for row in pair], axis=1) + other + shift
        peak = jnp.max(logits, axis=0, keepdims=True)
        yield
        probs = jnp.exp(logits - peak)
        total = jnp.sum(probs, axis=0, keepdims=True)
        yield
        target = jnp.concatenate([tgt[row : row + 1, :] for row in pair], axis=1)
        resid = 2.0 * (probs * (1.0 / total) - jnp.where(bins == target, 1.0, 0.0))
        res_hi, res_lo = split(resid)
        yield
        pair_grad = nn(wd3[...], jnp.concatenate([res_hi, res_lo, res_hi], axis=0))
        for n, row in enumerate(pair):
            dpt[row] = pair_grad[:, n * wide : (n + 1) * wide]
        yield
        out_grad = nn(wo[...], pair_grad.astype(BF))
        yield
        for n, row in enumerate(pair):
            gate = gt[row]
            gated = out_grad[:, n * wide : (n + 1) * wide] * gate
            grad_s[row] = gated.astype(BF)
            back_s[3 * width :, row * wide : (row + 1) * wide] = (
                gated * ot[row] * (1.0 - gate)
            ).astype(BF)
            yield

        def heads(row):
            lanes = slice(row * wide, (row + 1) * wide)
            for h in range(H):
                part = slice(h * HD, (h + 1) * HD)
                back_s[2 * width + h * HD : 2 * width + (h + 1) * HD, lanes] = nt(
                    grad_s[row, part, :], at[row, :, h * wide : (h + 1) * wide]
                ).astype(BF)
                yield
                weight_grad = nn(vn[row], head_block(grad_s[row, part, :], h))
                yield
                prob = at[row, :, h * wide : (h + 1) * wide].astype(F32)
                prod = prob * weight_grad
                total = jnp.sum(prod, axis=0, keepdims=True)
                yield
                prod = prod - prob * total
                prod_b = prod.astype(BF)
                acc[h] += prod
                yield
                back_s[h * HD : (h + 1) * HD, lanes] = (nn(kt[row, part, :], prod_b) * inv_root).astype(BF)
                back_s[width + h * HD : width + (h + 1) * HD, lanes] = (
                    nt(qt[row, part, :], prod_b) * inv_root
                ).astype(BF)
                yield

        both = [heads(row) for row in pair]
        while both:
            for row in list(both):
                try:
                    next(row)
                except StopIteration:
                    both.remove(row)
            yield
        normed_grad = nn(wall[...], back_s[:, first * wide : (first + 2) * wide])
        for n, row in enumerate(pair):
            dzn[row] = normed_grad[:, n * wide : (n + 1) * wide]
        yield

    interleave([one_pair(row) for row in range(0, rows, 2)], BWD_PACE)

    @pl.when(step == pl.num_programs(0) - 1)
    def _():
        for h in range(H):
            grad = acc[h].T
            for i in range(grid_side):
                for j in range(grid_side):
                    pieces = []
                    for p in range(groups):
                        source = ((i * groups + p) * grid_side + j) * group_rows
                        pieces.append(grad[source : source + group_rows])
                    order[i * grid_side + j, h * share : (h + 1) * share, :] = jnp.concatenate(
                        pieces, axis=0
                    )
        for k in range(tiles):
            sends[k][...] = order[mine ^ k].reshape(H, share, wide).astype(BF)


def finish_kernel(offsets, *refs, tiles):
    rdb = refs[:tiles]
    dpt, dzn, zr, wgs, lgc, out, sums = refs[tiles:]
    step = pl.program_id(0)
    rows, chans, wide = dzn.shape
    states, _, piece, _ = out.shape
    total_rows = rdb[0].shape[1]
    turn = offsets[lax.axis_index("state")] // piece

    @pl.when(step == 0)
    def _():
        for h in range(H):
            total = rdb[0][h].astype(F32)
            for part in rdb[1:]:
                total = total + part[h].astype(F32)
            sums[pl.ds(h * total_rows, total_rows), :] = total

    ident = eye(chans)

    def one_row(row):
        local = step * rows + row
        pair_t = nt(ident, zr[row])
        yield
        center = pair_t - jnp.mean(pair_t, axis=0, keepdims=True)
        yield
        inverse = lax.rsqrt(jnp.mean(center * center, axis=0, keepdims=True) + EPS)
        normed = center * inverse
        yield
        parts = [sums[pl.ds(h * total_rows + local, 1), :] for h in range(H)]
        high, low = split(jnp.concatenate(parts, axis=0))
        spread = jnp.concatenate([high.astype(F32), low.astype(F32), high.astype(F32), jnp.zeros((H, wide), F32)], axis=0)
        yield
        scaled = (dzn[row] + nn(wgs[...], spread.astype(BF))) * lgc[...]
        yield
        mean_a = jnp.mean(scaled, axis=0, keepdims=True)
        mean_b = jnp.mean(scaled * normed, axis=0, keepdims=True)
        yield
        total = dpt[row] + inverse * (scaled - mean_a - normed * mean_b)
        yield
        total = total.T.astype(BF)
        for c in range(wide // piece):
            out[lax.rem(turn + c, states), row] = total[c * piece : (c + 1) * piece]
        yield

    interleave([one_row(row) for row in range(rows)], FIN_PACE)


def place_kernel(offsets, rcv, out, *, side):
    states, grid_side, rows, piece, chans = rcv.shape
    start = lax.axis_index("state") * piece
    out[...] = jnp.zeros_like(out)
    for s in range(states):
        offset = offsets[s]
        half = (start < offset).astype(jnp.int32)
        base = offset // side
        for i in range(grid_side):
            out[base + i, :, half] += rcv[s, i].astype(F32)


def on_device(
    pair_tiles,
    targets,
    offsets,
    ln_gain,
    ln_bias,
    w_query,
    w_key,
    w_value,
    w_pairbias,
    w_gate,
    gate_bias,
    w_output,
    out_bias,
    w_distogram,
    dist_bias,
):
    tiles = lax.axis_size("tile")
    states = lax.axis_size("state")
    side, chans = pair_tiles.shape[3], pair_tiles.shape[4]
    wide = targets.shape[4]
    grid_side = wide // side
    owner_rows = side // tiles
    width = H * HD
    here = lax.axis_index("tile")
    tile_i = here // grid_side
    tile_j = lax.rem(here, grid_side)
    even = owner_rows % grid_side == 0
    groups = tiles if even else 1
    group_rows = side // groups // grid_side
    share = groups * group_rows
    per_head = side * side // wide
    piece = wide // states

    def shapes(*pairs):
        return [jax.ShapeDtypeStruct(s, t) for s, t in pairs]

    tile = pair_tiles.reshape(groups, grid_side, group_rows, side, chans)

    def rows_of(j):
        return lax.dynamic_index_in_dim(tile, j, 1, keepdims=False).reshape(share, side, chans)

    parts = [tile]
    for k in range(1, grid_side):
        perm = [
            (i * grid_side + j, i * grid_side + (j + k) % grid_side)
            for i in range(grid_side)
            for j in range(grid_side)
        ]
        parts.append(lax.ppermute(rows_of(lax.rem(tile_j + k, grid_side)), "tile", perm))

    gain_row = ln_gain.reshape(1, chans)
    shift_row = ln_bias.reshape(1, chans)
    prep_shapes = shapes(
        ((4 * width, chans), BF),
        ((chans, 2 * width), BF),
        ((2 * NB, width), BF),
        ((2 * NB, chans), BF),
        ((chans, 3 * NB), BF),
        ((chans, 4 * width), BF),
        ((width, wide), F32),
        ((chans, wide), F32),
        ((NB, wide), F32),
        ((chans, 4 * H), BF),
    )
    w4t, w2, wod, wdt, wd3, wall, gbc, lgc, cst, wgs = pl.pallas_call(
        prep_kernel, out_shape=prep_shapes, name="prep",
        compiler_params=pltpu.CompilerParams(vmem_limit_bytes=VMEM_BYTES)
    )(
        w_query,
        w_key,
        w_value,
        w_gate,
        w_output,
        gate_bias.reshape(1, width),
        out_bias.reshape(1, chans),
        w_distogram.T,
        dist_bias.reshape(1, NB),
        w_pairbias.T,
        gain_row,
    )

    lines = 8
    bias_rows = H * per_head
    target_rows = owner_rows * grid_side
    bias_mine = pl.pallas_call(
        functools.partial(bias_kernel, per_head=per_head),
        grid=(per_head // lines,),
        in_specs=[
            pl.BlockSpec((grid_side, lines, side, chans), lambda g: (0, g, 0, 0)),
            full((target_rows, wide)),
            full((1, chans)),
            full((1, chans)),
            full((H, chans)),
        ],
        out_specs=full((bias_rows + target_rows, wide)),
        out_shape=jax.ShapeDtypeStruct((bias_rows + target_rows, wide), F32),
        name="bias",
        compiler_params=pltpu.CompilerParams(vmem_limit_bytes=VMEM_BYTES),
    )(
        pair_tiles.reshape(grid_side, per_head, side, chans),
        targets.reshape(target_rows, wide),
        gain_row,
        shift_row,
        w_pairbias.T,
    )

    def to_partner(value, k):
        return lax.ppermute(value, "tile", [(t, t ^ k) for t in range(tiles)]) if k else value

    gathered = [to_partner(bias_mine, k) for k in range(tiles)]

    def by_row(*shape, rows, base=0):
        return pl.BlockSpec((rows,) + shape, lambda g, *_: (g + base,) + (0,) * len(shape))

    def cost(flops, moved):
        return pl.CostEstimate(flops=flops, bytes_accessed=moved, transcendentals=0)

    cell = wide * width * wide
    square_b = ((share, wide, width), BF)
    zr, qt, kt, vt, kn, vn, gt = pl.pallas_call(
        functools.partial(project_kernel, parts=grid_side),
        grid_spec=pltpu.PrefetchScalarGridSpec(
            num_scalar_prefetch=1,
            grid=(groups,),
            in_specs=[
                pl.BlockSpec(
                    (None, None, group_rows, side, chans), lambda g, own: (g, own[0], 0, 0, 0)
                )
            ]
            + [by_row(side, chans, rows=group_rows)] * (grid_side - 1)
            + [full((1, chans)), full((1, chans)), full(w4t.shape), full(w2.shape), full(gbc.shape)],
            out_specs=[by_row(wide, width, rows=group_rows)] * 7,
            scratch_shapes=[pltpu.VMEM((group_rows * wide, chans), BF)],
        ),
        out_shape=shapes(*([square_b] * 6), ((share, width, wide), F32)),
        cost_estimate=cost(80 * share * cell, 12 * share * wide * width * 2),
        name="project",
        compiler_params=pltpu.CompilerParams(vmem_limit_bytes=VMEM_BYTES),
    )(tile_j.reshape(1), *parts, gain_row, shift_row, w4t, w2, gbc)

    chunks = 2 if groups % 2 == 0 else 1
    chunk_groups = groups // chunks
    count = share // chunks
    block = group_rows
    layout = dict(grid_side=grid_side, groups=groups, group_rows=group_rows)
    saved_shapes = shapes(
        ((share, wide, H * wide), BF),
        ((share, width, wide), F32),
        ((share, NB, wide), F32),
        ((share, wide), F32),
        ((H, wide, wide), F32),
    )
    packed_shape = (share, count, 2 * NB)
    saved = []
    mirrored = []
    for c in range(chunks):
        base = c * chunk_groups
        inputs = [*gathered, kn, qt, vt, gt, zr, wod, wdt]
        first = len(inputs)
        call = pl.pallas_call(
            functools.partial(
                forward_kernel,
                tiles=tiles,
                base=base,
                count=count,
                bias_rows=bias_rows,
                owner_rows=owner_rows,
                extra=len(saved),
                **layout,
            ),
            grid=(count // block,),
            in_specs=[full(gathered[0].shape)] * tiles
            + [by_row(wide, width, rows=block, base=base)] * 5
            + [full(wod.shape), full(wdt.shape)]
            + [pl.BlockSpec(memory_space=pl.ANY)] * len(saved),
            out_specs=[
                by_row(wide, H * wide, rows=block, base=base),
                by_row(width, wide, rows=block, base=base),
                by_row(NB, wide, rows=block, base=base),
                by_row(wide, rows=block, base=base),
                full((H, wide, wide)),
            ]
            + [full(packed_shape)] * tiles,
            out_shape=saved_shapes + shapes(*([(packed_shape, BF)] * tiles)),
            scratch_shapes=[
                pltpu.VMEM((tiles,) + gathered[0].shape, F32),
                pltpu.VMEM((tiles * share * count, 2 * NB), F32),
            ],
            input_output_aliases={first + n: n for n in range(len(saved))},
            cost_estimate=cost(150 * count * cell, 14 * count * wide * width * 2),
            name="forward",
        compiler_params=pltpu.CompilerParams(vmem_limit_bytes=VMEM_BYTES),
        )
        results = call(*inputs, *saved)
        saved = list(results[:4])
        mirrored.append([to_partner(results[5 + k], k) for k in range(tiles)])
    at, ot, ut, tgt = saved

    results = pl.pallas_call(
        functools.partial(backward_kernel, tiles=tiles, chunks=chunks, **layout),
        grid=(share // block,),
        in_specs=[by_row(count, 2 * NB, rows=block)] * (tiles * chunks)
        + [
            by_row(wide, rows=block),
            by_row(wide, H * wide, rows=block),
            by_row(width, wide, rows=block),
            by_row(NB, wide, rows=block),
        ]
        + [by_row(wide, width, rows=block)] * 4
        + [full(w.shape) for w in (w_output, wd3, wall, cst)],
        out_specs=[by_row(chans, wide, rows=block)] * 2 + [full((H, share, wide))] * tiles,
        out_shape=shapes(*([((share, chans, wide), F32)] * 2), *([((H, share, wide), BF)] * tiles)),
        scratch_shapes=[
            pltpu.VMEM((H, wide, wide), F32),
            pltpu.VMEM((block, width, wide), BF),
            pltpu.VMEM((4 * width, block * wide), BF),
            pltpu.VMEM((block * wide, 2 * NB), F32),
            pltpu.VMEM((tiles, H * share, wide), F32),
        ],
        cost_estimate=cost(500 * share * cell, 20 * share * wide * width * 2),
        name="backward",
        compiler_params=pltpu.CompilerParams(vmem_limit_bytes=VMEM_BYTES),
    )(
        *[part for parts_c in mirrored for part in parts_c],
        tgt, at, ot, ut, gt, vn, kt, qt, w_output, wd3, wall, cst,
    )
    dpt, dzn = results[:2]
    rdb = [to_partner(results[2 + k], k) for k in range(tiles)]

    block = FIN_ROWS if share % FIN_ROWS == 0 else 1
    outgoing = pl.pallas_call(
        functools.partial(finish_kernel, tiles=tiles),
        grid_spec=pltpu.PrefetchScalarGridSpec(
            num_scalar_prefetch=1,
            grid=(share // block,),
            in_specs=[
                *([full(rdb[0].shape)] * tiles),
                pl.BlockSpec((block, chans, wide), lambda g, _: (g, 0, 0)),
                pl.BlockSpec((block, chans, wide), lambda g, _: (g, 0, 0)),
                pl.BlockSpec((block, wide, chans), lambda g, _: (g, 0, 0)),
                full(wgs.shape),
                full(lgc.shape),
            ],
            out_specs=pl.BlockSpec((states, block, piece, chans), lambda g, _: (0, g, 0, 0)),
            scratch_shapes=[pltpu.VMEM((H * share, wide), F32)],
        ),
        out_shape=jax.ShapeDtypeStruct((states, share, piece, chans), BF),
        name="finish",
        compiler_params=pltpu.CompilerParams(vmem_limit_bytes=VMEM_BYTES),
    )(offsets, *rdb, dpt, dzn, zr, wgs, lgc)

    if even:
        slots = outgoing.reshape(states * tiles, group_rows, piece, chans)
    else:
        slots = lax.dynamic_update_slice(
            jnp.zeros((states, tiles, owner_rows, piece, chans), BF),
            outgoing.reshape(states, grid_side, owner_rows, piece, chans),
            (0, tile_j * grid_side, 0, 0, 0),
        ).reshape(states * tiles, owner_rows, piece, chans)
    received = lax.all_to_all(slots, ("state", "tile"), split_axis=0, concat_axis=0, tiled=True)
    if even:
        received = received.reshape(states, grid_side, owner_rows, piece, chans)
    else:
        received = lax.dynamic_index_in_dim(
            received.reshape(states, grid_side, grid_side, owner_rows, piece, chans),
            tile_i,
            2,
            keepdims=False,
        )

    block = 4 if owner_rows % 4 == 0 else 1
    out_shape = (2 * grid_side, owner_rows, 2, piece, chans)
    placed = pl.pallas_call(
        functools.partial(place_kernel, side=side),
        grid_spec=pltpu.PrefetchScalarGridSpec(
            num_scalar_prefetch=1,
            grid=(owner_rows // block,),
            in_specs=[
                pl.BlockSpec(
                    (states, grid_side, block, piece, chans), lambda g, _: (0, 0, g, 0, 0)
                )
            ],
            out_specs=pl.BlockSpec(
                (2 * grid_side, block, 2, piece, chans), lambda g, _: (0, g, 0, 0, 0)
            ),
        ),
        out_shape=jax.ShapeDtypeStruct(out_shape, F32),
        name="place",
        compiler_params=pltpu.CompilerParams(vmem_limit_bytes=VMEM_BYTES),
    )(offsets, received)
    return placed.reshape(2 * grid_side, 1, owner_rows, 2, piece, chans)


def solution(mesh):
    in_specs = (
        P("state", "tile", None, None, None),
        P("state", "tile", None, None, None),
    ) + (P(),) * 13
    out_specs = P(None, "tile", None, None, "state", None)
    return jax.shard_map(
        on_device, mesh=mesh, in_specs=in_specs, out_specs=out_specs, check_vma=False
    )
```

```python
import functools
import math

import jax
import jax.numpy as jnp
from jax import lax
from jax.experimental import pallas as pl
from jax.experimental.pallas import tpu as pltpu
from jax.sharding import PartitionSpec as P

VMEM_BYTES = 16 << 20
H = 4
HD = 32
NB = 64
FWD_ROWS = 8
BWD_ROWS = 8
FWD_PACE = (8, 1, 0)
BWD_PACE = (2, 0, 3)
PROJ_PACE = (2, 0, 3)
FIN_PACE = (8, 1, 0)
PROJ_ROWS = 8
FIN_ROWS = 8
EPS = 1e-5
LOG2E = 1.0 / math.log(2.0)
BF = jnp.bfloat16
F32 = jnp.float32
HIGHEST = lax.Precision.HIGHEST


def nn(left, right, **kw):
    return lax.dot_general(left, right, (((1,), (0,)), ((), ())), preferred_element_type=F32, **kw)


def nt(left, right, **kw):
    return lax.dot_general(left, right, (((1,), (1,)), ((), ())), preferred_element_type=F32, **kw)


def split(value):
    high = value.astype(BF)
    low = (value - high.astype(F32)).astype(BF)
    return high, low


def transposed(value):
    return value.astype(F32).T.astype(value.dtype)


def column(row, lanes):
    return jnp.broadcast_to(row, (lanes, row.shape[1])).T


def eye(size):
    rows = lax.broadcasted_iota(jnp.int32, (size, size), 0)
    cols = lax.broadcasted_iota(jnp.int32, (size, size), 1)
    return jnp.where(rows == cols, 1.0, 0.0).astype(BF)


def rows_norm(pair_rows):
    mean = jnp.mean(pair_rows, axis=-1, keepdims=True)
    center = pair_rows - mean
    inverse = lax.rsqrt(jnp.mean(center * center, axis=-1, keepdims=True) + EPS)
    return center * inverse


def interleave(rows, pace):
    size, inner, outer = pace
    begin = {row: (r % size) * inner + (r // size) * outer for r, row in enumerate(rows)}
    tick = 0
    while begin:
        for row in list(begin):
            if begin[row] <= tick:
                try:
                    next(row)
                except StopIteration:
                    del begin[row]
        tick += 1


def full(shape):
    return pl.BlockSpec(shape, lambda *_: (0,) * len(shape))


def prep_kernel(wq, wk, wv, wg, wo, gb, ob, wd, db, wpb, lng, w4t, w2, wod, wdt, wd3, wall, gbc, lgc, cst, wgs):
    wide = gbc.shape[1]
    w4t[...] = jnp.concatenate([transposed(w[...]) for w in (wq, wk, wv, wg)], axis=0)
    w2[...] = jnp.concatenate([wk[...], wv[...]], axis=1)
    wall[...] = jnp.concatenate([wq[...], wk[...], wv[...], wg[...]], axis=1)
    dist_t = wd[...]
    dist = dist_t.T
    dist_hi, dist_lo = split(dist)
    wd3[...] = jnp.concatenate([dist_hi, dist_hi, dist_lo], axis=1)
    wdt[...] = jnp.concatenate(split(dist_t), axis=0)
    both = nn(wo[...].astype(F32), dist, precision=HIGHEST)
    wod[...] = jnp.concatenate(split(both.T), axis=0)
    gbc[...] = column(gb[...], wide)
    lgc[...] = column(lng[...], wide)
    shift = 2.0 * jnp.sum(dist_t * ob[...], axis=1, keepdims=True)
    cst[...] = column(db[...], wide) + shift
    proj = jnp.concatenate([wpb[...], jnp.zeros((wide - H, wpb.shape[1]), F32)], axis=0).T[:, :H]
    proj_hi, proj_lo = split(proj)
    wgs[...] = jnp.concatenate([proj_hi, proj_hi, proj_lo, jnp.zeros_like(proj_lo)], axis=1)


def bias_kernel(tile, targets, lng, lnb, wpb, out, *, per_head):
    step = pl.program_id(0)
    fold, lines, side, chans = tile.shape
    pieces = [tile[f, q] for q in range(lines) for f in range(fold)]
    pair = jnp.concatenate(pieces, axis=0)
    proj = wpb[...] * lng[...]
    high, rest = split(proj)
    mid = rest
    last = (proj - high.astype(F32) - mid.astype(F32)).astype(BF)
    left = jnp.concatenate(
        [high.astype(F32), mid.astype(F32), last.astype(F32), jnp.ones((H, chans), F32)], axis=0
    ).astype(BF)
    left = jnp.concatenate([eye(chans), left], axis=0)
    total = jnp.sum(proj, axis=1, keepdims=True)
    const = jnp.sum(wpb[...] * lnb[...], axis=1, keepdims=True)
    size = fold * side
    rows_out = []
    for q in range(lines):
        up = nt(left, pair[q * size : (q + 1) * size])
        extra = up[chans:]
        mean = extra[3 * H : 3 * H + 1] * (1.0 / chans)
        center = up[:chans] - mean
        inverse = lax.rsqrt(jnp.mean(center * center, axis=0, keepdims=True) + EPS)
        dotted = extra[:H] + extra[H : 2 * H] + extra[2 * H : 3 * H]
        rows_out.append(inverse * (dotted - mean * total) + const)
    bias = jnp.concatenate(rows_out, axis=1)
    width = fold * side
    for q in range(lines):
        for h in range(H):
            out[pl.ds(h * per_head + step * lines + q, 1), :] = bias[
                h : h + 1, q * width : (q + 1) * width
            ]

    @pl.when(step == 0)
    def _():
        count = targets.shape[0]
        out[pl.ds(H * per_head, count), :] = targets[...].astype(F32)


def project_kernel(own_ref, *refs, parts):
    own = own_ref[0]
    part_refs = refs[:parts]
    lng, lnb, w4t, w2, gbc, zr, qt, kt, vt, kn, vn, gt, flat_s = refs[parts:]
    rows, side, _ = part_refs[0].shape
    wide = zr.shape[1]
    width = H * HD
    for row in range(rows):
        for k in range(parts):
            block = lax.rem(own + parts - k, parts)
            zr[row, pl.ds(pl.multiple_of(block * side, side), side), :] = part_refs[k][row]

    def one_row(row):
        pair_row = zr[row].astype(F32)
        center = pair_row - jnp.mean(pair_row, axis=-1, keepdims=True)
        yield
        inverse = lax.rsqrt(jnp.mean(center * center, axis=-1, keepdims=True) + EPS)
        yield
        flat_s[row * wide : (row + 1) * wide, :] = (
            center * inverse * lng[...] + lnb[...]
        ).astype(BF)
        yield

    def one_pair(first):
        both = one_row(first), one_row(first + 1)
        for _ in range(3):
            for row in both:
                next(row)
            yield
        flat = flat_s[first * wide : (first + 2) * wide, :]
        for k, out in enumerate((qt, kt, vt)):
            up = nt(w4t[k * width : (k + 1) * width], flat)
            for n in range(2):
                out[first + n] = up[:, n * wide : (n + 1) * wide].astype(BF)
            yield
        up = nt(w4t[3 * width :], flat)
        for n in range(2):
            gt[first + n] = jax.nn.sigmoid(up[:, n * wide : (n + 1) * wide] + gbc[...])
            yield
        down = nn(flat, w2[...])
        for n in range(2):
            kn[first + n] = down[n * wide : (n + 1) * wide, :width].astype(BF)
            vn[first + n] = down[n * wide : (n + 1) * wide, width:].astype(BF)
        yield

    interleave([one_pair(row) for row in range(0, rows, 2)], PROJ_PACE)


def head_block(part, h):
    lanes = part.shape[1]
    pieces = []
    if h:
        pieces.append(jnp.zeros((h * HD, lanes), part.dtype))
    pieces.append(part)
    if h < H - 1:
        pieces.append(jnp.zeros(((H - 1 - h) * HD, lanes), part.dtype))
    return jnp.concatenate(pieces, axis=0)


def head_blocks(packed):
    return jnp.concatenate(
        [head_block(packed[h * HD : (h + 1) * HD], h) for h in range(H)], axis=1
    )


def forward_kernel(
    *refs, tiles, base, count, bias_rows, owner_rows, extra, grid_side, groups, group_rows
):
    gath = refs[:tiles]
    kn, qt, vt, gt, zr, wod, wdt = refs[tiles : tiles + 7]
    at, ot, ut, tgt, bias_t = refs[tiles + 7 + extra : tiles + 12 + extra]
    sends = refs[tiles + 12 + extra : 2 * tiles + 12 + extra]
    order, stage = refs[2 * tiles + 12 + extra :]
    step = pl.program_id(0)
    mine = lax.axis_index("tile")
    tile_i = mine // grid_side
    tile_j = lax.rem(mine, grid_side)
    rows = kn.shape[0]
    wide = kn.shape[1]
    side = wide // grid_side
    per_head = side * side // wide
    share = groups * group_rows
    span = side // groups

    @pl.when(step == 0)
    def _():
        for k in range(tiles):
            order[mine ^ k] = gath[k][...]
        lane = lax.broadcasted_iota(jnp.int32, (per_head, wide), 1) // side
        for h in range(H):
            pieces = []
            for i in range(grid_side):
                for f in range(grid_side):
                    total = None
                    for j in range(grid_side):
                        part = order[i * grid_side + j, h * per_head : (h + 1) * per_head, :]
                        turn = ((j - f) * side) % wide
                        if turn:
                            part = pltpu.roll(part, turn, 1)
                        total = part if total is None else jnp.where(lane == j, part, total)
                    pieces.append(total)
            bias_t[h] = jnp.concatenate(pieces, axis=0).T * LOG2E

    for row in range(rows):
        within = (base + step) * span + tile_j * group_rows + row
        tgt[row : row + 1, :] = order[
            within // owner_rows,
            pl.ds(bias_rows + lax.rem(within, owner_rows) * grid_side + tile_i, 1),
            :,
        ]

    scale = LOG2E / math.sqrt(HD)

    def one_row(row):
        blocks = head_blocks(qt[row])
        outs = []
        for pair in range(0, H, 2):
            scores = nn(kn[row], blocks[:, pair * wide : (pair + 2) * wide])
            yield
            for h in range(pair, pair + 2):
                part = scores[:, (h - pair) * wide : (h - pair + 1) * wide] * scale + bias_t[h]
                peak = jnp.max(part, axis=0, keepdims=True)
                yield
                part = jnp.exp2(part - peak)
                total = jnp.sum(part, axis=0, keepdims=True)
                yield
                part_b = (part * (1.0 / total)).astype(BF)
                at[row, :, h * wide : (h + 1) * wide] = part_b
                yield
                outs.append(nn(vt[row, h * HD : (h + 1) * HD, :], part_b))
                ot[row, h * HD : (h + 1) * HD, :] = outs[-1]
                yield
        gated = (gt[row] * ot[row]).astype(BF)
        yield
        both = nn(wod[...], gated) + nt(wdt[...], zr[row])
        yield
        logit = both[:NB] + both[NB:]
        ut[row] = logit
        high = logit.astype(BF).astype(F32)
        yield
        packed = jnp.concatenate([high, logit - high], axis=0).T
        here = step * rows + row
        yield
        for i in range(grid_side):
            for p in range(groups):
                for j in range(grid_side):
                    source = ((i * groups + p) * grid_side + j) * group_rows
                    target = ((i * grid_side + j) * share + p * group_rows) * count
                    stage[pl.ds(target + here, group_rows, stride=count), :] = packed[
                        source : source + group_rows
                    ]
                yield

    interleave([one_row(row) for row in range(rows)], FWD_PACE)

    @pl.when(step == pl.num_programs(0) - 1)
    def _():
        for k in range(tiles):
            start = (mine ^ k) * (share * count)
            for r in range(share):
                sends[k][r] = stage[
                    pl.ds(pl.multiple_of(start + r * count, 8), count), :
                ].astype(BF)


def backward_kernel(*refs, tiles, chunks, grid_side, groups, group_rows):
    rcv = refs[: tiles * chunks]
    tgt, at, ot, ut, gt, vn, kt, qt, wo, wd3, wall, cst, dpt, dzn = refs[
        tiles * chunks : tiles * chunks + 14
    ]
    sends = refs[tiles * chunks + 14 : tiles * chunks + 14 + tiles]
    acc, grad_s, back_s, mirror_s, order = refs[tiles * chunks + 14 + tiles :]
    width = H * HD
    step = pl.program_id(0)
    mine = lax.axis_index("tile")
    rows = vn.shape[0]
    wide = vn.shape[1]
    chunk_groups = groups // chunks
    share = groups * group_rows
    inv_root = 1.0 / math.sqrt(HD)
    adder = jnp.concatenate([eye(NB)] * 2, axis=1)
    bins = lax.broadcasted_iota(jnp.int32, (NB, 2 * wide), 0).astype(F32)

    @pl.when(step == 0)
    def _():
        acc[...] = jnp.zeros_like(acc)

    shift = jnp.concatenate([cst[...]] * 2, axis=1)

    def one_pair(first):
        pair = (first, first + 1)
        for row in pair:
            for k in range(tiles):
                source_i = (mine ^ k) // grid_side
                source_j = lax.rem(mine ^ k, grid_side)
                for p in range(groups):
                    start = ((source_i * groups + p) * grid_side + source_j) * group_rows
                    local = (p % chunk_groups) * group_rows
                    mirror_s[pl.ds(pl.multiple_of(row * wide + start, group_rows), group_rows), :] = rcv[
                        (p // chunk_groups) * tiles + k
                    ][row, local : local + group_rows].astype(F32)
        yield
        other = nt(adder, mirror_s[first * wide : (first + 2) * wide, :].astype(BF))
        yield
        logits = jnp.concatenate([ut[row] for row in pair], axis=1) + other + shift
        peak = jnp.max(logits, axis=0, keepdims=True)
        yield
        probs = jnp.exp(logits - peak)
        total = jnp.sum(probs, axis=0, keepdims=True)
        yield
        target = jnp.concatenate([tgt[row : row + 1, :] for row in pair], axis=1)
        resid = 2.0 * (probs * (1.0 / total) - jnp.where(bins == target, 1.0, 0.0))
        res_hi, res_lo = split(resid)
        yield
        pair_grad = nn(wd3[...], jnp.concatenate([res_hi, res_lo, res_hi], axis=0))
        for n, row in enumerate(pair):
            dpt[row] = pair_grad[:, n * wide : (n + 1) * wide]
        yield
        out_grad = nn(wo[...], pair_grad.astype(BF))
        yield
        for n, row in enumerate(pair):
            gate = gt[row]
            gated = out_grad[:, n * wide : (n + 1) * wide] * gate
            grad_s[row] = gated.astype(BF)
            back_s[3 * width :, row * wide : (row + 1) * wide] = (
                gated * ot[row] * (1.0 - gate)
            ).astype(BF)
            yield

        def heads(row):
            lanes = slice(row * wide, (row + 1) * wide)
            for h in range(H):
                part = slice(h * HD, (h + 1) * HD)
                back_s[2 * width + h * HD : 2 * width + (h + 1) * HD, lanes] = nt(
                    grad_s[row, part, :], at[row, :, h * wide : (h + 1) * wide]
                ).astype(BF)
                yield
                weight_grad = nn(vn[row], head_block(grad_s[row, part, :], h))
                yield
                prob = at[row, :, h * wide : (h + 1) * wide].astype(F32)
                prod = prob * weight_grad
                total = jnp.sum(prod, axis=0, keepdims=True)
                yield
                prod = prod - prob * total
                prod_b = prod.astype(BF)
                acc[h] += prod
                yield
                back_s[h * HD : (h + 1) * HD, lanes] = (nn(kt[row, part, :], prod_b) * inv_root).astype(BF)
                back_s[width + h * HD : width + (h + 1) * HD, lanes] = (
                    nt(qt[row, part, :], prod_b) * inv_root
                ).astype(BF)
                yield

        both = [heads(row) for row in pair]
        while both:
            for row in list(both):
                try:
                    next(row)
                except StopIteration:
                    both.remove(row)
            yield
        normed_grad = nn(wall[...], back_s[:, first * wide : (first + 2) * wide])
        for n, row in enumerate(pair):
            dzn[row] = normed_grad[:, n * wide : (n + 1) * wide]
        yield

    interleave([one_pair(row) for row in range(0, rows, 2)], BWD_PACE)

    @pl.when(step == pl.num_programs(0) - 1)
    def _():
        for h in range(H):
            grad = acc[h].T
            for i in range(grid_side):
                for j in range(grid_side):
                    pieces = []
                    for p in range(groups):
                        source = ((i * groups + p) * grid_side + j) * group_rows
                        pieces.append(grad[source : source + group_rows])
                    order[i * grid_side + j, h * share : (h + 1) * share, :] = jnp.concatenate(
                        pieces, axis=0
                    )
        for k in range(tiles):
            sends[k][...] = order[mine ^ k].reshape(H, share, wide).astype(BF)


def finish_kernel(offsets, *refs, tiles):
    rdb = refs[:tiles]
    dpt, dzn, zr, wgs, lgc, out, sums = refs[tiles:]
    step = pl.program_id(0)
    rows, chans, wide = dzn.shape
    states, _, piece, _ = out.shape
    total_rows = rdb[0].shape[1]
    turn = offsets[lax.axis_index("state")] // piece

    @pl.when(step == 0)
    def _():
        for h in range(H):
            total = rdb[0][h].astype(F32)
            for part in rdb[1:]:
                total = total + part[h].astype(F32)
            sums[pl.ds(h * total_rows, total_rows), :] = total

    ident = eye(chans)

    def one_row(row):
        local = step * rows + row
        pair_t = nt(ident, zr[row])
        yield
        center = pair_t - jnp.mean(pair_t, axis=0, keepdims=True)
        yield
        inverse = lax.rsqrt(jnp.mean(center * center, axis=0, keepdims=True) + EPS)
        normed = center * inverse
        yield
        parts = [sums[pl.ds(h * total_rows + local, 1), :] for h in range(H)]
        high, low = split(jnp.concatenate(parts, axis=0))
        spread = jnp.concatenate([high.astype(F32), low.astype(F32), high.astype(F32), jnp.zeros((H, wide), F32)], axis=0)
        yield
        scaled = (dzn[row] + nn(wgs[...], spread.astype(BF))) * lgc[...]
        yield
        mean_a = jnp.mean(scaled, axis=0, keepdims=True)
        mean_b = jnp.mean(scaled * normed, axis=0, keepdims=True)
        yield
        total = dpt[row] + inverse * (scaled - mean_a - normed * mean_b)
        yield
        total = total.T.astype(BF)
        for c in range(wide // piece):
            out[lax.rem(turn + c, states), row] = total[c * piece : (c + 1) * piece]
        yield

    interleave([one_row(row) for row in range(rows)], FIN_PACE)


def place_kernel(offsets, rcv, out, *, side):
    states, grid_side, rows, piece, chans = rcv.shape
    start = lax.axis_index("state") * piece
    out[...] = jnp.zeros_like(out)
    for s in range(states):
        offset = offsets[s]
        half = (start < offset).astype(jnp.int32)
        base = offset // side
        for i in range(grid_side):
            out[base + i, :, half] += rcv[s, i].astype(F32)


def on_device(
    pair_tiles,
    targets,
    offsets,
    ln_gain,
    ln_bias,
    w_query,
    w_key,
    w_value,
    w_pairbias,
    w_gate,
    gate_bias,
    w_output,
    out_bias,
    w_distogram,
    dist_bias,
):
    tiles = lax.axis_size("tile")
    states = lax.axis_size("state")
    side, chans = pair_tiles.shape[3], pair_tiles.shape[4]
    wide = targets.shape[4]
    grid_side = wide // side
    owner_rows = side // tiles
    width = H * HD
    here = lax.axis_index("tile")
    tile_i = here // grid_side
    tile_j = lax.rem(here, grid_side)
    even = owner_rows % grid_side == 0
    groups = tiles if even else 1
    group_rows = side // groups // grid_side
    share = groups * group_rows
    per_head = side * side // wide
    piece = wide // states

    def stay(value):
        return pltpu.with_memory_space_constraint(value, pltpu.HBM)

    def shapes(*pairs):
        return [jax.ShapeDtypeStruct(s, t) for s, t in pairs]

    tile = pair_tiles.reshape(groups, grid_side, group_rows, side, chans)

    def rows_of(j):
        return lax.dynamic_index_in_dim(tile, j, 1, keepdims=False).reshape(share, side, chans)

    parts = [tile]
    for k in range(1, grid_side):
        perm = [
            (i * grid_side + j, i * grid_side + (j + k) % grid_side)
            for i in range(grid_side)
            for j in range(grid_side)
        ]
        parts.append(lax.ppermute(rows_of(lax.rem(tile_j + k, grid_side)), "tile", perm))

    gain_row = ln_gain.reshape(1, chans)
    shift_row = ln_bias.reshape(1, chans)
    prep_shapes = shapes(
        ((4 * width, chans), BF),
        ((chans, 2 * width), BF),
        ((2 * NB, width), BF),
        ((2 * NB, chans), BF),
        ((chans, 3 * NB), BF),
        ((chans, 4 * width), BF),
        ((width, wide), F32),
        ((chans, wide), F32),
        ((NB, wide), F32),
        ((chans, 4 * H), BF),
    )
    w4t, w2, wod, wdt, wd3, wall, gbc, lgc, cst, wgs = pl.pallas_call(
        prep_kernel, out_shape=prep_shapes, name="prep",
        compiler_params=pltpu.CompilerParams(vmem_limit_bytes=VMEM_BYTES)
    )(
        *map(
            stay,
            (
                w_query,
                w_key,
                w_value,
                w_gate,
                w_output,
                gate_bias.reshape(1, width),
                out_bias.reshape(1, chans),
                w_distogram.T,
                dist_bias.reshape(1, NB),
                w_pairbias.T,
                gain_row,
            ),
        )
    )

    lines = 8
    bias_rows = H * per_head
    target_rows = owner_rows * grid_side
    bias_mine = pl.pallas_call(
        functools.partial(bias_kernel, per_head=per_head),
        grid=(per_head // lines,),
        in_specs=[
            pl.BlockSpec((grid_side, lines, side, chans), lambda g: (0, g, 0, 0)),
            full((target_rows, wide)),
            full((1, chans)),
            full((1, chans)),
            full((H, chans)),
        ],
        out_specs=full((bias_rows + target_rows, wide)),
        out_shape=jax.ShapeDtypeStruct((bias_rows + target_rows, wide), F32),
        name="bias",
        compiler_params=pltpu.CompilerParams(vmem_limit_bytes=VMEM_BYTES),
    )(
        *map(
            stay,
            (
                pair_tiles.reshape(grid_side, per_head, side, chans),
                targets.reshape(target_rows, wide),
                gain_row,
                shift_row,
                w_pairbias.T,
            ),
        )
    )

    def to_partner(value, k):
        return lax.ppermute(value, "tile", [(t, t ^ k) for t in range(tiles)]) if k else value

    gathered = [to_partner(bias_mine, k) for k in range(tiles)]

    def by_row(*shape, rows, base=0):
        return pl.BlockSpec((rows,) + shape, lambda g, *_: (g + base,) + (0,) * len(shape))

    def cost(flops, moved):
        return pl.CostEstimate(flops=flops, bytes_accessed=moved, transcendentals=0)

    cell = wide * width * wide
    square_b = ((share, wide, width), BF)
    zr, qt, kt, vt, kn, vn, gt = pl.pallas_call(
        functools.partial(project_kernel, parts=grid_side),
        grid_spec=pltpu.PrefetchScalarGridSpec(
            num_scalar_prefetch=1,
            grid=(groups,),
            in_specs=[
                pl.BlockSpec(
                    (None, None, group_rows, side, chans), lambda g, own: (g, own[0], 0, 0, 0)
                )
            ]
            + [by_row(side, chans, rows=group_rows)] * (grid_side - 1)
            + [full((1, chans)), full((1, chans)), full(w4t.shape), full(w2.shape), full(gbc.shape)],
            out_specs=[by_row(wide, width, rows=group_rows)] * 7,
            scratch_shapes=[pltpu.VMEM((group_rows * wide, chans), BF)],
        ),
        out_shape=shapes(*([square_b] * 6), ((share, width, wide), F32)),
        cost_estimate=cost(80 * share * cell, 12 * share * wide * width * 2),
        name="project",
        compiler_params=pltpu.CompilerParams(vmem_limit_bytes=VMEM_BYTES),
    )(tile_j.reshape(1), *parts, gain_row, shift_row, w4t, w2, gbc)

    chunks = 2 if groups % 2 == 0 else 1
    chunk_groups = groups // chunks
    count = share // chunks
    block = group_rows
    layout = dict(grid_side=grid_side, groups=groups, group_rows=group_rows)
    saved_shapes = shapes(
        ((share, wide, H * wide), BF),
        ((share, width, wide), F32),
        ((share, NB, wide), F32),
        ((share, wide), F32),
        ((H, wide, wide), F32),
    )
    packed_shape = (share, count, 2 * NB)
    saved = []
    mirrored = []
    for c in range(chunks):
        base = c * chunk_groups
        inputs = [*gathered, kn, qt, vt, gt, zr, wod, wdt]
        first = len(inputs)
        call = pl.pallas_call(
            functools.partial(
                forward_kernel,
                tiles=tiles,
                base=base,
                count=count,
                bias_rows=bias_rows,
                owner_rows=owner_rows,
                extra=len(saved),
                **layout,
            ),
            grid=(count // block,),
            in_specs=[full(gathered[0].shape)] * tiles
            + [by_row(wide, width, rows=block, base=base)] * 5
            + [full(wod.shape), full(wdt.shape)]
            + [pl.BlockSpec(memory_space=pl.ANY)] * len(saved),
            out_specs=[
                by_row(wide, H * wide, rows=block, base=base),
                by_row(width, wide, rows=block, base=base),
                by_row(NB, wide, rows=block, base=base),
                by_row(wide, rows=block, base=base),
                full((H, wide, wide)),
            ]
            + [full(packed_shape)] * tiles,
            out_shape=saved_shapes + shapes(*([(packed_shape, BF)] * tiles)),
            scratch_shapes=[
                pltpu.VMEM((tiles,) + gathered[0].shape, F32),
                pltpu.VMEM((tiles * share * count, 2 * NB), F32),
            ],
            input_output_aliases={first + n: n for n in range(len(saved))},
            cost_estimate=cost(150 * count * cell, 14 * count * wide * width * 2),
            name="forward",
        compiler_params=pltpu.CompilerParams(vmem_limit_bytes=VMEM_BYTES),
        )
        results = call(*inputs, *saved)
        saved = list(results[:4])
        mirrored.append([to_partner(results[5 + k], k) for k in range(tiles)])
    at, ot, ut, tgt = saved

    results = pl.pallas_call(
        functools.partial(backward_kernel, tiles=tiles, chunks=chunks, **layout),
        grid=(share // block,),
        in_specs=[by_row(count, 2 * NB, rows=block)] * (tiles * chunks)
        + [
            by_row(wide, rows=block),
            by_row(wide, H * wide, rows=block),
            by_row(width, wide, rows=block),
            by_row(NB, wide, rows=block),
        ]
        + [by_row(wide, width, rows=block)] * 4
        + [full(w.shape) for w in (w_output, wd3, wall, cst)],
        out_specs=[by_row(chans, wide, rows=block)] * 2 + [full((H, share, wide))] * tiles,
        out_shape=shapes(*([((share, chans, wide), F32)] * 2), *([((H, share, wide), BF)] * tiles)),
        scratch_shapes=[
            pltpu.VMEM((H, wide, wide), F32),
            pltpu.VMEM((block, width, wide), BF),
            pltpu.VMEM((4 * width, block * wide), BF),
            pltpu.VMEM((block * wide, 2 * NB), F32),
            pltpu.VMEM((tiles, H * share, wide), F32),
        ],
        cost_estimate=cost(500 * share * cell, 20 * share * wide * width * 2),
        name="backward",
        compiler_params=pltpu.CompilerParams(vmem_limit_bytes=VMEM_BYTES),
    )(
        *[part for parts_c in mirrored for part in parts_c],
        tgt, at, ot, ut, gt, vn, kt, qt, w_output, wd3, wall, cst,
    )
    dpt, dzn = results[:2]
    rdb = [to_partner(results[2 + k], k) for k in range(tiles)]

    block = FIN_ROWS if share % FIN_ROWS == 0 else 1
    outgoing = pl.pallas_call(
        functools.partial(finish_kernel, tiles=tiles),
        grid_spec=pltpu.PrefetchScalarGridSpec(
            num_scalar_prefetch=1,
            grid=(share // block,),
            in_specs=[
                *([full(rdb[0].shape)] * tiles),
                pl.BlockSpec((block, chans, wide), lambda g, _: (g, 0, 0)),
                pl.BlockSpec((block, chans, wide), lambda g, _: (g, 0, 0)),
                pl.BlockSpec((block, wide, chans), lambda g, _: (g, 0, 0)),
                full(wgs.shape),
                full(lgc.shape),
            ],
            out_specs=pl.BlockSpec((states, block, piece, chans), lambda g, _: (0, g, 0, 0)),
            scratch_shapes=[pltpu.VMEM((H * share, wide), F32)],
        ),
        out_shape=jax.ShapeDtypeStruct((states, share, piece, chans), BF),
        name="finish",
        compiler_params=pltpu.CompilerParams(vmem_limit_bytes=VMEM_BYTES),
    )(offsets, *rdb, dpt, dzn, zr, wgs, lgc)

    if even:
        slots = outgoing.reshape(states * tiles, group_rows, piece, chans)
    else:
        slots = lax.dynamic_update_slice(
            jnp.zeros((states, tiles, owner_rows, piece, chans), BF),
            outgoing.reshape(states, grid_side, owner_rows, piece, chans),
            (0, tile_j * grid_side, 0, 0, 0),
        ).reshape(states * tiles, owner_rows, piece, chans)
    received = lax.all_to_all(slots, ("state", "tile"), split_axis=0, concat_axis=0, tiled=True)
    if even:
        received = received.reshape(states, grid_side, owner_rows, piece, chans)
    else:
        received = lax.dynamic_index_in_dim(
            received.reshape(states, grid_side, grid_side, owner_rows, piece, chans),
            tile_i,
            2,
            keepdims=False,
        )

    block = 4 if owner_rows % 4 == 0 else 1
    out_shape = (2 * grid_side, owner_rows, 2, piece, chans)
    placed = pl.pallas_call(
        functools.partial(place_kernel, side=side),
        grid_spec=pltpu.PrefetchScalarGridSpec(
            num_scalar_prefetch=1,
            grid=(owner_rows // block,),
            in_specs=[
                pl.BlockSpec(
                    (states, grid_side, block, piece, chans), lambda g, _: (0, 0, g, 0, 0)
                )
            ],
            out_specs=pl.BlockSpec(
                (2 * grid_side, block, 2, piece, chans), lambda g, _: (0, g, 0, 0, 0)
            ),
        ),
        out_shape=jax.ShapeDtypeStruct(out_shape, F32),
        name="place",
        compiler_params=pltpu.CompilerParams(vmem_limit_bytes=VMEM_BYTES),
    )(offsets, received)
    return placed.reshape(2 * grid_side, 1, owner_rows, 2, piece, chans)


def solution(mesh):
    in_specs = (
        P("state", "tile", None, None, None),
        P("state", "tile", None, None, None),
    ) + (P(),) * 13
    out_specs = P(None, "tile", None, None, "state", None)
    return jax.shard_map(
        on_device, mesh=mesh, in_specs=in_specs, out_specs=out_specs, check_vma=False
    )
```

```python
import functools
import math

import jax
import jax.numpy as jnp
from jax import lax
from jax.experimental import pallas as pl
from jax.experimental.pallas import tpu as pltpu
from jax.sharding import PartitionSpec as P

VMEM_BYTES = 16 << 20
H = 4
HD = 32
NB = 64
FWD_ROWS = 8
BWD_ROWS = 8
FWD_PACE = (8, 1, 0)
BWD_PACE = (2, 0, 3)
PROJ_PACE = (2, 0, 3)
FIN_PACE = (8, 1, 0)
MID_PACE = (8, 1, 0)
PROJ_ROWS = 8
FIN_ROWS = 8
EPS = 1e-5
LOG2E = 1.0 / math.log(2.0)
BF = jnp.bfloat16
F32 = jnp.float32
HIGHEST = lax.Precision.HIGHEST


def nn(left, right, **kw):
    return lax.dot_general(left, right, (((1,), (0,)), ((), ())), preferred_element_type=F32, **kw)


def nt(left, right, **kw):
    return lax.dot_general(left, right, (((1,), (1,)), ((), ())), preferred_element_type=F32, **kw)


def split(value):
    high = value.astype(BF)
    low = (value - high.astype(F32)).astype(BF)
    return high, low


def transposed(value):
    return value.astype(F32).T.astype(value.dtype)


def column(row, lanes):
    return jnp.broadcast_to(row, (lanes, row.shape[1])).T


def eye(size):
    rows = lax.broadcasted_iota(jnp.int32, (size, size), 0)
    cols = lax.broadcasted_iota(jnp.int32, (size, size), 1)
    return jnp.where(rows == cols, 1.0, 0.0).astype(BF)


def rows_norm(pair_rows):
    mean = jnp.mean(pair_rows, axis=-1, keepdims=True)
    center = pair_rows - mean
    inverse = lax.rsqrt(jnp.mean(center * center, axis=-1, keepdims=True) + EPS)
    return center * inverse


def interleave(rows, pace):
    size, inner, outer = pace
    begin = {row: (r % size) * inner + (r // size) * outer for r, row in enumerate(rows)}
    tick = 0
    while begin:
        for row in list(begin):
            if begin[row] <= tick:
                try:
                    next(row)
                except StopIteration:
                    del begin[row]
        tick += 1


def full(shape):
    return pl.BlockSpec(shape, lambda *_: (0,) * len(shape))


def prep_kernel(wq, wk, wv, wg, wo, gb, wd, w4t, w2, wod, wdt, gbc):
    w4t[...] = jnp.concatenate([transposed(w[...]) for w in (wq, wk, wv, wg)], axis=0)
    w2[...] = jnp.concatenate([wk[...], wv[...]], axis=1)
    wdt[...] = jnp.concatenate(split(wd[...]), axis=0)
    both = nt(wd[...], wo[...].astype(F32), precision=HIGHEST)
    wod[...] = jnp.concatenate(split(both), axis=0)
    gbc[...] = column(gb[...], gbc.shape[1])


def middle_kernel(after, zr, wq, wk, wv, wg, ob, wd, db, wpb, lng, nrm, inv, wd3, wall, lgc, cst, wgs):
    del after
    rows, wide, chans = zr.shape

    @pl.when(pl.program_id(0) == 0)
    def _():
        wall[...] = jnp.concatenate([wq[...], wk[...], wv[...], wg[...]], axis=1)
        dist_hi, dist_lo = split(wd[...].T)
        wd3[...] = jnp.concatenate([dist_hi, dist_hi, dist_lo], axis=1)
        lgc[...] = column(lng[...], wide)
        shift = 2.0 * jnp.sum(wd[...] * ob[...], axis=1, keepdims=True)
        cst[...] = column(db[...], wide) + shift
        proj = wpb[...] * lng[...]
        proj = jnp.concatenate([proj, jnp.zeros((wide - H, chans), F32)], axis=0).T[:, :H]
        proj_hi, proj_lo = split(proj)
        wgs[...] = jnp.concatenate([proj_hi, proj_hi, proj_lo, jnp.zeros_like(proj_lo)], axis=1)

    ident = eye(chans)

    def one_row(row):
        pair_t = nt(ident, zr[row])
        yield
        center = pair_t - jnp.mean(pair_t, axis=0, keepdims=True)
        yield
        inverse = lax.rsqrt(jnp.mean(center * center, axis=0, keepdims=True) + EPS)
        inv[row : row + 1, :] = inverse
        nrm[row] = center * inverse
        yield

    interleave([one_row(row) for row in range(rows)], MID_PACE)


def main_kernel(dpt, dzn, nrm, inv, lgc, base):
    def one_row(row):
        scaled = dzn[row] * lgc[...]
        mean_a = jnp.mean(scaled, axis=0, keepdims=True)
        mean_b = jnp.mean(scaled * nrm[row], axis=0, keepdims=True)
        yield
        base[row] = dpt[row] + inv[row : row + 1, :] * (scaled - mean_a - nrm[row] * mean_b)
        yield

    interleave([one_row(row) for row in range(dzn.shape[0])], MID_PACE)


def bias_kernel(tile, targets, lng, lnb, wpb, out, *, per_head):
    step = pl.program_id(0)
    fold, lines, side, chans = tile.shape
    pieces = [tile[f, q] for q in range(lines) for f in range(fold)]
    pair = jnp.concatenate(pieces, axis=0)
    proj = wpb[...] * lng[...]
    high, rest = split(proj)
    mid = rest
    last = (proj - high.astype(F32) - mid.astype(F32)).astype(BF)
    left = jnp.concatenate(
        [high.astype(F32), mid.astype(F32), last.astype(F32), jnp.ones((H, chans), F32)], axis=0
    ).astype(BF)
    left = jnp.concatenate([eye(chans), left], axis=0)
    total = jnp.sum(proj, axis=1, keepdims=True)
    const = jnp.sum(wpb[...] * lnb[...], axis=1, keepdims=True)
    size = fold * side
    rows_out = []
    for q in range(lines):
        up = nt(left, pair[q * size : (q + 1) * size])
        extra = up[chans:]
        mean = extra[3 * H : 3 * H + 1] * (1.0 / chans)
        center = up[:chans] - mean
        inverse = lax.rsqrt(jnp.mean(center * center, axis=0, keepdims=True) + EPS)
        dotted = extra[:H] + extra[H : 2 * H] + extra[2 * H : 3 * H]
        rows_out.append(inverse * (dotted - mean * total) + const)
    bias = jnp.concatenate(rows_out, axis=1)
    width = fold * side
    for q in range(lines):
        for h in range(H):
            out[pl.ds(h * per_head + step * lines + q, 1), :] = bias[
                h : h + 1, q * width : (q + 1) * width
            ]

    @pl.when(step == 0)
    def _():
        count = targets.shape[0]
        out[pl.ds(H * per_head, count), :] = targets[...].astype(F32)


def project_kernel(own_ref, *refs, parts):
    own = own_ref[0]
    part_refs = refs[:parts]
    lng, lnb, w4t, w2, gbc, zr, qt, kt, vt, kn, vn, gt, flat_s = refs[parts:]
    rows, side, _ = part_refs[0].shape
    wide = zr.shape[1]
    width = H * HD
    for row in range(rows):
        for k in range(parts):
            block = lax.rem(own + parts - k, parts)
            zr[row, pl.ds(pl.multiple_of(block * side, side), side), :] = part_refs[k][row]

    def one_row(row):
        pair_row = zr[row].astype(F32)
        center = pair_row - jnp.mean(pair_row, axis=-1, keepdims=True)
        yield
        inverse = lax.rsqrt(jnp.mean(center * center, axis=-1, keepdims=True) + EPS)
        yield
        flat_s[row * wide : (row + 1) * wide, :] = (
            center * inverse * lng[...] + lnb[...]
        ).astype(BF)
        yield

    def one_pair(first):
        both = one_row(first), one_row(first + 1)
        for _ in range(3):
            for row in both:
                next(row)
            yield
        flat = flat_s[first * wide : (first + 2) * wide, :]
        for k, out in enumerate((qt, kt, vt)):
            up = nt(w4t[k * width : (k + 1) * width], flat)
            for n in range(2):
                out[first + n] = up[:, n * wide : (n + 1) * wide].astype(BF)
            yield
        up = nt(w4t[3 * width :], flat)
        for n in range(2):
            gt[first + n] = jax.nn.sigmoid(up[:, n * wide : (n + 1) * wide] + gbc[...])
            yield
        down = nn(flat, w2[...])
        for n in range(2):
            kn[first + n] = down[n * wide : (n + 1) * wide, :width].astype(BF)
            vn[first + n] = down[n * wide : (n + 1) * wide, width:].astype(BF)
        yield

    interleave([one_pair(row) for row in range(0, rows, 2)], PROJ_PACE)


def head_block(part, h):
    lanes = part.shape[1]
    pieces = []
    if h:
        pieces.append(jnp.zeros((h * HD, lanes), part.dtype))
    pieces.append(part)
    if h < H - 1:
        pieces.append(jnp.zeros(((H - 1 - h) * HD, lanes), part.dtype))
    return jnp.concatenate(pieces, axis=0)


def head_blocks(packed):
    return jnp.concatenate(
        [head_block(packed[h * HD : (h + 1) * HD], h) for h in range(H)], axis=1
    )


def forward_kernel(
    *refs, tiles, base, count, bias_rows, owner_rows, extra, grid_side, groups, group_rows
):
    gath = refs[:tiles]
    kn, qt, vt, gt, zr, wod, wdt = refs[tiles : tiles + 7]
    at, ot, ut, tgt, bias_t = refs[tiles + 7 + extra : tiles + 12 + extra]
    sends = refs[tiles + 12 + extra : 2 * tiles + 12 + extra]
    order, stage = refs[2 * tiles + 12 + extra :]
    step = pl.program_id(0)
    mine = lax.axis_index("tile")
    tile_i = mine // grid_side
    tile_j = lax.rem(mine, grid_side)
    rows = kn.shape[0]
    wide = kn.shape[1]
    side = wide // grid_side
    per_head = side * side // wide
    share = groups * group_rows
    span = side // groups

    @pl.when(step == 0)
    def _():
        for k in range(tiles):
            order[mine ^ k] = gath[k][...]
        lane = lax.broadcasted_iota(jnp.int32, (per_head, wide), 1) // side
        for h in range(H):
            pieces = []
            for i in range(grid_side):
                for f in range(grid_side):
                    total = None
                    for j in range(grid_side):
                        part = order[i * grid_side + j, h * per_head : (h + 1) * per_head, :]
                        turn = ((j - f) * side) % wide
                        if turn:
                            part = pltpu.roll(part, turn, 1)
                        total = part if total is None else jnp.where(lane == j, part, total)
                    pieces.append(total)
            bias_t[h] = jnp.concatenate(pieces, axis=0).T * LOG2E

    for row in range(rows):
        within = (base + step) * span + tile_j * group_rows + row
        tgt[row : row + 1, :] = order[
            within // owner_rows,
            pl.ds(bias_rows + lax.rem(within, owner_rows) * grid_side + tile_i, 1),
            :,
        ]

    scale = LOG2E / math.sqrt(HD)

    def one_row(row):
        blocks = head_blocks(qt[row])
        outs = []
        for pair in range(0, H, 2):
            scores = nn(kn[row], blocks[:, pair * wide : (pair + 2) * wide])
            yield
            for h in range(pair, pair + 2):
                part = scores[:, (h - pair) * wide : (h - pair + 1) * wide] * scale + bias_t[h]
                peak = jnp.max(part, axis=0, keepdims=True)
                yield
                part = jnp.exp2(part - peak)
                total = jnp.sum(part, axis=0, keepdims=True)
                yield
                part_b = (part * (1.0 / total)).astype(BF)
                at[row, :, h * wide : (h + 1) * wide] = part_b
                yield
                outs.append(nn(vt[row, h * HD : (h + 1) * HD, :], part_b))
                ot[row, h * HD : (h + 1) * HD, :] = outs[-1]
                yield
        gated = (gt[row] * ot[row]).astype(BF)
        yield
        both = nn(wod[...], gated) + nt(wdt[...], zr[row])
        yield
        logit = both[:NB] + both[NB:]
        ut[row] = logit
        logit = logit - jnp.max(logit, axis=0, keepdims=True)
        yield
        packed = jnp.concatenate([logit, logit], axis=0).T
        here = step * rows + row
        yield
        for i in range(grid_side):
            for p in range(groups):
                for j in range(grid_side):
                    source = ((i * groups + p) * grid_side + j) * group_rows
                    target = ((i * grid_side + j) * share + p * group_rows) * count
                    stage[pl.ds(target + here, group_rows, stride=count), :] = packed[
                        source : source + group_rows
                    ]
                yield

    interleave([one_row(row) for row in range(rows)], FWD_PACE)

    @pl.when(step == pl.num_programs(0) - 1)
    def _():
        left = lax.broadcasted_iota(jnp.int32, (count // 2, 2 * NB), 1) < NB
        for k in range(tiles):
            start = (mine ^ k) * (share * count)
            for r in range(share):
                both = stage[pl.ds(pl.multiple_of(start + r * count, 8), count), :]
                sends[k][r] = jnp.where(left, both[: count // 2], both[count // 2 :]).astype(BF)


def backward_kernel(*refs, tiles, chunks, grid_side, groups, group_rows):
    rcv = refs[: tiles * chunks]
    tgt, at, ot, ut, gt, vn, kt, qt, wo, wd3, wall, cst, dpt, dzn = refs[
        tiles * chunks : tiles * chunks + 14
    ]
    sends = refs[tiles * chunks + 14 : tiles * chunks + 14 + tiles]
    acc, grad_s, back_s, mirror_s, order = refs[tiles * chunks + 14 + tiles :]
    width = H * HD
    step = pl.program_id(0)
    mine = lax.axis_index("tile")
    rows = vn.shape[0]
    wide = vn.shape[1]
    chunk_groups = groups // chunks
    share = groups * group_rows
    inv_root = 1.0 / math.sqrt(HD)
    adder = jnp.concatenate([eye(NB)] * 2, axis=1)
    bins = lax.broadcasted_iota(jnp.int32, (NB, 2 * wide), 0).astype(F32)

    @pl.when(step == 0)
    def _():
        acc[...] = jnp.zeros_like(acc)

    shift = jnp.concatenate([cst[...]] * 2, axis=1)
    left = lax.broadcasted_iota(jnp.int32, (rcv[0].shape[1], 2 * NB), 1) < NB

    def one_pair(first):
        pair = (first, first + 1)
        for row in pair:
            for k in range(tiles):
                source_i = (mine ^ k) // grid_side
                source_j = lax.rem(mine ^ k, grid_side)
                for c in range(chunks):
                    part = rcv[c * tiles + k][row].astype(F32)
                    part = jnp.concatenate(
                        [jnp.where(left, part, 0.0), jnp.where(left, 0.0, part)], axis=0
                    )
                    for p in range(chunk_groups):
                        start = (
                            (source_i * groups + c * chunk_groups + p) * grid_side + source_j
                        ) * group_rows + row * wide
                        mirror_s[pl.ds(pl.multiple_of(start, group_rows), group_rows), :] = part[
                            p * group_rows : (p + 1) * group_rows
                        ]
        yield
        other = nt(adder, mirror_s[first * wide : (first + 2) * wide, :].astype(BF))
        yield
        logits = jnp.concatenate([ut[row] for row in pair], axis=1) + other + shift
        peak = jnp.max(logits, axis=0, keepdims=True)
        yield
        probs = jnp.exp(logits - peak)
        total = jnp.sum(probs, axis=0, keepdims=True)
        yield
        target = jnp.concatenate([tgt[row : row + 1, :] for row in pair], axis=1)
        resid = 2.0 * (probs * (1.0 / total) - jnp.where(bins == target, 1.0, 0.0))
        res_hi, res_lo = split(resid)
        yield
        pair_grad = nn(wd3[...], jnp.concatenate([res_hi, res_lo, res_hi], axis=0))
        for n, row in enumerate(pair):
            dpt[row] = pair_grad[:, n * wide : (n + 1) * wide]
        yield
        out_grad = nn(wo[...], pair_grad.astype(BF))
        yield
        for n, row in enumerate(pair):
            gate = gt[row]
            gated = out_grad[:, n * wide : (n + 1) * wide] * gate
            grad_s[row] = gated.astype(BF)
            back_s[3 * width :, row * wide : (row + 1) * wide] = (
                gated * ot[row] * (1.0 - gate)
            ).astype(BF)
            yield

        def heads(row):
            lanes = slice(row * wide, (row + 1) * wide)
            for h in range(H):
                part = slice(h * HD, (h + 1) * HD)
                back_s[2 * width + h * HD : 2 * width + (h + 1) * HD, lanes] = nt(
                    grad_s[row, part, :], at[row, :, h * wide : (h + 1) * wide]
                ).astype(BF)
                yield
                weight_grad = nn(vn[row], head_block(grad_s[row, part, :], h))
                yield
                prob = at[row, :, h * wide : (h + 1) * wide].astype(F32)
                prod = prob * weight_grad
                total = jnp.sum(prod, axis=0, keepdims=True)
                yield
                prod = prod - prob * total
                prod_b = prod.astype(BF)
                acc[h] += prod
                yield
                back_s[h * HD : (h + 1) * HD, lanes] = (nn(kt[row, part, :], prod_b) * inv_root).astype(BF)
                back_s[width + h * HD : width + (h + 1) * HD, lanes] = (
                    nt(qt[row, part, :], prod_b) * inv_root
                ).astype(BF)
                yield

        both = [heads(row) for row in pair]
        while both:
            for row in list(both):
                try:
                    next(row)
                except StopIteration:
                    both.remove(row)
            yield
        normed_grad = nn(wall[...], back_s[:, first * wide : (first + 2) * wide])
        for n, row in enumerate(pair):
            dzn[row] = normed_grad[:, n * wide : (n + 1) * wide]
        yield

    interleave([one_pair(row) for row in range(0, rows, 2)], BWD_PACE)

    @pl.when(step == pl.num_programs(0) - 1)
    def _():
        for h in range(H):
            grad = acc[h].T
            for i in range(grid_side):
                for j in range(grid_side):
                    pieces = []
                    for p in range(groups):
                        source = ((i * groups + p) * grid_side + j) * group_rows
                        pieces.append(grad[source : source + group_rows])
                    order[i * grid_side + j, h * share : (h + 1) * share, :] = jnp.concatenate(
                        pieces, axis=0
                    )
        for k in range(tiles):
            sends[k][...] = order[mine ^ k].reshape(H, share, wide).astype(BF)


def finish_kernel(offsets, *refs, tiles):
    rdb = refs[:tiles]
    base, nrm, inv, wgs, out, sums = refs[tiles:]
    step = pl.program_id(0)
    rows, chans, wide = base.shape
    states, _, piece, _ = out.shape
    total_rows = rdb[0].shape[1]
    turn = offsets[lax.axis_index("state")] // piece

    @pl.when(step == 0)
    def _():
        for h in range(H):
            total = rdb[0][h].astype(F32)
            for part in rdb[1:]:
                total = total + part[h].astype(F32)
            sums[pl.ds(h * total_rows, total_rows), :] = total

    def one_row(row):
        local = step * rows + row
        parts = [sums[pl.ds(h * total_rows + local, 1), :] for h in range(H)]
        high, low = split(jnp.concatenate(parts, axis=0))
        high, low = high.astype(F32), low.astype(F32)
        spread = jnp.concatenate([high, low, high, jnp.zeros((H, wide), F32)], axis=0)
        yield
        scaled = nn(wgs[...], spread.astype(BF))
        yield
        mean_a = jnp.mean(scaled, axis=0, keepdims=True)
        mean_b = jnp.mean(scaled * nrm[row], axis=0, keepdims=True)
        yield
        total = base[row] + inv[row : row + 1, :] * (scaled - mean_a - nrm[row] * mean_b)
        yield
        total = total.T.astype(BF)
        for c in range(wide // piece):
            out[lax.rem(turn + c, states), row] = total[c * piece : (c + 1) * piece]
        yield

    interleave([one_row(row) for row in range(rows)], FIN_PACE)


def place_kernel(offsets, rcv, out, *, side):
    states, grid_side, rows, piece, chans = rcv.shape
    start = lax.axis_index("state") * piece
    out[...] = jnp.zeros_like(out)
    for s in range(states):
        offset = offsets[s]
        half = (start < offset).astype(jnp.int32)
        base = offset // side
        for i in range(grid_side):
            out[base + i, :, half] += rcv[s, i].astype(F32)


def on_device(
    pair_tiles,
    targets,
    offsets,
    ln_gain,
    ln_bias,
    w_query,
    w_key,
    w_value,
    w_pairbias,
    w_gate,
    gate_bias,
    w_output,
    out_bias,
    w_distogram,
    dist_bias,
):
    tiles = lax.axis_size("tile")
    states = lax.axis_size("state")
    side, chans = pair_tiles.shape[3], pair_tiles.shape[4]
    wide = targets.shape[4]
    grid_side = wide // side
    owner_rows = side // tiles
    width = H * HD
    here = lax.axis_index("tile")
    tile_i = here // grid_side
    tile_j = lax.rem(here, grid_side)
    even = owner_rows % grid_side == 0
    groups = tiles if even else 1
    group_rows = side // groups // grid_side
    share = groups * group_rows
    per_head = side * side // wide
    piece = wide // states

    def stay(value):
        return pltpu.with_memory_space_constraint(value, pltpu.HBM)

    def shapes(*pairs):
        return [jax.ShapeDtypeStruct(s, t) for s, t in pairs]

    tile = pair_tiles.reshape(groups, grid_side, group_rows, side, chans)

    def rows_of(j):
        return lax.dynamic_index_in_dim(tile, j, 1, keepdims=False).reshape(share, side, chans)

    parts = [tile]
    for k in range(1, grid_side):
        perm = [
            (i * grid_side + j, i * grid_side + (j + k) % grid_side)
            for i in range(grid_side)
            for j in range(grid_side)
        ]
        parts.append(lax.ppermute(rows_of(lax.rem(tile_j + k, grid_side)), "tile", perm))

    gain_row = ln_gain.reshape(1, chans)
    shift_row = ln_bias.reshape(1, chans)
    prep_shapes = shapes(
        ((4 * width, chans), BF),
        ((chans, 2 * width), BF),
        ((2 * NB, width), BF),
        ((2 * NB, chans), BF),
        ((width, wide), F32),
    )
    w4t, w2, wod, wdt, gbc = pl.pallas_call(
        prep_kernel,
        out_shape=prep_shapes,
        name="prep",
        compiler_params=pltpu.CompilerParams(vmem_limit_bytes=VMEM_BYTES),
    )(
        *map(
            stay,
            (
                w_query,
                w_key,
                w_value,
                w_gate,
                w_output,
                gate_bias.reshape(1, width),
                w_distogram.T,
            ),
        )
    )

    lines = 8
    bias_rows = H * per_head
    target_rows = owner_rows * grid_side
    bias_mine = pl.pallas_call(
        functools.partial(bias_kernel, per_head=per_head),
        grid=(per_head // lines,),
        in_specs=[
            pl.BlockSpec((grid_side, lines, side, chans), lambda g: (0, g, 0, 0)),
            full((target_rows, wide)),
            full((1, chans)),
            full((1, chans)),
            full((H, chans)),
        ],
        out_specs=full((bias_rows + target_rows, wide)),
        out_shape=jax.ShapeDtypeStruct((bias_rows + target_rows, wide), F32),
        name="bias",
        compiler_params=pltpu.CompilerParams(vmem_limit_bytes=VMEM_BYTES),
    )(
        *map(
            stay,
            (
                pair_tiles.reshape(grid_side, per_head, side, chans),
                targets.reshape(target_rows, wide),
                gain_row,
                shift_row,
                w_pairbias.T,
            ),
        )
    )

    def to_partner(value, k):
        return lax.ppermute(value, "tile", [(t, t ^ k) for t in range(tiles)]) if k else value

    gathered = [to_partner(bias_mine, k) for k in range(tiles)]

    def by_row(*shape, rows, base=0):
        return pl.BlockSpec((rows,) + shape, lambda g, *_: (g + base,) + (0,) * len(shape))

    def cost(flops, moved):
        return pl.CostEstimate(flops=flops, bytes_accessed=moved, transcendentals=0)

    cell = wide * width * wide
    square_b = ((share, wide, width), BF)
    zr, qt, kt, vt, kn, vn, gt = pl.pallas_call(
        functools.partial(project_kernel, parts=grid_side),
        grid_spec=pltpu.PrefetchScalarGridSpec(
            num_scalar_prefetch=1,
            grid=(groups,),
            in_specs=[
                pl.BlockSpec(
                    (None, None, group_rows, side, chans), lambda g, own: (g, own[0], 0, 0, 0)
                )
            ]
            + [by_row(side, chans, rows=group_rows)] * (grid_side - 1)
            + [full((1, chans)), full((1, chans)), full(w4t.shape), full(w2.shape), full(gbc.shape)],
            out_specs=[by_row(wide, width, rows=group_rows)] * 7,
            scratch_shapes=[pltpu.VMEM((group_rows * wide, chans), BF)],
        ),
        out_shape=shapes(*([square_b] * 6), ((share, width, wide), F32)),
        cost_estimate=cost(80 * share * cell, 12 * share * wide * width * 2),
        name="project",
        compiler_params=pltpu.CompilerParams(vmem_limit_bytes=VMEM_BYTES),
    )(tile_j.reshape(1), *parts, gain_row, shift_row, w4t, w2, gbc)

    chunks = 2 if groups % 2 == 0 else 1
    chunk_groups = groups // chunks
    count = share // chunks
    block = group_rows
    layout = dict(grid_side=grid_side, groups=groups, group_rows=group_rows)
    saved_shapes = shapes(
        ((share, wide, H * wide), BF),
        ((share, width, wide), F32),
        ((share, NB, wide), F32),
        ((share, wide), F32),
        ((H, wide, wide), F32),
    )
    packed_shape = (share, count // 2, 2 * NB)
    saved = []
    mirrored = []
    for c in range(chunks):
        base = c * chunk_groups
        inputs = [*gathered, kn, qt, vt, gt, zr, wod, wdt]
        first = len(inputs)
        call = pl.pallas_call(
            functools.partial(
                forward_kernel,
                tiles=tiles,
                base=base,
                count=count,
                bias_rows=bias_rows,
                owner_rows=owner_rows,
                extra=len(saved),
                **layout,
            ),
            grid=(count // block,),
            in_specs=[full(gathered[0].shape)] * tiles
            + [by_row(wide, width, rows=block, base=base)] * 5
            + [full(wod.shape), full(wdt.shape)]
            + [pl.BlockSpec(memory_space=pl.ANY)] * len(saved),
            out_specs=[
                by_row(wide, H * wide, rows=block, base=base),
                by_row(width, wide, rows=block, base=base),
                by_row(NB, wide, rows=block, base=base),
                by_row(wide, rows=block, base=base),
                full((H, wide, wide)),
            ]
            + [full(packed_shape)] * tiles,
            out_shape=saved_shapes + shapes(*([(packed_shape, BF)] * tiles)),
            scratch_shapes=[
                pltpu.VMEM((tiles,) + gathered[0].shape, F32),
                pltpu.VMEM((tiles * share * count, 2 * NB), F32),
            ],
            input_output_aliases={first + n: n for n in range(len(saved))},
            cost_estimate=cost(150 * count * cell, 14 * count * wide * width * 2),
            name="forward",
        compiler_params=pltpu.CompilerParams(vmem_limit_bytes=VMEM_BYTES),
        )
        results = call(*inputs, *saved)
        saved = list(results[:4])
        mirrored.append([to_partner(results[5 + k], k) for k in range(tiles)])
    at, ot, ut, tgt = saved

    late = (
        w_query,
        w_key,
        w_value,
        w_gate,
        out_bias.reshape(1, chans),
        w_distogram.T,
        dist_bias.reshape(1, NB),
        w_pairbias.T,
        gain_row,
    )
    late_shapes = (
        ((chans, 3 * NB), BF),
        ((chans, 4 * width), BF),
        ((chans, wide), F32),
        ((NB, wide), F32),
        ((chans, 4 * H), BF),
    )
    nrm, inv, wd3, wall, lgc, cst, wgs = pl.pallas_call(
        middle_kernel,
        grid=(share // block,),
        in_specs=[pl.BlockSpec((8, wide), lambda g: (0, 0)), by_row(wide, chans, rows=block)]
        + [full(w.shape) for w in late],
        out_specs=[by_row(chans, wide, rows=block), by_row(wide, rows=block)]
        + [full(shape) for shape, _ in late_shapes],
        out_shape=shapes(((share, chans, wide), F32), ((share, wide), F32), *late_shapes),
        cost_estimate=cost(20 * share * cell, 3 * share * wide * width * 2),
        name="middle",
        compiler_params=pltpu.CompilerParams(vmem_limit_bytes=VMEM_BYTES),
    )(tgt, zr, *map(stay, late))

    results = pl.pallas_call(
        functools.partial(backward_kernel, tiles=tiles, chunks=chunks, **layout),
        grid=(share // block,),
        in_specs=[by_row(count // 2, 2 * NB, rows=block)] * (tiles * chunks)
        + [
            by_row(wide, rows=block),
            by_row(wide, H * wide, rows=block),
            by_row(width, wide, rows=block),
            by_row(NB, wide, rows=block),
        ]
        + [by_row(wide, width, rows=block)] * 4
        + [full(w.shape) for w in (w_output, wd3, wall, cst)],
        out_specs=[by_row(chans, wide, rows=block)] * 2 + [full((H, share, wide))] * tiles,
        out_shape=shapes(*([((share, chans, wide), F32)] * 2), *([((H, share, wide), BF)] * tiles)),
        scratch_shapes=[
            pltpu.VMEM((H, wide, wide), F32),
            pltpu.VMEM((block, width, wide), BF),
            pltpu.VMEM((4 * width, block * wide), BF),
            pltpu.VMEM((block * wide, 2 * NB), F32),
            pltpu.VMEM((tiles, H * share, wide), F32),
        ],
        cost_estimate=cost(500 * share * cell, 20 * share * wide * width * 2),
        name="backward",
        compiler_params=pltpu.CompilerParams(vmem_limit_bytes=VMEM_BYTES),
    )(
        *[part for parts_c in mirrored for part in parts_c],
        tgt, at, ot, ut, gt, vn, kt, qt, w_output, wd3, wall, cst,
    )
    dpt, dzn = results[:2]
    rdb = [to_partner(results[2 + k], k) for k in range(tiles)]

    base = pl.pallas_call(
        main_kernel,
        grid=(share // block,),
        in_specs=[by_row(chans, wide, rows=block)] * 3
        + [by_row(wide, rows=block), full(lgc.shape)],
        out_specs=by_row(chans, wide, rows=block),
        out_shape=jax.ShapeDtypeStruct((share, chans, wide), F32),
        cost_estimate=cost(20 * share * cell, 8 * share * wide * width * 2),
        name="main",
        compiler_params=pltpu.CompilerParams(vmem_limit_bytes=VMEM_BYTES),
    )(dpt, dzn, nrm, inv, lgc)

    block = FIN_ROWS if share % FIN_ROWS == 0 else 1
    outgoing = pl.pallas_call(
        functools.partial(finish_kernel, tiles=tiles),
        grid_spec=pltpu.PrefetchScalarGridSpec(
            num_scalar_prefetch=1,
            grid=(share // block,),
            in_specs=[
                *([full(rdb[0].shape)] * tiles),
                by_row(chans, wide, rows=block),
                by_row(chans, wide, rows=block),
                by_row(wide, rows=block),
                full(wgs.shape),
            ],
            out_specs=pl.BlockSpec((states, block, piece, chans), lambda g, _: (0, g, 0, 0)),
            scratch_shapes=[pltpu.VMEM((H * share, wide), F32)],
        ),
        out_shape=jax.ShapeDtypeStruct((states, share, piece, chans), BF),
        name="finish",
        compiler_params=pltpu.CompilerParams(vmem_limit_bytes=VMEM_BYTES),
    )(offsets, *rdb, base, nrm, inv, wgs)

    if even:
        slots = outgoing.reshape(states * tiles, group_rows, piece, chans)
    else:
        slots = lax.dynamic_update_slice(
            jnp.zeros((states, tiles, owner_rows, piece, chans), BF),
            outgoing.reshape(states, grid_side, owner_rows, piece, chans),
            (0, tile_j * grid_side, 0, 0, 0),
        ).reshape(states * tiles, owner_rows, piece, chans)
    received = lax.all_to_all(slots, ("state", "tile"), split_axis=0, concat_axis=0, tiled=True)
    if even:
        received = received.reshape(states, grid_side, owner_rows, piece, chans)
    else:
        received = lax.dynamic_index_in_dim(
            received.reshape(states, grid_side, grid_side, owner_rows, piece, chans),
            tile_i,
            2,
            keepdims=False,
        )

    block = 4 if owner_rows % 4 == 0 else 1
    out_shape = (2 * grid_side, owner_rows, 2, piece, chans)
    placed = pl.pallas_call(
        functools.partial(place_kernel, side=side),
        grid_spec=pltpu.PrefetchScalarGridSpec(
            num_scalar_prefetch=1,
            grid=(owner_rows // block,),
            in_specs=[
                pl.BlockSpec(
                    (states, grid_side, block, piece, chans), lambda g, _: (0, 0, g, 0, 0)
                )
            ],
            out_specs=pl.BlockSpec(
                (2 * grid_side, block, 2, piece, chans), lambda g, _: (0, g, 0, 0, 0)
            ),
        ),
        out_shape=jax.ShapeDtypeStruct(out_shape, F32),
        name="place",
        compiler_params=pltpu.CompilerParams(vmem_limit_bytes=VMEM_BYTES),
    )(offsets, received)
    return placed.reshape(2 * grid_side, 1, owner_rows, 2, piece, chans)


def solution(mesh):
    in_specs = (
        P("state", "tile", None, None, None),
        P("state", "tile", None, None, None),
    ) + (P(),) * 13
    out_specs = P(None, "tile", None, None, "state", None)
    return jax.shard_map(
        on_device, mesh=mesh, in_specs=in_specs, out_specs=out_specs, check_vma=False
    )
```

```python
import functools
import math

import jax
import jax.numpy as jnp
from jax import lax
from jax.experimental import pallas as pl
from jax.experimental.pallas import tpu as pltpu
from jax.sharding import PartitionSpec as P

VMEM_BYTES = 16 << 20
H = 4
HD = 32
NB = 64
FWD_PACE = (8, 1, 0)
BWD_PACE = (4, 1, 0)
PROJ_PACE = (2, 0, 3)
FIN_PACE = (8, 1, 0)
MID_PACE = (8, 1, 0)
EPS = 1e-5
BLOCK = 8
LOG2E = 1.0 / math.log(2.0)
BF = jnp.bfloat16
F32 = jnp.float32
HIGHEST = lax.Precision.HIGHEST


def nn(left, right, **kw):
    return lax.dot_general(left, right, (((1,), (0,)), ((), ())), preferred_element_type=F32, **kw)


def nt(left, right, **kw):
    return lax.dot_general(left, right, (((1,), (1,)), ((), ())), preferred_element_type=F32, **kw)


def split(value):
    high = value.astype(BF)
    low = (value - high.astype(F32)).astype(BF)
    return high, low


def transposed(value):
    return value.astype(F32).T.astype(value.dtype)


def column(row, lanes):
    return jnp.broadcast_to(row, (lanes, row.shape[1])).T


def eye(size):
    rows = lax.broadcasted_iota(jnp.int32, (size, size), 0)
    cols = lax.broadcasted_iota(jnp.int32, (size, size), 1)
    return jnp.where(rows == cols, 1.0, 0.0).astype(BF)


def rows_norm(pair_rows):
    mean = jnp.mean(pair_rows, axis=-1, keepdims=True)
    center = pair_rows - mean
    inverse = lax.rsqrt(jnp.mean(center * center, axis=-1, keepdims=True) + EPS)
    return center * inverse


def interleave(rows, pace):
    size, inner, outer = pace
    begin = {row: (r % size) * inner + (r // size) * outer for r, row in enumerate(rows)}
    tick = 0
    while begin:
        for row in list(begin):
            if begin[row] <= tick:
                try:
                    next(row)
                except StopIteration:
                    del begin[row]
        tick += 1


def blocks_of(refs, block):
    return [ref.at[pl.ds(pl.multiple_of(block * BLOCK, BLOCK), BLOCK)] for ref in refs]


def loop_blocks(rows, body):
    def one(block, carry):
        body(block)
        return carry

    lax.fori_loop(0, rows // BLOCK, one, 0)


def full(shape):
    return pl.BlockSpec(shape, lambda *_: (0,) * len(shape))


def prep_kernel(wq, wk, wv, wg, wo, gb, wd, w4t, w2, wod, wdt, gbc):
    w4t[...] = jnp.concatenate([transposed(w[...]) for w in (wq, wk, wv, wg)], axis=0)
    w2[...] = jnp.concatenate([wk[...], wv[...]], axis=1)
    wdt[...] = jnp.concatenate(split(wd[...]), axis=0)
    both = nt(wd[...], wo[...].astype(F32), precision=HIGHEST)
    wod[...] = jnp.concatenate(split(both), axis=0)
    gbc[...] = column(gb[...], gbc.shape[1])


def middle_kernel(after, zr, wq, wk, wv, wg, ob, wd, db, wpb, lng, nrm, inv, wd3, wall, lgc, cst, wgs):
    del after
    rows, wide, chans = zr.shape
    wall[...] = jnp.concatenate([wq[...], wk[...], wv[...], wg[...]], axis=1)
    dist_hi, dist_lo = split(wd[...].T)
    wd3[...] = jnp.concatenate([dist_hi, dist_hi, dist_lo], axis=1)
    lgc[...] = column(lng[...], wide)
    shift = 2.0 * jnp.sum(wd[...] * ob[...], axis=1, keepdims=True)
    cst[...] = column(db[...], wide) + shift
    proj = wpb[...] * lng[...]
    proj = jnp.concatenate([proj, jnp.zeros((wide - H, chans), F32)], axis=0).T[:, :H]
    proj_hi, proj_lo = split(proj)
    wgs[...] = jnp.concatenate([proj_hi, proj_hi, proj_lo, jnp.zeros_like(proj_lo)], axis=1)

    ident = eye(chans)

    def one_block(step):
        zr_b, nrm_b, inv_b = blocks_of((zr, nrm, inv), step)

        def one_row(row):
            pair_t = nt(ident, zr_b[row])
            yield
            center = pair_t - jnp.mean(pair_t, axis=0, keepdims=True)
            yield
            inverse = lax.rsqrt(jnp.mean(center * center, axis=0, keepdims=True) + EPS)
            inv_b[row : row + 1, :] = inverse
            nrm_b[row] = center * inverse
            yield

        interleave([one_row(row) for row in range(BLOCK)], MID_PACE)

    loop_blocks(rows, one_block)


def main_kernel(dpt, dzn, nrm, inv, lgc, base):
    def one_block(step):
        dpt_b, dzn_b, nrm_b, inv_b, base_b = blocks_of((dpt, dzn, nrm, inv, base), step)

        def one_row(row):
            scaled = dzn_b[row] * lgc[...]
            mean_a = jnp.mean(scaled, axis=0, keepdims=True)
            mean_b = jnp.mean(scaled * nrm_b[row], axis=0, keepdims=True)
            yield
            base_b[row] = dpt_b[row] + inv_b[row : row + 1, :] * (
                scaled - mean_a - nrm_b[row] * mean_b
            )
            yield

        interleave([one_row(row) for row in range(BLOCK)], MID_PACE)

    loop_blocks(dzn.shape[0], one_block)


def bias_kernel(tile, targets, lng, lnb, wpb, out, *, per_head):
    step = pl.program_id(0)
    fold, lines, side, chans = tile.shape
    pieces = [tile[f, q] for q in range(lines) for f in range(fold)]
    pair = jnp.concatenate(pieces, axis=0)
    proj = wpb[...] * lng[...]
    high, rest = split(proj)
    mid = rest
    last = (proj - high.astype(F32) - mid.astype(F32)).astype(BF)
    left = jnp.concatenate(
        [high.astype(F32), mid.astype(F32), last.astype(F32), jnp.ones((H, chans), F32)], axis=0
    ).astype(BF)
    left = jnp.concatenate([eye(chans), left], axis=0)
    total = jnp.sum(proj, axis=1, keepdims=True)
    const = jnp.sum(wpb[...] * lnb[...], axis=1, keepdims=True)
    size = fold * side
    rows_out = []
    for q in range(lines):
        up = nt(left, pair[q * size : (q + 1) * size])
        extra = up[chans:]
        mean = extra[3 * H : 3 * H + 1] * (1.0 / chans)
        center = up[:chans] - mean
        inverse = lax.rsqrt(jnp.mean(center * center, axis=0, keepdims=True) + EPS)
        dotted = extra[:H] + extra[H : 2 * H] + extra[2 * H : 3 * H]
        rows_out.append(inverse * (dotted - mean * total) + const)
    bias = jnp.concatenate(rows_out, axis=1)
    width = fold * side
    for q in range(lines):
        for h in range(H):
            out[pl.ds(h * per_head + step * lines + q, 1), :] = bias[
                h : h + 1, q * width : (q + 1) * width
            ]

    @pl.when(step == 0)
    def _():
        count = targets.shape[0]
        out[pl.ds(H * per_head, count), :] = targets[...].astype(F32)


def project_kernel(own_ref, *refs, parts):
    own = own_ref[0]
    part_refs = refs[:parts]
    lng, lnb, w4t, w2, gbc, zr, qt, kt, vt, kn, vn, gt, flat_s = refs[parts:]
    loop_blocks(
        zr.shape[0],
        lambda step: project_block(
            own,
            [part_refs[0].at[step]] + blocks_of(part_refs[1:], step),
            (lng, lnb, w4t, w2, gbc, flat_s),
            blocks_of((zr, qt, kt, vt, kn, vn, gt), step),
        ),
    )


def project_block(own, part_refs, weights, outs):
    lng, lnb, w4t, w2, gbc, flat_s = weights
    zr, qt, kt, vt, kn, vn, gt = outs
    parts = len(part_refs)
    rows, side, _ = part_refs[0].shape
    wide = zr.shape[1]
    width = H * HD
    for row in range(rows):
        for k in range(parts):
            block = lax.rem(own + parts - k, parts)
            zr[row, pl.ds(pl.multiple_of(block * side, side), side), :] = part_refs[k][row]

    def one_row(row):
        pair_row = zr[row].astype(F32)
        center = pair_row - jnp.mean(pair_row, axis=-1, keepdims=True)
        yield
        inverse = lax.rsqrt(jnp.mean(center * center, axis=-1, keepdims=True) + EPS)
        yield
        flat_s[row * wide : (row + 1) * wide, :] = (
            center * inverse * lng[...] + lnb[...]
        ).astype(BF)
        yield

    def one_pair(first):
        both = one_row(first), one_row(first + 1)
        for _ in range(3):
            for row in both:
                next(row)
            yield
        flat = flat_s[first * wide : (first + 2) * wide, :]
        for k, out in enumerate((qt, kt, vt)):
            up = nt(w4t[k * width : (k + 1) * width], flat)
            for n in range(2):
                out[first + n] = up[:, n * wide : (n + 1) * wide].astype(BF)
            yield
        up = nt(w4t[3 * width :], flat)
        for n in range(2):
            gt[first + n] = jax.nn.sigmoid(up[:, n * wide : (n + 1) * wide] + gbc[...])
            yield
        down = nn(flat, w2[...])
        for n in range(2):
            kn[first + n] = down[n * wide : (n + 1) * wide, :width].astype(BF)
            vn[first + n] = down[n * wide : (n + 1) * wide, width:].astype(BF)
        yield

    interleave([one_pair(row) for row in range(0, rows, 2)], PROJ_PACE)


def head_block(part, h):
    lanes = part.shape[1]
    pieces = []
    if h:
        pieces.append(jnp.zeros((h * HD, lanes), part.dtype))
    pieces.append(part)
    if h < H - 1:
        pieces.append(jnp.zeros(((H - 1 - h) * HD, lanes), part.dtype))
    return jnp.concatenate(pieces, axis=0)


def head_blocks(packed):
    return jnp.concatenate(
        [head_block(packed[h * HD : (h + 1) * HD], h) for h in range(H)], axis=1
    )


def forward_kernel(
    *refs, tiles, base, count, bias_rows, owner_rows, extra, grid_side, groups, group_rows
):
    gath = refs[:tiles]
    kn, qt, vt, gt, zr, wod, wdt = refs[tiles : tiles + 7]
    at, ot, ut, tgt, bias_t = refs[tiles + 7 + extra : tiles + 12 + extra]
    sends = refs[tiles + 12 + extra : 2 * tiles + 12 + extra]
    order, stage = refs[2 * tiles + 12 + extra :]
    mine = lax.axis_index("tile")
    tile_i = mine // grid_side
    tile_j = lax.rem(mine, grid_side)
    wide = kn.shape[1]
    side = wide // grid_side
    per_head = side * side // wide
    share = groups * group_rows
    span = side // groups

    for k in range(tiles):
        order[mine ^ k] = gath[k][...]
    lane = lax.broadcasted_iota(jnp.int32, (per_head, wide), 1) // side
    for h in range(H):
        pieces = []
        for i in range(grid_side):
            for f in range(grid_side):
                total = None
                for j in range(grid_side):
                    part = order[i * grid_side + j, h * per_head : (h + 1) * per_head, :]
                    turn = ((j - f) * side) % wide
                    if turn:
                        part = pltpu.roll(part, turn, 1)
                    total = part if total is None else jnp.where(lane == j, part, total)
                pieces.append(total)
        bias_t[h] = jnp.concatenate(pieces, axis=0).T * LOG2E

    whole = (kn, qt, vt, gt, zr, at, ot, ut, tgt)

    def one_block(step):
        rows = BLOCK
        kn, qt, vt, gt, zr, at, ot, ut, tgt = blocks_of(whole, step)
        for row in range(rows):
            within = (base + step) * span + tile_j * group_rows + row
            tgt[row : row + 1, :] = order[
                within // owner_rows,
                pl.ds(bias_rows + lax.rem(within, owner_rows) * grid_side + tile_i, 1),
                :,
            ]

        scale = LOG2E / math.sqrt(HD)

        def one_row(row):
            blocks = head_blocks(qt[row])
            outs = []
            for pair in range(0, H, 2):
                scores = nn(kn[row], blocks[:, pair * wide : (pair + 2) * wide])
                yield
                for h in range(pair, pair + 2):
                    part = scores[:, (h - pair) * wide : (h - pair + 1) * wide] * scale + bias_t[h]
                    peak = jnp.max(part, axis=0, keepdims=True)
                    yield
                    part = jnp.exp2(part - peak)
                    total = jnp.sum(part, axis=0, keepdims=True)
                    yield
                    part_b = (part * (1.0 / total)).astype(BF)
                    at[row, :, h * wide : (h + 1) * wide] = part_b
                    yield
                    outs.append(nn(vt[row, h * HD : (h + 1) * HD, :], part_b))
                    ot[row, h * HD : (h + 1) * HD, :] = outs[-1]
                    yield
            gated = (gt[row] * ot[row]).astype(BF)
            yield
            both = nn(wod[...], gated) + nt(wdt[...], zr[row])
            yield
            logit = both[:NB] + both[NB:]
            ut[row] = logit
            logit = logit - jnp.max(logit, axis=0, keepdims=True)
            yield
            packed = jnp.concatenate([logit, logit], axis=0).T
            here = step * rows + row
            yield
            for i in range(grid_side):
                for p in range(groups):
                    for j in range(grid_side):
                        source = ((i * groups + p) * grid_side + j) * group_rows
                        target = ((i * grid_side + j) * share + p * group_rows) * count
                        stage[pl.ds(target + here, group_rows, stride=count), :] = packed[
                            source : source + group_rows
                        ]
                    yield

        interleave([one_row(row) for row in range(rows)], FWD_PACE)

    loop_blocks(count, one_block)

    left = lax.broadcasted_iota(jnp.int32, (count // 2, 2 * NB), 1) < NB
    for k in range(tiles):
        start = (mine ^ k) * (share * count)
        for r in range(share):
            both = stage[pl.ds(pl.multiple_of(start + r * count, 8), count), :]
            sends[k][r] = jnp.where(left, both[: count // 2], both[count // 2 :]).astype(BF)


def backward_kernel(*refs, tiles, chunks, grid_side, groups, group_rows):
    rcv = refs[: tiles * chunks]
    tgt, at, ot, ut, gt, vn, kt, qt, wo, wd3, wall, cst, dpt, dzn = refs[
        tiles * chunks : tiles * chunks + 14
    ]
    sends = refs[tiles * chunks + 14 : tiles * chunks + 14 + tiles]
    acc, grad_s, back_s, mirror_s, order = refs[tiles * chunks + 14 + tiles :]
    width = H * HD
    mine = lax.axis_index("tile")
    wide = vn.shape[1]
    chunk_groups = groups // chunks
    share = groups * group_rows
    inv_root = 1.0 / math.sqrt(HD)
    adder = jnp.concatenate([eye(NB)] * 2, axis=1)
    bins = lax.broadcasted_iota(jnp.int32, (NB, 2 * wide), 0).astype(F32)

    acc[...] = jnp.zeros_like(acc)

    shift = jnp.concatenate([cst[...]] * 2, axis=1)
    left = lax.broadcasted_iota(jnp.int32, (rcv[0].shape[1], 2 * NB), 1) < NB

    whole = (tgt, at, ot, ut, gt, vn, kt, qt, dpt, dzn) + tuple(rcv)

    def one_block(step):
        rows = BLOCK
        tgt, at, ot, ut, gt, vn, kt, qt, dpt, dzn, *rcv = blocks_of(whole, step)

        def one_pair(first):
            pair = (first, first + 1)
            for row in pair:
                for k in range(tiles):
                    source_i = (mine ^ k) // grid_side
                    source_j = lax.rem(mine ^ k, grid_side)
                    for c in range(chunks):
                        part = rcv[c * tiles + k][row].astype(F32)
                        part = jnp.concatenate(
                            [jnp.where(left, part, 0.0), jnp.where(left, 0.0, part)], axis=0
                        )
                        for p in range(chunk_groups):
                            start = (
                                (source_i * groups + c * chunk_groups + p) * grid_side + source_j
                            ) * group_rows + row * wide
                            mirror_s[pl.ds(pl.multiple_of(start, group_rows), group_rows), :] = part[
                                p * group_rows : (p + 1) * group_rows
                            ]
            yield
            other = nt(adder, mirror_s[first * wide : (first + 2) * wide, :].astype(BF))
            yield
            logits = jnp.concatenate([ut[row] for row in pair], axis=1) + other + shift
            peak = jnp.max(logits, axis=0, keepdims=True)
            yield
            probs = jnp.exp(logits - peak)
            total = jnp.sum(probs, axis=0, keepdims=True)
            yield
            target = jnp.concatenate([tgt[row : row + 1, :] for row in pair], axis=1)
            resid = 2.0 * (probs * (1.0 / total) - jnp.where(bins == target, 1.0, 0.0))
            res_hi, res_lo = split(resid)
            yield
            pair_grad = nn(wd3[...], jnp.concatenate([res_hi, res_lo, res_hi], axis=0))
            for n, row in enumerate(pair):
                dpt[row] = pair_grad[:, n * wide : (n + 1) * wide]
            yield
            out_grad = nn(wo[...], pair_grad.astype(BF))
            yield
            for n, row in enumerate(pair):
                gate = gt[row]
                gated = out_grad[:, n * wide : (n + 1) * wide] * gate
                grad_s[row] = gated.astype(BF)
                back_s[3 * width :, row * wide : (row + 1) * wide] = (
                    gated * ot[row] * (1.0 - gate)
                ).astype(BF)
                yield

            def heads(row):
                lanes = slice(row * wide, (row + 1) * wide)
                for h in range(H):
                    part = slice(h * HD, (h + 1) * HD)
                    back_s[2 * width + h * HD : 2 * width + (h + 1) * HD, lanes] = nt(
                        grad_s[row, part, :], at[row, :, h * wide : (h + 1) * wide]
                    ).astype(BF)
                    yield
                    weight_grad = nn(vn[row], head_block(grad_s[row, part, :], h))
                    yield
                    prob = at[row, :, h * wide : (h + 1) * wide].astype(F32)
                    prod = prob * weight_grad
                    total = jnp.sum(prod, axis=0, keepdims=True)
                    yield
                    prod = prod - prob * total
                    prod_b = prod.astype(BF)
                    acc[h] += prod
                    yield
                    back_s[h * HD : (h + 1) * HD, lanes] = (nn(kt[row, part, :], prod_b) * inv_root).astype(BF)
                    back_s[width + h * HD : width + (h + 1) * HD, lanes] = (
                        nt(qt[row, part, :], prod_b) * inv_root
                    ).astype(BF)
                    yield

            both = [heads(row) for row in pair]
            while both:
                for row in list(both):
                    try:
                        next(row)
                    except StopIteration:
                        both.remove(row)
                yield
            normed_grad = nn(wall[...], back_s[:, first * wide : (first + 2) * wide])
            for n, row in enumerate(pair):
                dzn[row] = normed_grad[:, n * wide : (n + 1) * wide]
            yield

        interleave([one_pair(row) for row in range(0, rows, 2)], BWD_PACE)

    loop_blocks(share, one_block)

    for h in range(H):
        grad = acc[h].T
        for i in range(grid_side):
            for j in range(grid_side):
                pieces = []
                for p in range(groups):
                    source = ((i * groups + p) * grid_side + j) * group_rows
                    pieces.append(grad[source : source + group_rows])
                order[i * grid_side + j, h * share : (h + 1) * share, :] = jnp.concatenate(
                    pieces, axis=0
                )
    for k in range(tiles):
        sends[k][...] = order[mine ^ k].reshape(H, share, wide).astype(BF)


def finish_kernel(offsets, *refs, tiles):
    rdb = refs[:tiles]
    base, nrm, inv, wgs, out, sums = refs[tiles:]
    share, chans, wide = base.shape
    states, _, piece, _ = out.shape
    total_rows = rdb[0].shape[1]
    turn = offsets[lax.axis_index("state")] // piece

    for h in range(H):
        total = rdb[0][h].astype(F32)
        for part in rdb[1:]:
            total = total + part[h].astype(F32)
        sums[pl.ds(h * total_rows, total_rows), :] = total

    def one_block(step):
        base_b, nrm_b, inv_b = blocks_of((base, nrm, inv), step)

        def one_row(row):
            local = step * BLOCK + row
            parts = [sums[pl.ds(h * total_rows + local, 1), :] for h in range(H)]
            high, low = split(jnp.concatenate(parts, axis=0))
            high, low = high.astype(F32), low.astype(F32)
            spread = jnp.concatenate([high, low, high, jnp.zeros((H, wide), F32)], axis=0)
            yield
            scaled = nn(wgs[...], spread.astype(BF))
            yield
            mean_a = jnp.mean(scaled, axis=0, keepdims=True)
            mean_b = jnp.mean(scaled * nrm_b[row], axis=0, keepdims=True)
            yield
            total = base_b[row] + inv_b[row : row + 1, :] * (scaled - mean_a - nrm_b[row] * mean_b)
            yield
            total = total.T.astype(BF)
            for c in range(wide // piece):
                out[lax.rem(turn + c, states), local] = total[c * piece : (c + 1) * piece]
            yield

        interleave([one_row(row) for row in range(BLOCK)], FIN_PACE)

    loop_blocks(share, one_block)


def place_kernel(offsets, rcv, out, *, side):
    states, grid_side, rows, piece, chans = rcv.shape
    start = lax.axis_index("state") * piece
    out[...] = jnp.zeros_like(out)
    for s in range(states):
        offset = offsets[s]
        half = (start < offset).astype(jnp.int32)
        base = offset // side
        for i in range(grid_side):
            out[base + i, :, half] += rcv[s, i].astype(F32)


def on_device(
    pair_tiles,
    targets,
    offsets,
    ln_gain,
    ln_bias,
    w_query,
    w_key,
    w_value,
    w_pairbias,
    w_gate,
    gate_bias,
    w_output,
    out_bias,
    w_distogram,
    dist_bias,
):
    tiles = lax.axis_size("tile")
    states = lax.axis_size("state")
    side, chans = pair_tiles.shape[3], pair_tiles.shape[4]
    wide = targets.shape[4]
    grid_side = wide // side
    owner_rows = side // tiles
    width = H * HD
    here = lax.axis_index("tile")
    tile_i = here // grid_side
    tile_j = lax.rem(here, grid_side)
    even = owner_rows % grid_side == 0
    groups = tiles if even else 1
    group_rows = side // groups // grid_side
    share = groups * group_rows
    per_head = side * side // wide
    piece = wide // states

    def stay(value):
        return pltpu.with_memory_space_constraint(value, pltpu.HBM)

    def shapes(*pairs):
        return [jax.ShapeDtypeStruct(s, t) for s, t in pairs]

    tile = pair_tiles.reshape(groups, grid_side, group_rows, side, chans)

    def rows_of(j):
        return lax.dynamic_index_in_dim(tile, j, 1, keepdims=False).reshape(share, side, chans)

    parts = [tile]
    for k in range(1, grid_side):
        perm = [
            (i * grid_side + j, i * grid_side + (j + k) % grid_side)
            for i in range(grid_side)
            for j in range(grid_side)
        ]
        parts.append(lax.ppermute(rows_of(lax.rem(tile_j + k, grid_side)), "tile", perm))

    gain_row = ln_gain.reshape(1, chans)
    shift_row = ln_bias.reshape(1, chans)
    prep_shapes = shapes(
        ((4 * width, chans), BF),
        ((chans, 2 * width), BF),
        ((2 * NB, width), BF),
        ((2 * NB, chans), BF),
        ((width, wide), F32),
    )
    w4t, w2, wod, wdt, gbc = pl.pallas_call(
        prep_kernel,
        out_shape=prep_shapes,
        name="prep",
        compiler_params=pltpu.CompilerParams(vmem_limit_bytes=VMEM_BYTES),
    )(
        *map(
            stay,
            (
                w_query,
                w_key,
                w_value,
                w_gate,
                w_output,
                gate_bias.reshape(1, width),
                w_distogram.T,
            ),
        )
    )

    lines = per_head
    bias_rows = H * per_head
    target_rows = owner_rows * grid_side
    bias_mine = pl.pallas_call(
        functools.partial(bias_kernel, per_head=per_head),
        grid=(per_head // lines,),
        in_specs=[
            pl.BlockSpec((grid_side, lines, side, chans), lambda g: (0, g, 0, 0)),
            full((target_rows, wide)),
            full((1, chans)),
            full((1, chans)),
            full((H, chans)),
        ],
        out_specs=full((bias_rows + target_rows, wide)),
        out_shape=jax.ShapeDtypeStruct((bias_rows + target_rows, wide), F32),
        name="bias",
        compiler_params=pltpu.CompilerParams(vmem_limit_bytes=VMEM_BYTES),
    )(
        *map(
            stay,
            (
                pair_tiles.reshape(grid_side, per_head, side, chans),
                targets.reshape(target_rows, wide),
                gain_row,
                shift_row,
                w_pairbias.T,
            ),
        )
    )

    def to_partner(value, k):
        return lax.ppermute(value, "tile", [(t, t ^ k) for t in range(tiles)]) if k else value

    gathered = [to_partner(bias_mine, k) for k in range(tiles)]

    def by_row(*shape, rows, base=0):
        return pl.BlockSpec((rows,) + shape, lambda g, *_: (g + base,) + (0,) * len(shape))

    def cost(flops, moved):
        return pl.CostEstimate(flops=flops, bytes_accessed=moved, transcendentals=0)

    cell = wide * width * wide
    square_b = ((share, wide, width), BF)
    zr, qt, kt, vt, kn, vn, gt = pl.pallas_call(
        functools.partial(project_kernel, parts=grid_side),
        grid_spec=pltpu.PrefetchScalarGridSpec(
            num_scalar_prefetch=1,
            grid=(1,),
            in_specs=[
                pl.BlockSpec(
                    (groups, None, group_rows, side, chans), lambda g, own: (0, own[0], 0, 0, 0)
                )
            ]
            + [by_row(side, chans, rows=share)] * (grid_side - 1)
            + [full((1, chans)), full((1, chans)), full(w4t.shape), full(w2.shape), full(gbc.shape)],
            out_specs=[by_row(wide, width, rows=share)] * 7,
            scratch_shapes=[pltpu.VMEM((group_rows * wide, chans), BF)],
        ),
        out_shape=shapes(*([square_b] * 6), ((share, width, wide), F32)),
        cost_estimate=cost(80 * share * cell, 12 * share * wide * width * 2),
        name="project",
        compiler_params=pltpu.CompilerParams(vmem_limit_bytes=VMEM_BYTES),
    )(tile_j.reshape(1), *parts, gain_row, shift_row, w4t, w2, gbc)

    chunks = 2 if groups % 2 == 0 else 1
    chunk_groups = groups // chunks
    count = share // chunks
    layout = dict(grid_side=grid_side, groups=groups, group_rows=group_rows)
    saved_shapes = shapes(
        ((share, wide, H * wide), BF),
        ((share, width, wide), F32),
        ((share, NB, wide), F32),
        ((share, wide), F32),
        ((H, wide, wide), F32),
    )
    packed_shape = (share, count // 2, 2 * NB)
    saved = []
    mirrored = []
    for c in range(chunks):
        base = c * chunk_groups
        inputs = [*gathered, kn, qt, vt, gt, zr, wod, wdt]
        first = len(inputs)
        call = pl.pallas_call(
            functools.partial(
                forward_kernel,
                tiles=tiles,
                base=base,
                count=count,
                bias_rows=bias_rows,
                owner_rows=owner_rows,
                extra=len(saved),
                **layout,
            ),
            grid=(1,),
            in_specs=[full(gathered[0].shape)] * tiles
            + [by_row(wide, width, rows=count, base=c)] * 5
            + [full(wod.shape), full(wdt.shape)]
            + [pl.BlockSpec(memory_space=pl.ANY)] * len(saved),
            out_specs=[
                by_row(wide, H * wide, rows=count, base=c),
                by_row(width, wide, rows=count, base=c),
                by_row(NB, wide, rows=count, base=c),
                by_row(wide, rows=count, base=c),
                full((H, wide, wide)),
            ]
            + [full(packed_shape)] * tiles,
            out_shape=saved_shapes + shapes(*([(packed_shape, BF)] * tiles)),
            scratch_shapes=[
                pltpu.VMEM((tiles,) + gathered[0].shape, F32),
                pltpu.VMEM((tiles * share * count, 2 * NB), F32),
            ],
            input_output_aliases={first + n: n for n in range(len(saved))},
            cost_estimate=cost(150 * count * cell, 14 * count * wide * width * 2),
            name="forward",
        compiler_params=pltpu.CompilerParams(vmem_limit_bytes=VMEM_BYTES),
        )
        results = call(*inputs, *saved)
        saved = list(results[:4])
        mirrored.append([to_partner(results[5 + k], k) for k in range(tiles)])
    at, ot, ut, tgt = saved

    late = (
        w_query,
        w_key,
        w_value,
        w_gate,
        out_bias.reshape(1, chans),
        w_distogram.T,
        dist_bias.reshape(1, NB),
        w_pairbias.T,
        gain_row,
    )
    late_shapes = (
        ((chans, 3 * NB), BF),
        ((chans, 4 * width), BF),
        ((chans, wide), F32),
        ((NB, wide), F32),
        ((chans, 4 * H), BF),
    )
    nrm, inv, wd3, wall, lgc, cst, wgs = pl.pallas_call(
        middle_kernel,
        grid=(1,),
        in_specs=[pl.BlockSpec((8, wide), lambda g: (0, 0)), by_row(wide, chans, rows=share)]
        + [full(w.shape) for w in late],
        out_specs=[by_row(chans, wide, rows=share), by_row(wide, rows=share)]
        + [full(shape) for shape, _ in late_shapes],
        out_shape=shapes(((share, chans, wide), F32), ((share, wide), F32), *late_shapes),
        cost_estimate=cost(20 * share * cell, 3 * share * wide * width * 2),
        name="middle",
        compiler_params=pltpu.CompilerParams(vmem_limit_bytes=VMEM_BYTES),
    )(tgt, zr, *map(stay, late))

    results = pl.pallas_call(
        functools.partial(backward_kernel, tiles=tiles, chunks=chunks, **layout),
        grid=(1,),
        in_specs=[by_row(count // 2, 2 * NB, rows=share)] * (tiles * chunks)
        + [
            by_row(wide, rows=share),
            by_row(wide, H * wide, rows=share),
            by_row(width, wide, rows=share),
            by_row(NB, wide, rows=share),
        ]
        + [by_row(wide, width, rows=share)] * 4
        + [full(w.shape) for w in (w_output, wd3, wall, cst)],
        out_specs=[by_row(chans, wide, rows=share)] * 2 + [full((H, share, wide))] * tiles,
        out_shape=shapes(*([((share, chans, wide), F32)] * 2), *([((H, share, wide), BF)] * tiles)),
        scratch_shapes=[
            pltpu.VMEM((H, wide, wide), F32),
            pltpu.VMEM((BLOCK, width, wide), BF),
            pltpu.VMEM((4 * width, BLOCK * wide), BF),
            pltpu.VMEM((BLOCK * wide, 2 * NB), F32),
            pltpu.VMEM((tiles, H * share, wide), F32),
        ],
        cost_estimate=cost(500 * share * cell, 20 * share * wide * width * 2),
        name="backward",
        compiler_params=pltpu.CompilerParams(vmem_limit_bytes=VMEM_BYTES),
    )(
        *[part for parts_c in mirrored for part in parts_c],
        tgt, at, ot, ut, gt, vn, kt, qt, w_output, wd3, wall, cst,
    )
    dpt, dzn = results[:2]
    rdb = [to_partner(results[2 + k], k) for k in range(tiles)]

    base = pl.pallas_call(
        main_kernel,
        grid=(1,),
        in_specs=[by_row(chans, wide, rows=share)] * 3
        + [by_row(wide, rows=share), full(lgc.shape)],
        out_specs=by_row(chans, wide, rows=share),
        out_shape=jax.ShapeDtypeStruct((share, chans, wide), F32),
        cost_estimate=cost(20 * share * cell, 8 * share * wide * width * 2),
        name="main",
        compiler_params=pltpu.CompilerParams(vmem_limit_bytes=VMEM_BYTES),
    )(dpt, dzn, nrm, inv, lgc)

    outgoing = pl.pallas_call(
        functools.partial(finish_kernel, tiles=tiles),
        grid_spec=pltpu.PrefetchScalarGridSpec(
            num_scalar_prefetch=1,
            grid=(1,),
            in_specs=[
                *([full(rdb[0].shape)] * tiles),
                by_row(chans, wide, rows=share),
                by_row(chans, wide, rows=share),
                by_row(wide, rows=share),
                full(wgs.shape),
            ],
            out_specs=pl.BlockSpec((states, share, piece, chans), lambda g, _: (0, g, 0, 0)),
            scratch_shapes=[pltpu.VMEM((H * share, wide), F32)],
        ),
        out_shape=jax.ShapeDtypeStruct((states, share, piece, chans), BF),
        name="finish",
        compiler_params=pltpu.CompilerParams(vmem_limit_bytes=VMEM_BYTES),
    )(offsets, *rdb, base, nrm, inv, wgs)

    if even:
        slots = outgoing.reshape(states * tiles, group_rows, piece, chans)
    else:
        slots = lax.dynamic_update_slice(
            jnp.zeros((states, tiles, owner_rows, piece, chans), BF),
            outgoing.reshape(states, grid_side, owner_rows, piece, chans),
            (0, tile_j * grid_side, 0, 0, 0),
        ).reshape(states * tiles, owner_rows, piece, chans)
    received = lax.all_to_all(slots, ("state", "tile"), split_axis=0, concat_axis=0, tiled=True)
    if even:
        received = received.reshape(states, grid_side, owner_rows, piece, chans)
    else:
        received = lax.dynamic_index_in_dim(
            received.reshape(states, grid_side, grid_side, owner_rows, piece, chans),
            tile_i,
            2,
            keepdims=False,
        )

    block = owner_rows
    out_shape = (2 * grid_side, owner_rows, 2, piece, chans)
    placed = pl.pallas_call(
        functools.partial(place_kernel, side=side),
        grid_spec=pltpu.PrefetchScalarGridSpec(
            num_scalar_prefetch=1,
            grid=(owner_rows // block,),
            in_specs=[
                pl.BlockSpec(
                    (states, grid_side, block, piece, chans), lambda g, _: (0, 0, g, 0, 0)
                )
            ],
            out_specs=pl.BlockSpec(
                (2 * grid_side, block, 2, piece, chans), lambda g, _: (0, g, 0, 0, 0)
            ),
        ),
        out_shape=jax.ShapeDtypeStruct(out_shape, F32),
        name="place",
        compiler_params=pltpu.CompilerParams(vmem_limit_bytes=VMEM_BYTES),
    )(offsets, received)
    return placed.reshape(2 * grid_side, 1, owner_rows, 2, piece, chans)


def solution(mesh):
    in_specs = (
        P("state", "tile", None, None, None),
        P("state", "tile", None, None, None),
    ) + (P(),) * 13
    out_specs = P(None, "tile", None, None, "state", None)
    return jax.shard_map(
        on_device, mesh=mesh, in_specs=in_specs, out_specs=out_specs, check_vma=False
    )
```

```python
import functools
import math

import jax
import jax.numpy as jnp
from jax import lax
from jax.experimental import pallas as pl
from jax.experimental.pallas import tpu as pltpu
from jax.sharding import PartitionSpec as P

VMEM_BYTES = 16 << 20
H = 4
HD = 32
NB = 64
FWD_PACE = (8, 1, 0)
BWD_PACE = (4, 1, 0)
PROJ_PACE = (2, 0, 3)
FIN_PACE = (8, 1, 0)
MID_PACE = (8, 1, 0)
EPS = 1e-5
BLOCK = 8
LOG2E = 1.0 / math.log(2.0)
BF = jnp.bfloat16
F32 = jnp.float32
HIGHEST = lax.Precision.HIGHEST


def nn(left, right, **kw):
    return lax.dot_general(left, right, (((1,), (0,)), ((), ())), preferred_element_type=F32, **kw)


def nt(left, right, **kw):
    return lax.dot_general(left, right, (((1,), (1,)), ((), ())), preferred_element_type=F32, **kw)


def split(value):
    high = value.astype(BF)
    low = (value - high.astype(F32)).astype(BF)
    return high, low


def transposed(value):
    return value.astype(F32).T.astype(value.dtype)


def column(row, lanes):
    return jnp.broadcast_to(row, (lanes, row.shape[1])).T


def eye(size):
    rows = lax.broadcasted_iota(jnp.int32, (size, size), 0)
    cols = lax.broadcasted_iota(jnp.int32, (size, size), 1)
    return jnp.where(rows == cols, 1.0, 0.0).astype(BF)


def rows_norm(pair_rows):
    mean = jnp.mean(pair_rows, axis=-1, keepdims=True)
    center = pair_rows - mean
    inverse = lax.rsqrt(jnp.mean(center * center, axis=-1, keepdims=True) + EPS)
    return center * inverse


def interleave(rows, pace):
    size, inner, outer = pace
    begin = {row: (r % size) * inner + (r // size) * outer for r, row in enumerate(rows)}
    tick = 0
    while begin:
        for row in list(begin):
            if begin[row] <= tick:
                try:
                    next(row)
                except StopIteration:
                    del begin[row]
        tick += 1


def blocks_of(refs, block):
    return [ref.at[pl.ds(pl.multiple_of(block * BLOCK, BLOCK), BLOCK)] for ref in refs]


def loop_blocks(rows, body):
    def one(block, carry):
        body(block)
        return carry

    lax.fori_loop(0, rows // BLOCK, one, 0)


def full(shape):
    return pl.BlockSpec(shape, lambda *_: (0,) * len(shape))


def prep_kernel(wq, wk, wv, wg, wo, gb, wd, w4t, w2, wod, wdt, gbc):
    w4t[...] = jnp.concatenate([transposed(w[...]) for w in (wq, wk, wv, wg)], axis=0)
    w2[...] = jnp.concatenate([wk[...], wv[...]], axis=1)
    wdt[...] = jnp.concatenate(split(wd[...]), axis=0)
    both = nt(wd[...], wo[...].astype(F32), precision=HIGHEST)
    wod[...] = jnp.concatenate(split(both), axis=0)
    gbc[...] = column(gb[...], gbc.shape[1])


def middle_kernel(after, zr, wq, wk, wv, wg, ob, wd, db, wpb, lng, nrm, inv, wd3, wall, lgc, cst, wgs):
    del after
    rows, wide, chans = zr.shape
    wall[...] = jnp.concatenate([wq[...], wk[...], wv[...], wg[...]], axis=1)
    dist_hi, dist_lo = split(wd[...].T)
    wd3[...] = jnp.concatenate([dist_hi, dist_hi, dist_lo], axis=1)
    lgc[...] = column(lng[...], wide)
    shift = 2.0 * jnp.sum(wd[...] * ob[...], axis=1, keepdims=True)
    cst[...] = column(db[...], wide) + shift
    proj = wpb[...] * lng[...]
    proj = jnp.concatenate([proj, jnp.zeros((wide - H, chans), F32)], axis=0).T[:, :H]
    proj_hi, proj_lo = split(proj)
    wgs[...] = jnp.concatenate([proj_hi, proj_hi, proj_lo, jnp.zeros_like(proj_lo)], axis=1)

    ident = eye(chans)

    def one_block(step):
        zr_b, nrm_b, inv_b = blocks_of((zr, nrm, inv), step)

        def one_row(row):
            pair_t = nt(ident, zr_b[row])
            yield
            center = pair_t - jnp.mean(pair_t, axis=0, keepdims=True)
            yield
            inverse = lax.rsqrt(jnp.mean(center * center, axis=0, keepdims=True) + EPS)
            inv_b[row : row + 1, :] = inverse
            nrm_b[row] = center * inverse
            yield

        interleave([one_row(row) for row in range(BLOCK)], MID_PACE)

    loop_blocks(rows, one_block)


def main_kernel(dpt, dzn, nrm, inv, lgc, base):
    def one_block(step):
        dpt_b, dzn_b, nrm_b, inv_b, base_b = blocks_of((dpt, dzn, nrm, inv, base), step)

        def one_row(row):
            scaled = dzn_b[row] * lgc[...]
            mean_a = jnp.mean(scaled, axis=0, keepdims=True)
            mean_b = jnp.mean(scaled * nrm_b[row], axis=0, keepdims=True)
            yield
            base_b[row] = dpt_b[row] + inv_b[row : row + 1, :] * (
                scaled - mean_a - nrm_b[row] * mean_b
            )
            yield

        interleave([one_row(row) for row in range(BLOCK)], MID_PACE)

    loop_blocks(dzn.shape[0], one_block)


def bias_kernel(own_ref, tile, targets, lng, lnb, wpb, out, gain, shift, *sends, per_head, groups):
    step = pl.program_id(0)
    parts = len(sends)
    runs = per_head // BLOCK
    gain[...] = lng[...]
    shift[...] = lnb[...]
    for k in range(parts):
        owner = lax.rem(own_ref[0] + k, parts)
        for p in range(groups):
            run = p * parts + owner
            first = pl.multiple_of(lax.rem(run, runs) * BLOCK, BLOCK)
            sends[k][p * BLOCK : (p + 1) * BLOCK] = tile[run // runs, pl.ds(first, BLOCK)]
    fold, lines, side, chans = tile.shape
    pieces = [tile[f, q] for q in range(lines) for f in range(fold)]
    pair = jnp.concatenate(pieces, axis=0)
    proj = wpb[...] * lng[...]
    high, rest = split(proj)
    mid = rest
    last = (proj - high.astype(F32) - mid.astype(F32)).astype(BF)
    left = jnp.concatenate(
        [high.astype(F32), mid.astype(F32), last.astype(F32), jnp.ones((H, chans), F32)], axis=0
    ).astype(BF)
    left = jnp.concatenate([eye(chans), left], axis=0)
    total = jnp.sum(proj, axis=1, keepdims=True)
    const = jnp.sum(wpb[...] * lnb[...], axis=1, keepdims=True)
    size = fold * side
    rows_out = []
    for q in range(lines):
        up = nt(left, pair[q * size : (q + 1) * size])
        extra = up[chans:]
        mean = extra[3 * H : 3 * H + 1] * (1.0 / chans)
        center = up[:chans] - mean
        inverse = lax.rsqrt(jnp.mean(center * center, axis=0, keepdims=True) + EPS)
        dotted = extra[:H] + extra[H : 2 * H] + extra[2 * H : 3 * H]
        rows_out.append(inverse * (dotted - mean * total) + const)
    bias = jnp.concatenate(rows_out, axis=1)
    width = fold * side
    for q in range(lines):
        for h in range(H):
            out[pl.ds(h * per_head + step * lines + q, 1), :] = bias[
                h : h + 1, q * width : (q + 1) * width
            ]

    @pl.when(step == 0)
    def _():
        count = targets.shape[0]
        out[pl.ds(H * per_head, count), :] = targets[...].astype(F32)


def project_kernel(own_ref, *refs, parts):
    own = own_ref[0]
    part_refs = refs[:parts]
    lng, lnb, w4t, w2, gbc, zr, qt, kt, vt, kn, vn, gt, flat_s = refs[parts:]
    loop_blocks(
        zr.shape[0],
        lambda step: project_block(
            own,
            blocks_of(part_refs, step),
            (lng, lnb, w4t, w2, gbc, flat_s),
            blocks_of((zr, qt, kt, vt, kn, vn, gt), step),
        ),
    )


def project_block(own, part_refs, weights, outs):
    lng, lnb, w4t, w2, gbc, flat_s = weights
    zr, qt, kt, vt, kn, vn, gt = outs
    parts = len(part_refs)
    rows, side, _ = part_refs[0].shape
    wide = zr.shape[1]
    width = H * HD
    for row in range(rows):
        for k in range(parts):
            block = lax.rem(own + parts - k, parts)
            zr[row, pl.ds(pl.multiple_of(block * side, side), side), :] = part_refs[k][row]

    def one_row(row):
        pair_row = zr[row].astype(F32)
        center = pair_row - jnp.mean(pair_row, axis=-1, keepdims=True)
        yield
        inverse = lax.rsqrt(jnp.mean(center * center, axis=-1, keepdims=True) + EPS)
        yield
        flat_s[row * wide : (row + 1) * wide, :] = (
            center * inverse * lng[...] + lnb[...]
        ).astype(BF)
        yield

    def one_pair(first):
        both = one_row(first), one_row(first + 1)
        for _ in range(3):
            for row in both:
                next(row)
            yield
        flat = flat_s[first * wide : (first + 2) * wide, :]
        for k, out in enumerate((qt, kt, vt)):
            up = nt(w4t[k * width : (k + 1) * width], flat)
            for n in range(2):
                out[first + n] = up[:, n * wide : (n + 1) * wide].astype(BF)
            yield
        up = nt(w4t[3 * width :], flat)
        for n in range(2):
            gt[first + n] = jax.nn.sigmoid(up[:, n * wide : (n + 1) * wide] + gbc[...])
            yield
        down = nn(flat, w2[...])
        for n in range(2):
            kn[first + n] = down[n * wide : (n + 1) * wide, :width].astype(BF)
            vn[first + n] = down[n * wide : (n + 1) * wide, width:].astype(BF)
        yield

    interleave([one_pair(row) for row in range(0, rows, 2)], PROJ_PACE)


def head_block(part, h):
    lanes = part.shape[1]
    pieces = []
    if h:
        pieces.append(jnp.zeros((h * HD, lanes), part.dtype))
    pieces.append(part)
    if h < H - 1:
        pieces.append(jnp.zeros(((H - 1 - h) * HD, lanes), part.dtype))
    return jnp.concatenate(pieces, axis=0)


def head_blocks(packed):
    return jnp.concatenate(
        [head_block(packed[h * HD : (h + 1) * HD], h) for h in range(H)], axis=1
    )


def forward_kernel(
    *refs, tiles, base, count, bias_rows, owner_rows, extra, grid_side, groups, group_rows
):
    gath = refs[:tiles]
    kn, qt, vt, gt, zr, wod, wdt = refs[tiles : tiles + 7]
    at, ot, ut, tgt, bias_t = refs[tiles + 7 + extra : tiles + 12 + extra]
    sends = refs[tiles + 12 + extra : 2 * tiles + 12 + extra]
    order, stage = refs[2 * tiles + 12 + extra :]
    mine = lax.axis_index("tile")
    tile_i = mine // grid_side
    tile_j = lax.rem(mine, grid_side)
    wide = kn.shape[1]
    side = wide // grid_side
    per_head = side * side // wide
    share = groups * group_rows
    span = side // groups

    for k in range(tiles):
        order[mine ^ k] = gath[k][...]
    lane = lax.broadcasted_iota(jnp.int32, (per_head, wide), 1) // side
    for h in range(H):
        pieces = []
        for i in range(grid_side):
            for f in range(grid_side):
                total = None
                for j in range(grid_side):
                    part = order[i * grid_side + j, h * per_head : (h + 1) * per_head, :]
                    turn = ((j - f) * side) % wide
                    if turn:
                        part = pltpu.roll(part, turn, 1)
                    total = part if total is None else jnp.where(lane == j, part, total)
                pieces.append(total)
        bias_t[h] = jnp.concatenate(pieces, axis=0).T * LOG2E

    whole = (kn, qt, vt, gt, zr, at, ot, ut, tgt)

    def one_block(step):
        rows = BLOCK
        kn, qt, vt, gt, zr, at, ot, ut, tgt = blocks_of(whole, step)
        for row in range(rows):
            within = (base + step) * span + tile_j * group_rows + row
            tgt[row : row + 1, :] = order[
                within // owner_rows,
                pl.ds(bias_rows + lax.rem(within, owner_rows) * grid_side + tile_i, 1),
                :,
            ]

        scale = LOG2E / math.sqrt(HD)

        def one_row(row):
            blocks = head_blocks(qt[row])
            outs = []
            for pair in range(0, H, 2):
                scores = nn(kn[row], blocks[:, pair * wide : (pair + 2) * wide])
                yield
                for h in range(pair, pair + 2):
                    part = scores[:, (h - pair) * wide : (h - pair + 1) * wide] * scale + bias_t[h]
                    peak = jnp.max(part, axis=0, keepdims=True)
                    yield
                    part = jnp.exp2(part - peak)
                    total = jnp.sum(part, axis=0, keepdims=True)
                    yield
                    part_b = (part * (1.0 / total)).astype(BF)
                    at[row, :, h * wide : (h + 1) * wide] = part_b
                    yield
                    outs.append(nn(vt[row, h * HD : (h + 1) * HD, :], part_b))
                    ot[row, h * HD : (h + 1) * HD, :] = outs[-1]
                    yield
            gated = (gt[row] * ot[row]).astype(BF)
            yield
            both = nn(wod[...], gated) + nt(wdt[...], zr[row])
            yield
            logit = both[:NB] + both[NB:]
            ut[row] = logit
            logit = logit - jnp.max(logit, axis=0, keepdims=True)
            yield
            packed = jnp.concatenate([logit, logit], axis=0).T
            here = step * rows + row
            yield
            for i in range(grid_side):
                for p in range(groups):
                    for j in range(grid_side):
                        source = ((i * groups + p) * grid_side + j) * group_rows
                        target = ((i * grid_side + j) * share + p * group_rows) * count
                        stage[pl.ds(target + here, group_rows, stride=count), :] = packed[
                            source : source + group_rows
                        ]
                    yield

        interleave([one_row(row) for row in range(rows)], FWD_PACE)

    loop_blocks(count, one_block)

    left = lax.broadcasted_iota(jnp.int32, (count // 2, 2 * NB), 1) < NB
    for k in range(tiles):
        start = (mine ^ k) * (share * count)
        for r in range(share):
            both = stage[pl.ds(pl.multiple_of(start + r * count, 8), count), :]
            sends[k][r] = jnp.where(left, both[: count // 2], both[count // 2 :]).astype(BF)


def backward_kernel(*refs, tiles, chunks, grid_side, groups, group_rows):
    rcv = refs[: tiles * chunks]
    tgt, at, ot, ut, gt, vn, kt, qt, wo, wd3, wall, cst, dpt, dzn = refs[
        tiles * chunks : tiles * chunks + 14
    ]
    sends = refs[tiles * chunks + 14 : tiles * chunks + 14 + tiles]
    acc, grad_s, back_s, mirror_s, order = refs[tiles * chunks + 14 + tiles :]
    width = H * HD
    mine = lax.axis_index("tile")
    wide = vn.shape[1]
    chunk_groups = groups // chunks
    share = groups * group_rows
    inv_root = 1.0 / math.sqrt(HD)
    adder = jnp.concatenate([eye(NB)] * 2, axis=1)
    bins = lax.broadcasted_iota(jnp.int32, (NB, 2 * wide), 0).astype(F32)

    acc[...] = jnp.zeros_like(acc)

    shift = jnp.concatenate([cst[...]] * 2, axis=1)
    left = lax.broadcasted_iota(jnp.int32, (rcv[0].shape[1], 2 * NB), 1) < NB

    whole = (tgt, at, ot, ut, gt, vn, kt, qt, dpt, dzn) + tuple(rcv)

    def one_block(step):
        rows = BLOCK
        tgt, at, ot, ut, gt, vn, kt, qt, dpt, dzn, *rcv = blocks_of(whole, step)

        def one_pair(first):
            pair = (first, first + 1)
            for row in pair:
                for k in range(tiles):
                    source_i = (mine ^ k) // grid_side
                    source_j = lax.rem(mine ^ k, grid_side)
                    for c in range(chunks):
                        part = rcv[c * tiles + k][row].astype(F32)
                        part = jnp.concatenate(
                            [jnp.where(left, part, 0.0), jnp.where(left, 0.0, part)], axis=0
                        )
                        for p in range(chunk_groups):
                            start = (
                                (source_i * groups + c * chunk_groups + p) * grid_side + source_j
                            ) * group_rows + row * wide
                            mirror_s[pl.ds(pl.multiple_of(start, group_rows), group_rows), :] = part[
                                p * group_rows : (p + 1) * group_rows
                            ]
            yield
            other = nt(adder, mirror_s[first * wide : (first + 2) * wide, :].astype(BF))
            yield
            logits = jnp.concatenate([ut[row] for row in pair], axis=1) + other + shift
            peak = jnp.max(logits, axis=0, keepdims=True)
            yield
            probs = jnp.exp(logits - peak)
            total = jnp.sum(probs, axis=0, keepdims=True)
            yield
            target = jnp.concatenate([tgt[row : row + 1, :] for row in pair], axis=1)
            resid = 2.0 * (probs * (1.0 / total) - jnp.where(bins == target, 1.0, 0.0))
            res_hi, res_lo = split(resid)
            yield
            pair_grad = nn(wd3[...], jnp.concatenate([res_hi, res_lo, res_hi], axis=0))
            for n, row in enumerate(pair):
                dpt[row] = pair_grad[:, n * wide : (n + 1) * wide]
            yield
            out_grad = nn(wo[...], pair_grad.astype(BF))
            yield
            for n, row in enumerate(pair):
                gate = gt[row]
                gated = out_grad[:, n * wide : (n + 1) * wide] * gate
                grad_s[row] = gated.astype(BF)
                back_s[3 * width :, row * wide : (row + 1) * wide] = (
                    gated * ot[row] * (1.0 - gate)
                ).astype(BF)
                yield

            def heads(row):
                lanes = slice(row * wide, (row + 1) * wide)
                for h in range(H):
                    part = slice(h * HD, (h + 1) * HD)
                    back_s[2 * width + h * HD : 2 * width + (h + 1) * HD, lanes] = nt(
                        grad_s[row, part, :], at[row, :, h * wide : (h + 1) * wide]
                    ).astype(BF)
                    yield
                    weight_grad = nn(vn[row], head_block(grad_s[row, part, :], h))
                    yield
                    prob = at[row, :, h * wide : (h + 1) * wide].astype(F32)
                    prod = prob * weight_grad
                    total = jnp.sum(prod, axis=0, keepdims=True)
                    yield
                    prod = prod - prob * total
                    prod_b = prod.astype(BF)
                    acc[h] += prod
                    yield
                    back_s[h * HD : (h + 1) * HD, lanes] = (nn(kt[row, part, :], prod_b) * inv_root).astype(BF)
                    back_s[width + h * HD : width + (h + 1) * HD, lanes] = (
                        nt(qt[row, part, :], prod_b) * inv_root
                    ).astype(BF)
                    yield

            both = [heads(row) for row in pair]
            while both:
                for row in list(both):
                    try:
                        next(row)
                    except StopIteration:
                        both.remove(row)
                yield
            normed_grad = nn(wall[...], back_s[:, first * wide : (first + 2) * wide])
            for n, row in enumerate(pair):
                dzn[row] = normed_grad[:, n * wide : (n + 1) * wide]
            yield

        interleave([one_pair(row) for row in range(0, rows, 2)], BWD_PACE)

    loop_blocks(share, one_block)

    for h in range(H):
        grad = acc[h].T
        for i in range(grid_side):
            for j in range(grid_side):
                pieces = []
                for p in range(groups):
                    source = ((i * groups + p) * grid_side + j) * group_rows
                    pieces.append(grad[source : source + group_rows])
                order[i * grid_side + j, h * share : (h + 1) * share, :] = jnp.concatenate(
                    pieces, axis=0
                )
    for k in range(tiles):
        sends[k][...] = order[mine ^ k].reshape(H, share, wide).astype(BF)


def finish_kernel(offsets, *refs, tiles):
    rdb = refs[:tiles]
    base, nrm, inv, wgs, out, sums = refs[tiles:]
    share, chans, wide = base.shape
    states, _, piece, _ = out.shape
    total_rows = rdb[0].shape[1]
    turn = offsets[lax.axis_index("state")] // piece

    for h in range(H):
        total = rdb[0][h].astype(F32)
        for part in rdb[1:]:
            total = total + part[h].astype(F32)
        sums[pl.ds(h * total_rows, total_rows), :] = total

    def one_block(step):
        base_b, nrm_b, inv_b = blocks_of((base, nrm, inv), step)

        def one_row(row):
            local = step * BLOCK + row
            parts = [sums[pl.ds(h * total_rows + local, 1), :] for h in range(H)]
            high, low = split(jnp.concatenate(parts, axis=0))
            high, low = high.astype(F32), low.astype(F32)
            spread = jnp.concatenate([high, low, high, jnp.zeros((H, wide), F32)], axis=0)
            yield
            scaled = nn(wgs[...], spread.astype(BF))
            yield
            mean_a = jnp.mean(scaled, axis=0, keepdims=True)
            mean_b = jnp.mean(scaled * nrm_b[row], axis=0, keepdims=True)
            yield
            total = base_b[row] + inv_b[row : row + 1, :] * (scaled - mean_a - nrm_b[row] * mean_b)
            yield
            total = total.T.astype(BF)
            for c in range(wide // piece):
                out[lax.rem(turn + c, states), local] = total[c * piece : (c + 1) * piece]
            yield

        interleave([one_row(row) for row in range(BLOCK)], FIN_PACE)

    loop_blocks(share, one_block)


def place_kernel(offsets, rcv, out, *, side):
    states, grid_side, rows, piece, chans = rcv.shape
    start = lax.axis_index("state") * piece
    out[...] = jnp.zeros_like(out)
    for s in range(states):
        offset = offsets[s]
        half = (start < offset).astype(jnp.int32)
        base = offset // side
        for i in range(grid_side):
            out[base + i, :, half] += rcv[s, i].astype(F32)


def on_device(
    pair_tiles,
    targets,
    offsets,
    ln_gain,
    ln_bias,
    w_query,
    w_key,
    w_value,
    w_pairbias,
    w_gate,
    gate_bias,
    w_output,
    out_bias,
    w_distogram,
    dist_bias,
):
    tiles = lax.axis_size("tile")
    states = lax.axis_size("state")
    side, chans = pair_tiles.shape[3], pair_tiles.shape[4]
    wide = targets.shape[4]
    grid_side = wide // side
    owner_rows = side // tiles
    width = H * HD
    here = lax.axis_index("tile")
    tile_i = here // grid_side
    tile_j = lax.rem(here, grid_side)
    even = owner_rows % grid_side == 0
    groups = tiles if even else 1
    group_rows = side // groups // grid_side
    share = groups * group_rows
    per_head = side * side // wide
    piece = wide // states

    def stay(value):
        return pltpu.with_memory_space_constraint(value, pltpu.HBM)

    def shapes(*pairs):
        return [jax.ShapeDtypeStruct(s, t) for s, t in pairs]

    own = tile_j.reshape(1)
    gain_row = ln_gain.reshape(1, chans)
    shift_row = ln_bias.reshape(1, chans)
    prep_shapes = shapes(
        ((4 * width, chans), BF),
        ((chans, 2 * width), BF),
        ((2 * NB, width), BF),
        ((2 * NB, chans), BF),
        ((width, wide), F32),
    )
    w4t, w2, wod, wdt, gbc = pl.pallas_call(
        prep_kernel,
        out_shape=prep_shapes,
        name="prep",
        compiler_params=pltpu.CompilerParams(vmem_limit_bytes=VMEM_BYTES),
    )(
        *map(
            stay,
            (
                w_query,
                w_key,
                w_value,
                w_gate,
                w_output,
                gate_bias.reshape(1, width),
                w_distogram.T,
            ),
        )
    )

    bias_rows = H * per_head
    target_rows = owner_rows * grid_side
    bias_mine, gain_near, shift_near, *outgoing_rows = pl.pallas_call(
        functools.partial(bias_kernel, per_head=per_head, groups=groups),
        grid_spec=pltpu.PrefetchScalarGridSpec(
            num_scalar_prefetch=1,
            grid=(1,),
            in_specs=[
                full((grid_side, per_head, side, chans)),
                full((target_rows, wide)),
                full((1, chans)),
                full((1, chans)),
                full((H, chans)),
            ],
            out_specs=[full((bias_rows + target_rows, wide))]
            + [full((1, chans))] * 2
            + [full((share, side, chans))] * grid_side,
        ),
        out_shape=shapes(
            ((bias_rows + target_rows, wide), F32),
            *([((1, chans), F32)] * 2),
            *([((share, side, chans), BF)] * grid_side),
        ),
        name="bias",
        compiler_params=pltpu.CompilerParams(vmem_limit_bytes=VMEM_BYTES),
    )(
        own,
        *map(
            stay,
            (
                pair_tiles.reshape(grid_side, per_head, side, chans),
                targets.reshape(target_rows, wide),
                gain_row,
                shift_row,
                w_pairbias.T,
            ),
        ),
    )
    parts = [outgoing_rows[0]]
    for k in range(1, grid_side):
        perm = [
            (i * grid_side + j, i * grid_side + (j + k) % grid_side)
            for i in range(grid_side)
            for j in range(grid_side)
        ]
        parts.append(lax.ppermute(outgoing_rows[k], "tile", perm))

    def to_partner(value, k):
        return lax.ppermute(value, "tile", [(t, t ^ k) for t in range(tiles)]) if k else value

    gathered = [to_partner(bias_mine, k) for k in range(tiles)]

    def by_row(*shape, rows, base=0):
        return pl.BlockSpec((rows,) + shape, lambda g, *_: (g + base,) + (0,) * len(shape))

    def cost(flops, moved):
        return pl.CostEstimate(flops=flops, bytes_accessed=moved, transcendentals=0)

    cell = wide * width * wide
    square_b = ((share, wide, width), BF)
    zr, qt, kt, vt, kn, vn, gt = pl.pallas_call(
        functools.partial(project_kernel, parts=grid_side),
        grid_spec=pltpu.PrefetchScalarGridSpec(
            num_scalar_prefetch=1,
            grid=(1,),
            in_specs=[by_row(side, chans, rows=share)] * grid_side
            + [full((1, chans)), full((1, chans)), full(w4t.shape), full(w2.shape), full(gbc.shape)],
            out_specs=[by_row(wide, width, rows=share)] * 7,
            scratch_shapes=[pltpu.VMEM((group_rows * wide, chans), BF)],
        ),
        out_shape=shapes(*([square_b] * 6), ((share, width, wide), F32)),
        cost_estimate=cost(80 * share * cell, 12 * share * wide * width * 2),
        name="project",
        compiler_params=pltpu.CompilerParams(vmem_limit_bytes=VMEM_BYTES),
    )(own, *parts, gain_near, shift_near, w4t, w2, gbc)

    chunks = 2 if groups % 2 == 0 else 1
    chunk_groups = groups // chunks
    count = share // chunks
    layout = dict(grid_side=grid_side, groups=groups, group_rows=group_rows)
    saved_shapes = shapes(
        ((share, wide, H * wide), BF),
        ((share, width, wide), F32),
        ((share, NB, wide), F32),
        ((share, wide), F32),
        ((H, wide, wide), F32),
    )
    packed_shape = (share, count // 2, 2 * NB)
    saved = []
    mirrored = []
    for c in range(chunks):
        base = c * chunk_groups
        inputs = [*gathered, kn, qt, vt, gt, zr, wod, wdt]
        first = len(inputs)
        call = pl.pallas_call(
            functools.partial(
                forward_kernel,
                tiles=tiles,
                base=base,
                count=count,
                bias_rows=bias_rows,
                owner_rows=owner_rows,
                extra=len(saved),
                **layout,
            ),
            grid=(1,),
            in_specs=[full(gathered[0].shape)] * tiles
            + [by_row(wide, width, rows=count, base=c)] * 5
            + [full(wod.shape), full(wdt.shape)]
            + [pl.BlockSpec(memory_space=pl.ANY)] * len(saved),
            out_specs=[
                by_row(wide, H * wide, rows=count, base=c),
                by_row(width, wide, rows=count, base=c),
                by_row(NB, wide, rows=count, base=c),
                by_row(wide, rows=count, base=c),
                full((H, wide, wide)),
            ]
            + [full(packed_shape)] * tiles,
            out_shape=saved_shapes + shapes(*([(packed_shape, BF)] * tiles)),
            scratch_shapes=[
                pltpu.VMEM((tiles,) + gathered[0].shape, F32),
                pltpu.VMEM((tiles * share * count, 2 * NB), F32),
            ],
            input_output_aliases={first + n: n for n in range(len(saved))},
            cost_estimate=cost(150 * count * cell, 14 * count * wide * width * 2),
            name="forward",
        compiler_params=pltpu.CompilerParams(vmem_limit_bytes=VMEM_BYTES),
        )
        results = call(*inputs, *saved)
        saved = list(results[:4])
        mirrored.append([to_partner(results[5 + k], k) for k in range(tiles)])
    at, ot, ut, tgt = saved

    late = (
        w_query,
        w_key,
        w_value,
        w_gate,
        out_bias.reshape(1, chans),
        w_distogram.T,
        dist_bias.reshape(1, NB),
        w_pairbias.T,
        gain_row,
    )
    late_shapes = (
        ((chans, 3 * NB), BF),
        ((chans, 4 * width), BF),
        ((chans, wide), F32),
        ((NB, wide), F32),
        ((chans, 4 * H), BF),
    )
    nrm, inv, wd3, wall, lgc, cst, wgs = pl.pallas_call(
        middle_kernel,
        grid=(1,),
        in_specs=[pl.BlockSpec((8, wide), lambda g: (0, 0)), by_row(wide, chans, rows=share)]
        + [full(w.shape) for w in late],
        out_specs=[by_row(chans, wide, rows=share), by_row(wide, rows=share)]
        + [full(shape) for shape, _ in late_shapes],
        out_shape=shapes(((share, chans, wide), F32), ((share, wide), F32), *late_shapes),
        cost_estimate=cost(20 * share * cell, 3 * share * wide * width * 2),
        name="middle",
        compiler_params=pltpu.CompilerParams(vmem_limit_bytes=VMEM_BYTES),
    )(tgt, zr, *map(stay, late))

    results = pl.pallas_call(
        functools.partial(backward_kernel, tiles=tiles, chunks=chunks, **layout),
        grid=(1,),
        in_specs=[by_row(count // 2, 2 * NB, rows=share)] * (tiles * chunks)
        + [
            by_row(wide, rows=share),
            by_row(wide, H * wide, rows=share),
            by_row(width, wide, rows=share),
            by_row(NB, wide, rows=share),
        ]
        + [by_row(wide, width, rows=share)] * 4
        + [full(w.shape) for w in (w_output, wd3, wall, cst)],
        out_specs=[by_row(chans, wide, rows=share)] * 2 + [full((H, share, wide))] * tiles,
        out_shape=shapes(*([((share, chans, wide), F32)] * 2), *([((H, share, wide), BF)] * tiles)),
        scratch_shapes=[
            pltpu.VMEM((H, wide, wide), F32),
            pltpu.VMEM((BLOCK, width, wide), BF),
            pltpu.VMEM((4 * width, BLOCK * wide), BF),
            pltpu.VMEM((BLOCK * wide, 2 * NB), F32),
            pltpu.VMEM((tiles, H * share, wide), F32),
        ],
        cost_estimate=cost(500 * share * cell, 20 * share * wide * width * 2),
        name="backward",
        compiler_params=pltpu.CompilerParams(vmem_limit_bytes=VMEM_BYTES),
    )(
        *[part for parts_c in mirrored for part in parts_c],
        tgt, at, ot, ut, gt, vn, kt, qt, w_output, wd3, wall, cst,
    )
    dpt, dzn = results[:2]
    rdb = [to_partner(results[2 + k], k) for k in range(tiles)]

    base = pl.pallas_call(
        main_kernel,
        grid=(1,),
        in_specs=[by_row(chans, wide, rows=share)] * 3
        + [by_row(wide, rows=share), full(lgc.shape)],
        out_specs=by_row(chans, wide, rows=share),
        out_shape=jax.ShapeDtypeStruct((share, chans, wide), F32),
        cost_estimate=cost(20 * share * cell, 8 * share * wide * width * 2),
        name="main",
        compiler_params=pltpu.CompilerParams(vmem_limit_bytes=VMEM_BYTES),
    )(dpt, dzn, nrm, inv, lgc)

    outgoing = pl.pallas_call(
        functools.partial(finish_kernel, tiles=tiles),
        grid_spec=pltpu.PrefetchScalarGridSpec(
            num_scalar_prefetch=1,
            grid=(1,),
            in_specs=[
                *([full(rdb[0].shape)] * tiles),
                by_row(chans, wide, rows=share),
                by_row(chans, wide, rows=share),
                by_row(wide, rows=share),
                full(wgs.shape),
            ],
            out_specs=pl.BlockSpec((states, share, piece, chans), lambda g, _: (0, g, 0, 0)),
            scratch_shapes=[pltpu.VMEM((H * share, wide), F32)],
        ),
        out_shape=jax.ShapeDtypeStruct((states, share, piece, chans), BF),
        name="finish",
        compiler_params=pltpu.CompilerParams(vmem_limit_bytes=VMEM_BYTES),
    )(offsets, *rdb, base, nrm, inv, wgs)

    if even:
        slots = outgoing.reshape(states * tiles, group_rows, piece, chans)
    else:
        slots = lax.dynamic_update_slice(
            jnp.zeros((states, tiles, owner_rows, piece, chans), BF),
            outgoing.reshape(states, grid_side, owner_rows, piece, chans),
            (0, tile_j * grid_side, 0, 0, 0),
        ).reshape(states * tiles, owner_rows, piece, chans)
    received = lax.all_to_all(slots, ("state", "tile"), split_axis=0, concat_axis=0, tiled=True)
    if even:
        received = received.reshape(states, grid_side, owner_rows, piece, chans)
    else:
        received = lax.dynamic_index_in_dim(
            received.reshape(states, grid_side, grid_side, owner_rows, piece, chans),
            tile_i,
            2,
            keepdims=False,
        )

    block = owner_rows
    out_shape = (2 * grid_side, owner_rows, 2, piece, chans)
    placed = pl.pallas_call(
        functools.partial(place_kernel, side=side),
        grid_spec=pltpu.PrefetchScalarGridSpec(
            num_scalar_prefetch=1,
            grid=(owner_rows // block,),
            in_specs=[
                pl.BlockSpec(
                    (states, grid_side, block, piece, chans), lambda g, _: (0, 0, g, 0, 0)
                )
            ],
            out_specs=pl.BlockSpec(
                (2 * grid_side, block, 2, piece, chans), lambda g, _: (0, g, 0, 0, 0)
            ),
        ),
        out_shape=jax.ShapeDtypeStruct(out_shape, F32),
        name="place",
        compiler_params=pltpu.CompilerParams(vmem_limit_bytes=VMEM_BYTES),
    )(offsets, received)
    return placed.reshape(2 * grid_side, 1, owner_rows, 2, piece, chans)


def solution(mesh):
    in_specs = (
        P("state", "tile", None, None, None),
        P("state", "tile", None, None, None),
    ) + (P(),) * 13
    out_specs = P(None, "tile", None, None, "state", None)
    return jax.shard_map(
        on_device, mesh=mesh, in_specs=in_specs, out_specs=out_specs, check_vma=False
    )
```

```python
import functools
import math

import jax
import jax.numpy as jnp
from jax import lax
from jax.experimental import pallas as pl
from jax.experimental.pallas import tpu as pltpu
from jax.sharding import PartitionSpec as P

VMEM_BYTES = 16 << 20
H = 4
HD = 32
NB = 64
FWD_PACE = (8, 1, 0)
BWD_PACE = (4, 1, 0)
PROJ_PACE = (2, 0, 3)
FIN_PACE = (8, 1, 0)
MID_PACE = (8, 1, 0)
EPS = 1e-5
BLOCK = 8
LOG2E = 1.0 / math.log(2.0)
BF = jnp.bfloat16
F32 = jnp.float32
HIGHEST = lax.Precision.HIGHEST


def nn(left, right, **kw):
    return lax.dot_general(left, right, (((1,), (0,)), ((), ())), preferred_element_type=F32, **kw)


def nt(left, right, **kw):
    return lax.dot_general(left, right, (((1,), (1,)), ((), ())), preferred_element_type=F32, **kw)


def split(value):
    high = value.astype(BF)
    low = (value - high.astype(F32)).astype(BF)
    return high, low


def transposed(value):
    return value.astype(F32).T.astype(value.dtype)


def column(row, lanes):
    return jnp.broadcast_to(row, (lanes, row.shape[1])).T


def eye(size):
    rows = lax.broadcasted_iota(jnp.int32, (size, size), 0)
    cols = lax.broadcasted_iota(jnp.int32, (size, size), 1)
    return jnp.where(rows == cols, 1.0, 0.0).astype(BF)


def rows_norm(pair_rows):
    mean = jnp.mean(pair_rows, axis=-1, keepdims=True)
    center = pair_rows - mean
    inverse = lax.rsqrt(jnp.mean(center * center, axis=-1, keepdims=True) + EPS)
    return center * inverse


def interleave(rows, pace):
    size, inner, outer = pace
    begin = {row: (r % size) * inner + (r // size) * outer for r, row in enumerate(rows)}
    tick = 0
    while begin:
        for row in list(begin):
            if begin[row] <= tick:
                try:
                    next(row)
                except StopIteration:
                    del begin[row]
        tick += 1


def blocks_of(refs, block):
    return [ref.at[pl.ds(pl.multiple_of(block * BLOCK, BLOCK), BLOCK)] for ref in refs]


def loop_blocks(rows, body):
    def one(block, carry):
        body(block)
        return carry

    lax.fori_loop(0, rows // BLOCK, one, 0)


def full(shape):
    return pl.BlockSpec(shape, lambda *_: (0,) * len(shape))


def prep_kernel(wq, wk, wv, wg, wo, gb, wd, w4t, w2, wod, wdt, gbc):
    w4t[...] = jnp.concatenate([transposed(w[...]) for w in (wq, wk, wv, wg)], axis=0)
    w2[...] = jnp.concatenate([wk[...], wv[...]], axis=1)
    wdt[...] = jnp.concatenate(split(wd[...]), axis=0)
    both = nt(wd[...], wo[...].astype(F32), precision=HIGHEST)
    wod[...] = jnp.concatenate(split(both), axis=0)
    gbc[...] = column(gb[...], gbc.shape[1])


def middle_kernel(after, zr, wq, wk, wv, wg, ob, wd, db, wpb, lng, nrm, inv, wd3, wall, lgc, cst, wgs):
    del after
    rows, wide, chans = zr.shape
    wall[...] = jnp.concatenate([wq[...], wk[...], wv[...], wg[...]], axis=1)
    dist_hi, dist_lo = split(wd[...].T)
    wd3[...] = jnp.concatenate([dist_hi, dist_hi, dist_lo], axis=1)
    lgc[...] = column(lng[...], wide)
    shift = 2.0 * jnp.sum(wd[...] * ob[...], axis=1, keepdims=True)
    cst[...] = column(db[...], wide) + shift
    proj = wpb[...] * lng[...]
    proj = jnp.concatenate([proj, jnp.zeros((wide - H, chans), F32)], axis=0).T[:, :H]
    proj_hi, proj_lo = split(proj)
    wgs[...] = jnp.concatenate([proj_hi, proj_hi, proj_lo, jnp.zeros_like(proj_lo)], axis=1)

    ident = eye(chans)

    def one_block(step):
        zr_b, nrm_b, inv_b = blocks_of((zr, nrm, inv), step)

        def one_row(row):
            pair_t = nt(ident, zr_b[row])
            yield
            center = pair_t - jnp.mean(pair_t, axis=0, keepdims=True)
            yield
            inverse = lax.rsqrt(jnp.mean(center * center, axis=0, keepdims=True) + EPS)
            inv_b[row : row + 1, :] = inverse
            nrm_b[row] = center * inverse
            yield

        interleave([one_row(row) for row in range(BLOCK)], MID_PACE)

    loop_blocks(rows, one_block)


def main_kernel(dpt, dzn, nrm, inv, lgc, base):
    def one_block(step):
        dpt_b, dzn_b, nrm_b, inv_b, base_b = blocks_of((dpt, dzn, nrm, inv, base), step)

        def one_row(row):
            scaled = dzn_b[row] * lgc[...]
            mean_a = jnp.mean(scaled, axis=0, keepdims=True)
            mean_b = jnp.mean(scaled * nrm_b[row], axis=0, keepdims=True)
            yield
            base_b[row] = dpt_b[row] + inv_b[row : row + 1, :] * (
                scaled - mean_a - nrm_b[row] * mean_b
            )
            yield

        interleave([one_row(row) for row in range(BLOCK)], MID_PACE)

    loop_blocks(dzn.shape[0], one_block)


def bias_kernel(own_ref, tile, targets, lng, lnb, wpb, out, gain, shift, *sends, per_head, groups):
    step = pl.program_id(0)
    parts = len(sends)
    runs = per_head // BLOCK
    gain[...] = lng[...]
    shift[...] = lnb[...]
    for k in range(parts):
        owner = lax.rem(own_ref[0] + k, parts)
        for p in range(groups):
            run = p * parts + owner
            first = pl.multiple_of(lax.rem(run, runs) * BLOCK, BLOCK)
            sends[k][p * BLOCK : (p + 1) * BLOCK] = tile[run // runs, pl.ds(first, BLOCK)]
    fold, lines, side, chans = tile.shape
    pieces = [tile[f, q] for q in range(lines) for f in range(fold)]
    pair = jnp.concatenate(pieces, axis=0)
    proj = wpb[...] * lng[...]
    high, rest = split(proj)
    mid = rest
    last = (proj - high.astype(F32) - mid.astype(F32)).astype(BF)
    left = jnp.concatenate(
        [high.astype(F32), mid.astype(F32), last.astype(F32), jnp.ones((H, chans), F32)], axis=0
    ).astype(BF)
    left = jnp.concatenate([eye(chans), left], axis=0)
    total = jnp.sum(proj, axis=1, keepdims=True)
    const = jnp.sum(wpb[...] * lnb[...], axis=1, keepdims=True)
    size = fold * side
    rows_out = []
    for q in range(lines):
        up = nt(left, pair[q * size : (q + 1) * size])
        extra = up[chans:]
        mean = extra[3 * H : 3 * H + 1] * (1.0 / chans)
        center = up[:chans] - mean
        inverse = lax.rsqrt(jnp.mean(center * center, axis=0, keepdims=True) + EPS)
        dotted = extra[:H] + extra[H : 2 * H] + extra[2 * H : 3 * H]
        rows_out.append(inverse * (dotted - mean * total) + const)
    bias = jnp.concatenate(rows_out, axis=1)
    width = fold * side
    for q in range(lines):
        for h in range(H):
            out[pl.ds(h * per_head + step * lines + q, 1), :] = bias[
                h : h + 1, q * width : (q + 1) * width
            ]

    @pl.when(step == 0)
    def _():
        count = targets.shape[0]
        out[pl.ds(H * per_head, count), :] = targets[...].astype(F32)


def project_kernel(own_ref, *refs, parts):
    own = own_ref[0]
    part_refs = refs[:parts]
    lng, lnb, w4t, w2, gbc, zr, qt, kt, vt, kn, vn, gt, flat_s = refs[parts:]
    loop_blocks(
        zr.shape[0],
        lambda step: project_block(
            own,
            blocks_of(part_refs, step),
            (lng, lnb, w4t, w2, gbc, flat_s),
            blocks_of((zr, qt, kt, vt, kn, vn, gt), step),
        ),
    )


def project_block(own, part_refs, weights, outs):
    lng, lnb, w4t, w2, gbc, flat_s = weights
    zr, qt, kt, vt, kn, vn, gt = outs
    parts = len(part_refs)
    rows, side, _ = part_refs[0].shape
    wide = zr.shape[1]
    width = H * HD
    for row in range(rows):
        for k in range(parts):
            block = lax.rem(own + parts - k, parts)
            zr[row, pl.ds(pl.multiple_of(block * side, side), side), :] = part_refs[k][row]

    def one_row(row):
        pair_row = zr[row].astype(F32)
        center = pair_row - jnp.mean(pair_row, axis=-1, keepdims=True)
        yield
        inverse = lax.rsqrt(jnp.mean(center * center, axis=-1, keepdims=True) + EPS)
        yield
        flat_s[row * wide : (row + 1) * wide, :] = (
            center * inverse * lng[...] + lnb[...]
        ).astype(BF)
        yield

    def one_pair(first):
        both = one_row(first), one_row(first + 1)
        for _ in range(3):
            for row in both:
                next(row)
            yield
        flat = flat_s[first * wide : (first + 2) * wide, :]
        for k, out in enumerate((qt, kt, vt)):
            up = nt(w4t[k * width : (k + 1) * width], flat)
            for n in range(2):
                out[first + n] = up[:, n * wide : (n + 1) * wide].astype(BF)
            yield
        up = nt(w4t[3 * width :], flat)
        for n in range(2):
            gt[first + n] = jax.nn.sigmoid(up[:, n * wide : (n + 1) * wide] + gbc[...])
            yield
        down = nn(flat, w2[...])
        for n in range(2):
            kn[first + n] = down[n * wide : (n + 1) * wide, :width].astype(BF)
            vn[first + n] = down[n * wide : (n + 1) * wide, width:].astype(BF)
        yield

    interleave([one_pair(row) for row in range(0, rows, 2)], PROJ_PACE)


def head_block(part, h):
    lanes = part.shape[1]
    pieces = []
    if h:
        pieces.append(jnp.zeros((h * HD, lanes), part.dtype))
    pieces.append(part)
    if h < H - 1:
        pieces.append(jnp.zeros(((H - 1 - h) * HD, lanes), part.dtype))
    return jnp.concatenate(pieces, axis=0)


def head_blocks(packed):
    return jnp.concatenate(
        [head_block(packed[h * HD : (h + 1) * HD], h) for h in range(H)], axis=1
    )


def forward_kernel(
    *refs, tiles, base, count, bias_rows, owner_rows, extra, grid_side, groups, group_rows
):
    gath = refs[:tiles]
    kn, qt, vt, gt, zr, wod, wdt = refs[tiles : tiles + 7]
    at, ot, ut, tgt, bias_t = refs[tiles + 7 + extra : tiles + 12 + extra]
    sends = refs[tiles + 12 + extra : 2 * tiles + 12 + extra]
    order, stage = refs[2 * tiles + 12 + extra :]
    mine = lax.axis_index("tile")
    tile_i = mine // grid_side
    tile_j = lax.rem(mine, grid_side)
    wide = kn.shape[1]
    side = wide // grid_side
    per_head = side * side // wide
    share = groups * group_rows
    span = side // groups

    for k in range(tiles):
        order[mine ^ k] = gath[k][...]
    lane = lax.broadcasted_iota(jnp.int32, (per_head, wide), 1) // side
    for h in range(H):
        pieces = []
        for i in range(grid_side):
            for f in range(grid_side):
                total = None
                for j in range(grid_side):
                    part = order[i * grid_side + j, h * per_head : (h + 1) * per_head, :]
                    turn = ((j - f) * side) % wide
                    if turn:
                        part = pltpu.roll(part, turn, 1)
                    total = part if total is None else jnp.where(lane == j, part, total)
                pieces.append(total)
        bias_t[h] = jnp.concatenate(pieces, axis=0).T * LOG2E

    whole = (kn, qt, vt, gt, zr, at, ot, ut, tgt)

    def one_block(step):
        rows = BLOCK
        kn, qt, vt, gt, zr, at, ot, ut, tgt = blocks_of(whole, step)
        for row in range(rows):
            within = (base + step) * span + tile_j * group_rows + row
            tgt[row : row + 1, :] = order[
                within // owner_rows,
                pl.ds(bias_rows + lax.rem(within, owner_rows) * grid_side + tile_i, 1),
                :,
            ]

        scale = LOG2E / math.sqrt(HD)

        def one_row(row):
            blocks = head_blocks(qt[row])
            outs = []
            for pair in range(0, H, 2):
                scores = nn(kn[row], blocks[:, pair * wide : (pair + 2) * wide])
                yield
                for h in range(pair, pair + 2):
                    part = scores[:, (h - pair) * wide : (h - pair + 1) * wide] * scale + bias_t[h]
                    peak = jnp.max(part, axis=0, keepdims=True)
                    yield
                    part = jnp.exp2(part - peak)
                    total = jnp.sum(part, axis=0, keepdims=True)
                    yield
                    part_b = (part * (1.0 / total)).astype(BF)
                    at[row, :, h * wide : (h + 1) * wide] = part_b
                    yield
                    outs.append(nn(vt[row, h * HD : (h + 1) * HD, :], part_b))
                    ot[row, h * HD : (h + 1) * HD, :] = outs[-1]
                    yield
            gated = (gt[row] * ot[row]).astype(BF)
            yield
            both = nn(wod[...], gated) + nt(wdt[...], zr[row])
            yield
            logit = both[:NB] + both[NB:]
            ut[row] = logit
            logit = logit - jnp.max(logit, axis=0, keepdims=True)
            yield
            packed = jnp.concatenate([logit, logit], axis=0).T
            here = step * rows + row
            yield
            for i in range(grid_side):
                for p in range(groups):
                    for j in range(grid_side):
                        source = ((i * groups + p) * grid_side + j) * group_rows
                        target = ((i * grid_side + j) * share + p * group_rows) * count
                        stage[pl.ds(target + here, group_rows, stride=count), :] = packed[
                            source : source + group_rows
                        ]
                    yield

        interleave([one_row(row) for row in range(rows)], FWD_PACE)

    loop_blocks(count, one_block)

    left = lax.broadcasted_iota(jnp.int32, (count // 2, 2 * NB), 1) < NB
    for k in range(tiles):
        start = (mine ^ k) * (share * count)
        for r in range(share):
            both = stage[pl.ds(pl.multiple_of(start + r * count, 8), count), :]
            sends[k][r] = jnp.where(left, both[: count // 2], both[count // 2 :]).astype(BF)


def backward_kernel(*refs, tiles, spans, grid_side, groups, group_rows):
    chunks = len(spans)
    rcv = refs[: tiles * chunks]
    tgt, at, ot, ut, gt, vn, kt, qt, wo, wd3, wall, cst, dpt, dzn = refs[
        tiles * chunks : tiles * chunks + 14
    ]
    sends = refs[tiles * chunks + 14 : tiles * chunks + 14 + tiles]
    acc, grad_s, back_s, mirror_s, order = refs[tiles * chunks + 14 + tiles :]
    width = H * HD
    mine = lax.axis_index("tile")
    wide = vn.shape[1]
    share = groups * group_rows
    inv_root = 1.0 / math.sqrt(HD)
    adder = jnp.concatenate([eye(NB)] * 2, axis=1)
    bins = lax.broadcasted_iota(jnp.int32, (NB, 2 * wide), 0).astype(F32)

    acc[...] = jnp.zeros_like(acc)

    shift = jnp.concatenate([cst[...]] * 2, axis=1)

    whole = (tgt, at, ot, ut, gt, vn, kt, qt, dpt, dzn) + tuple(rcv)

    def one_block(step):
        rows = BLOCK
        tgt, at, ot, ut, gt, vn, kt, qt, dpt, dzn, *rcv = blocks_of(whole, step)

        def one_pair(first):
            pair = (first, first + 1)
            for row in pair:
                for k in range(tiles):
                    source_i = (mine ^ k) // grid_side
                    source_j = lax.rem(mine ^ k, grid_side)
                    for c, (base, chunk_groups) in enumerate(spans):
                        part = rcv[c * tiles + k][row].astype(F32)
                        left = lax.broadcasted_iota(jnp.int32, part.shape, 1) < NB
                        part = jnp.concatenate(
                            [jnp.where(left, part, 0.0), jnp.where(left, 0.0, part)], axis=0
                        )
                        for p in range(chunk_groups):
                            start = (
                                (source_i * groups + base + p) * grid_side + source_j
                            ) * group_rows + row * wide
                            mirror_s[pl.ds(pl.multiple_of(start, group_rows), group_rows), :] = part[
                                p * group_rows : (p + 1) * group_rows
                            ]
            yield
            other = nt(adder, mirror_s[first * wide : (first + 2) * wide, :].astype(BF))
            yield
            logits = jnp.concatenate([ut[row] for row in pair], axis=1) + other + shift
            peak = jnp.max(logits, axis=0, keepdims=True)
            yield
            probs = jnp.exp(logits - peak)
            total = jnp.sum(probs, axis=0, keepdims=True)
            yield
            target = jnp.concatenate([tgt[row : row + 1, :] for row in pair], axis=1)
            resid = 2.0 * (probs * (1.0 / total) - jnp.where(bins == target, 1.0, 0.0))
            res_hi, res_lo = split(resid)
            yield
            pair_grad = nn(wd3[...], jnp.concatenate([res_hi, res_lo, res_hi], axis=0))
            for n, row in enumerate(pair):
                dpt[row] = pair_grad[:, n * wide : (n + 1) * wide]
            yield
            out_grad = nn(wo[...], pair_grad.astype(BF))
            yield
            for n, row in enumerate(pair):
                gate = gt[row]
                gated = out_grad[:, n * wide : (n + 1) * wide] * gate
                grad_s[row] = gated.astype(BF)
                back_s[3 * width :, row * wide : (row + 1) * wide] = (
                    gated * ot[row] * (1.0 - gate)
                ).astype(BF)
                yield

            def heads(row):
                lanes = slice(row * wide, (row + 1) * wide)
                for h in range(H):
                    part = slice(h * HD, (h + 1) * HD)
                    back_s[2 * width + h * HD : 2 * width + (h + 1) * HD, lanes] = nt(
                        grad_s[row, part, :], at[row, :, h * wide : (h + 1) * wide]
                    ).astype(BF)
                    yield
                    weight_grad = nn(vn[row], head_block(grad_s[row, part, :], h))
                    yield
                    prob = at[row, :, h * wide : (h + 1) * wide].astype(F32)
                    prod = prob * weight_grad
                    total = jnp.sum(prod, axis=0, keepdims=True)
                    yield
                    prod = prod - prob * total
                    prod_b = prod.astype(BF)
                    acc[h] += prod
                    yield
                    back_s[h * HD : (h + 1) * HD, lanes] = (nn(kt[row, part, :], prod_b) * inv_root).astype(BF)
                    back_s[width + h * HD : width + (h + 1) * HD, lanes] = (
                        nt(qt[row, part, :], prod_b) * inv_root
                    ).astype(BF)
                    yield

            both = [heads(row) for row in pair]
            while both:
                for row in list(both):
                    try:
                        next(row)
                    except StopIteration:
                        both.remove(row)
                yield
            normed_grad = nn(wall[...], back_s[:, first * wide : (first + 2) * wide])
            for n, row in enumerate(pair):
                dzn[row] = normed_grad[:, n * wide : (n + 1) * wide]
            yield

        interleave([one_pair(row) for row in range(0, rows, 2)], BWD_PACE)

    loop_blocks(share, one_block)

    for h in range(H):
        grad = acc[h].T
        for i in range(grid_side):
            for j in range(grid_side):
                pieces = []
                for p in range(groups):
                    source = ((i * groups + p) * grid_side + j) * group_rows
                    pieces.append(grad[source : source + group_rows])
                order[i * grid_side + j, h * share : (h + 1) * share, :] = jnp.concatenate(
                    pieces, axis=0
                )
    for k in range(tiles):
        sends[k][...] = order[mine ^ k].reshape(H, share, wide).astype(BF)


def finish_kernel(offsets, *refs, tiles):
    rdb = refs[:tiles]
    base, nrm, inv, wgs, out, sums = refs[tiles:]
    share, chans, wide = base.shape
    states, _, piece, _ = out.shape
    total_rows = rdb[0].shape[1]
    turn = offsets[lax.axis_index("state")] // piece

    for h in range(H):
        total = rdb[0][h].astype(F32)
        for part in rdb[1:]:
            total = total + part[h].astype(F32)
        sums[pl.ds(h * total_rows, total_rows), :] = total

    def one_block(step):
        base_b, nrm_b, inv_b = blocks_of((base, nrm, inv), step)

        def one_row(row):
            local = step * BLOCK + row
            parts = [sums[pl.ds(h * total_rows + local, 1), :] for h in range(H)]
            high, low = split(jnp.concatenate(parts, axis=0))
            high, low = high.astype(F32), low.astype(F32)
            spread = jnp.concatenate([high, low, high, jnp.zeros((H, wide), F32)], axis=0)
            yield
            scaled = nn(wgs[...], spread.astype(BF))
            yield
            mean_a = jnp.mean(scaled, axis=0, keepdims=True)
            mean_b = jnp.mean(scaled * nrm_b[row], axis=0, keepdims=True)
            yield
            total = base_b[row] + inv_b[row : row + 1, :] * (scaled - mean_a - nrm_b[row] * mean_b)
            yield
            total = total.T.astype(BF)
            for c in range(wide // piece):
                out[lax.rem(turn + c, states), local] = total[c * piece : (c + 1) * piece]
            yield

        interleave([one_row(row) for row in range(BLOCK)], FIN_PACE)

    loop_blocks(share, one_block)


def place_kernel(offsets, rcv, out, *, side):
    states, grid_side, rows, piece, chans = rcv.shape
    start = lax.axis_index("state") * piece
    out[...] = jnp.zeros_like(out)
    for s in range(states):
        offset = offsets[s]
        half = (start < offset).astype(jnp.int32)
        base = offset // side
        for i in range(grid_side):
            out[base + i, :, half] += rcv[s, i].astype(F32)


def on_device(
    pair_tiles,
    targets,
    offsets,
    ln_gain,
    ln_bias,
    w_query,
    w_key,
    w_value,
    w_pairbias,
    w_gate,
    gate_bias,
    w_output,
    out_bias,
    w_distogram,
    dist_bias,
):
    tiles = lax.axis_size("tile")
    states = lax.axis_size("state")
    side, chans = pair_tiles.shape[3], pair_tiles.shape[4]
    wide = targets.shape[4]
    grid_side = wide // side
    owner_rows = side // tiles
    width = H * HD
    here = lax.axis_index("tile")
    tile_i = here // grid_side
    tile_j = lax.rem(here, grid_side)
    even = owner_rows % grid_side == 0
    groups = tiles if even else 1
    group_rows = side // groups // grid_side
    share = groups * group_rows
    per_head = side * side // wide
    piece = wide // states

    def stay(value):
        return pltpu.with_memory_space_constraint(value, pltpu.HBM)

    def shapes(*pairs):
        return [jax.ShapeDtypeStruct(s, t) for s, t in pairs]

    own = tile_j.reshape(1)
    gain_row = ln_gain.reshape(1, chans)
    shift_row = ln_bias.reshape(1, chans)
    prep_shapes = shapes(
        ((4 * width, chans), BF),
        ((chans, 2 * width), BF),
        ((2 * NB, width), BF),
        ((2 * NB, chans), BF),
        ((width, wide), F32),
    )
    w4t, w2, wod, wdt, gbc = pl.pallas_call(
        prep_kernel,
        out_shape=prep_shapes,
        name="prep",
        compiler_params=pltpu.CompilerParams(vmem_limit_bytes=VMEM_BYTES),
    )(
        *map(
            stay,
            (
                w_query,
                w_key,
                w_value,
                w_gate,
                w_output,
                gate_bias.reshape(1, width),
                w_distogram.T,
            ),
        )
    )

    bias_rows = H * per_head
    target_rows = owner_rows * grid_side
    bias_mine, gain_near, shift_near, *outgoing_rows = pl.pallas_call(
        functools.partial(bias_kernel, per_head=per_head, groups=groups),
        grid_spec=pltpu.PrefetchScalarGridSpec(
            num_scalar_prefetch=1,
            grid=(1,),
            in_specs=[
                full((grid_side, per_head, side, chans)),
                full((target_rows, wide)),
                full((1, chans)),
                full((1, chans)),
                full((H, chans)),
            ],
            out_specs=[full((bias_rows + target_rows, wide))]
            + [full((1, chans))] * 2
            + [full((share, side, chans))] * grid_side,
        ),
        out_shape=shapes(
            ((bias_rows + target_rows, wide), F32),
            *([((1, chans), F32)] * 2),
            *([((share, side, chans), BF)] * grid_side),
        ),
        name="bias",
        compiler_params=pltpu.CompilerParams(vmem_limit_bytes=VMEM_BYTES),
    )(
        own,
        *map(
            stay,
            (
                pair_tiles.reshape(grid_side, per_head, side, chans),
                targets.reshape(target_rows, wide),
                gain_row,
                shift_row,
                w_pairbias.T,
            ),
        ),
    )
    parts = [outgoing_rows[0]]
    for k in range(1, grid_side):
        perm = [
            (i * grid_side + j, i * grid_side + (j + k) % grid_side)
            for i in range(grid_side)
            for j in range(grid_side)
        ]
        parts.append(lax.ppermute(outgoing_rows[k], "tile", perm))

    def to_partner(value, k):
        return lax.ppermute(value, "tile", [(t, t ^ k) for t in range(tiles)]) if k else value

    gathered = [to_partner(bias_mine, k) for k in range(tiles)]

    def by_row(*shape, rows, base=0):
        return pl.BlockSpec((rows,) + shape, lambda g, *_: (g + base,) + (0,) * len(shape))

    def cost(flops, moved):
        return pl.CostEstimate(flops=flops, bytes_accessed=moved, transcendentals=0)

    cell = wide * width * wide
    square_b = ((share, wide, width), BF)
    zr, qt, kt, vt, kn, vn, gt = pl.pallas_call(
        functools.partial(project_kernel, parts=grid_side),
        grid_spec=pltpu.PrefetchScalarGridSpec(
            num_scalar_prefetch=1,
            grid=(1,),
            in_specs=[by_row(side, chans, rows=share)] * grid_side
            + [full((1, chans)), full((1, chans)), full(w4t.shape), full(w2.shape), full(gbc.shape)],
            out_specs=[by_row(wide, width, rows=share)] * 7,
            scratch_shapes=[pltpu.VMEM((group_rows * wide, chans), BF)],
        ),
        out_shape=shapes(*([square_b] * 6), ((share, width, wide), F32)),
        cost_estimate=cost(80 * share * cell, 12 * share * wide * width * 2),
        name="project",
        compiler_params=pltpu.CompilerParams(vmem_limit_bytes=VMEM_BYTES),
    )(own, *parts, gain_near, shift_near, w4t, w2, gbc)

    last_groups = groups // 4
    spans = [(0, groups - last_groups)] + [(groups - last_groups, last_groups)] * (last_groups > 0)
    layout = dict(grid_side=grid_side, groups=groups, group_rows=group_rows)
    saved_shapes = shapes(
        ((share, wide, H * wide), BF),
        ((share, width, wide), F32),
        ((share, NB, wide), F32),
        ((share, wide), F32),
        ((H, wide, wide), F32),
    )
    saved = []
    mirrored = []
    for base, chunk_groups in spans:
        count = chunk_groups * group_rows
        c = base // chunk_groups
        packed_shape = (share, count // 2, 2 * NB)
        inputs = [*gathered, kn, qt, vt, gt, zr, wod, wdt]
        first = len(inputs)
        call = pl.pallas_call(
            functools.partial(
                forward_kernel,
                tiles=tiles,
                base=base,
                count=count,
                bias_rows=bias_rows,
                owner_rows=owner_rows,
                extra=len(saved),
                **layout,
            ),
            grid=(1,),
            in_specs=[full(gathered[0].shape)] * tiles
            + [by_row(wide, width, rows=count, base=c)] * 5
            + [full(wod.shape), full(wdt.shape)]
            + [pl.BlockSpec(memory_space=pl.ANY)] * len(saved),
            out_specs=[
                by_row(wide, H * wide, rows=count, base=c),
                by_row(width, wide, rows=count, base=c),
                by_row(NB, wide, rows=count, base=c),
                by_row(wide, rows=count, base=c),
                full((H, wide, wide)),
            ]
            + [full(packed_shape)] * tiles,
            out_shape=saved_shapes + shapes(*([(packed_shape, BF)] * tiles)),
            scratch_shapes=[
                pltpu.VMEM((tiles,) + gathered[0].shape, F32),
                pltpu.VMEM((tiles * share * count, 2 * NB), F32),
            ],
            input_output_aliases={first + n: n for n in range(len(saved))},
            cost_estimate=cost(150 * count * cell, 14 * count * wide * width * 2),
            name="forward",
        compiler_params=pltpu.CompilerParams(vmem_limit_bytes=VMEM_BYTES),
        )
        results = call(*inputs, *saved)
        saved = list(results[:4])
        mirrored.append([to_partner(results[5 + k], k) for k in range(tiles)])
    at, ot, ut, tgt = saved

    late = (
        w_query,
        w_key,
        w_value,
        w_gate,
        out_bias.reshape(1, chans),
        w_distogram.T,
        dist_bias.reshape(1, NB),
        w_pairbias.T,
        gain_row,
    )
    late_shapes = (
        ((chans, 3 * NB), BF),
        ((chans, 4 * width), BF),
        ((chans, wide), F32),
        ((NB, wide), F32),
        ((chans, 4 * H), BF),
    )
    nrm, inv, wd3, wall, lgc, cst, wgs = pl.pallas_call(
        middle_kernel,
        grid=(1,),
        in_specs=[pl.BlockSpec((8, wide), lambda g: (0, 0)), by_row(wide, chans, rows=share)]
        + [full(w.shape) for w in late],
        out_specs=[by_row(chans, wide, rows=share), by_row(wide, rows=share)]
        + [full(shape) for shape, _ in late_shapes],
        out_shape=shapes(((share, chans, wide), F32), ((share, wide), F32), *late_shapes),
        cost_estimate=cost(20 * share * cell, 3 * share * wide * width * 2),
        name="middle",
        compiler_params=pltpu.CompilerParams(vmem_limit_bytes=VMEM_BYTES),
    )(tgt, zr, *map(stay, late))

    results = pl.pallas_call(
        functools.partial(backward_kernel, tiles=tiles, spans=tuple(spans), **layout),
        grid=(1,),
        in_specs=[
            by_row(size * group_rows // 2, 2 * NB, rows=share) for _, size in spans for _ in range(tiles)
        ]
        + [
            by_row(wide, rows=share),
            by_row(wide, H * wide, rows=share),
            by_row(width, wide, rows=share),
            by_row(NB, wide, rows=share),
        ]
        + [by_row(wide, width, rows=share)] * 4
        + [full(w.shape) for w in (w_output, wd3, wall, cst)],
        out_specs=[by_row(chans, wide, rows=share)] * 2 + [full((H, share, wide))] * tiles,
        out_shape=shapes(*([((share, chans, wide), F32)] * 2), *([((H, share, wide), BF)] * tiles)),
        scratch_shapes=[
            pltpu.VMEM((H, wide, wide), F32),
            pltpu.VMEM((BLOCK, width, wide), BF),
            pltpu.VMEM((4 * width, BLOCK * wide), BF),
            pltpu.VMEM((BLOCK * wide, 2 * NB), F32),
            pltpu.VMEM((tiles, H * share, wide), F32),
        ],
        cost_estimate=cost(500 * share * cell, 20 * share * wide * width * 2),
        name="backward",
        compiler_params=pltpu.CompilerParams(vmem_limit_bytes=VMEM_BYTES),
    )(
        *[part for parts_c in mirrored for part in parts_c],
        tgt, at, ot, ut, gt, vn, kt, qt, w_output, wd3, wall, cst,
    )
    dpt, dzn = results[:2]
    rdb = [to_partner(results[2 + k], k) for k in range(tiles)]

    base = pl.pallas_call(
        main_kernel,
        grid=(1,),
        in_specs=[by_row(chans, wide, rows=share)] * 3
        + [by_row(wide, rows=share), full(lgc.shape)],
        out_specs=by_row(chans, wide, rows=share),
        out_shape=jax.ShapeDtypeStruct((share, chans, wide), F32),
        cost_estimate=cost(20 * share * cell, 8 * share * wide * width * 2),
        name="main",
        compiler_params=pltpu.CompilerParams(vmem_limit_bytes=VMEM_BYTES),
    )(dpt, dzn, nrm, inv, lgc)

    outgoing = pl.pallas_call(
        functools.partial(finish_kernel, tiles=tiles),
        grid_spec=pltpu.PrefetchScalarGridSpec(
            num_scalar_prefetch=1,
            grid=(1,),
            in_specs=[
                *([full(rdb[0].shape)] * tiles),
                by_row(chans, wide, rows=share),
                by_row(chans, wide, rows=share),
                by_row(wide, rows=share),
                full(wgs.shape),
            ],
            out_specs=pl.BlockSpec((states, share, piece, chans), lambda g, _: (0, g, 0, 0)),
            scratch_shapes=[pltpu.VMEM((H * share, wide), F32)],
        ),
        out_shape=jax.ShapeDtypeStruct((states, share, piece, chans), BF),
        name="finish",
        compiler_params=pltpu.CompilerParams(vmem_limit_bytes=VMEM_BYTES),
    )(offsets, *rdb, base, nrm, inv, wgs)

    if even:
        slots = outgoing.reshape(states * tiles, group_rows, piece, chans)
    else:
        slots = lax.dynamic_update_slice(
            jnp.zeros((states, tiles, owner_rows, piece, chans), BF),
            outgoing.reshape(states, grid_side, owner_rows, piece, chans),
            (0, tile_j * grid_side, 0, 0, 0),
        ).reshape(states * tiles, owner_rows, piece, chans)
    received = lax.all_to_all(slots, ("state", "tile"), split_axis=0, concat_axis=0, tiled=True)
    if even:
        received = received.reshape(states, grid_side, owner_rows, piece, chans)
    else:
        received = lax.dynamic_index_in_dim(
            received.reshape(states, grid_side, grid_side, owner_rows, piece, chans),
            tile_i,
            2,
            keepdims=False,
        )

    block = owner_rows
    out_shape = (2 * grid_side, owner_rows, 2, piece, chans)
    placed = pl.pallas_call(
        functools.partial(place_kernel, side=side),
        grid_spec=pltpu.PrefetchScalarGridSpec(
            num_scalar_prefetch=1,
            grid=(owner_rows // block,),
            in_specs=[
                pl.BlockSpec(
                    (states, grid_side, block, piece, chans), lambda g, _: (0, 0, g, 0, 0)
                )
            ],
            out_specs=pl.BlockSpec(
                (2 * grid_side, block, 2, piece, chans), lambda g, _: (0, g, 0, 0, 0)
            ),
        ),
        out_shape=jax.ShapeDtypeStruct(out_shape, F32),
        name="place",
        compiler_params=pltpu.CompilerParams(vmem_limit_bytes=VMEM_BYTES),
    )(offsets, received)
    return placed.reshape(2 * grid_side, 1, owner_rows, 2, piece, chans)


def solution(mesh):
    in_specs = (
        P("state", "tile", None, None, None),
        P("state", "tile", None, None, None),
    ) + (P(),) * 13
    out_specs = P(None, "tile", None, None, "state", None)
    return jax.shard_map(
        on_device, mesh=mesh, in_specs=in_specs, out_specs=out_specs, check_vma=False
    )
```
